32 devices in a mesh: seq: 16 (over z, x, core), tensor: 2 (over y).
Axes of the slice: x: 2, y: 2, z: 4, core: 2. Of those that a mesh axis runs over, the one named last changes fastest.
Arguments:
- hidden: bfloat16 [3072, 4096], P('seq', 'tensor'), may hold values from -170 to 170
- depth: int32 [3072], P('seq'), may hold values from 0 to 4, as said below
- norm_gain: float32 [4096], replicated, may hold values from 0.5 to 2
- w_query: bfloat16 [4096, 2048], P('seq', 'tensor'), may hold values from -2.5 to 2.5
- w_key: bfloat16 [4096, 1024], P('seq', 'tensor'), may hold values from -1 to 1
- w_value: bfloat16 [4096, 1024], P('seq', 'tensor'), may hold values from -0.09375 to 0.09375
- w_out: bfloat16 [2048, 4096], P('tensor', 'seq'), may hold values from -0.1875 to 0.1875
Outputs:
- mixed: bfloat16 [3072, 4096], P('seq', 'tensor')
The draws below stay inside these ranges and needn't reach their ends.
Inputs may be any that keep to these rules, and one draw needn't show every extreme that they name: A token takes part in this step when its depth exceeds 2. In each aligned block of 192 tokens at most 96 take part, and some block holds exactly 96.
All inputs are finite; a program needn't handle non-finite values.
Results may differ from the reference program's by a relative error of at most 0.015.
Values may be sent and summed in bfloat16 or wider, within the bound.
A program may use at most 64 MiB of HBM per device.

```python
import math
import jax
import jax.numpy as jnp
from jax import lax

D = 4096
HD = 128
KVH = 8
QH = 16
STEP = 2
TOK_DEV = 192
CAP = 96
DOCUMENT_TOKENS = 3072
N_TENSOR = 2


def permuted(subkey):
    return jax.random.permutation(subkey, TOK_DEV)


def continuing_tokens(key):
    blocks = DOCUMENT_TOKENS // TOK_DEV
    subkeys = jax.random.split(jax.random.fold_in(key, 101), 2)
    block_ids = jnp.arange(blocks, dtype=jnp.int32)
    ceiling = CAP * (block_ids + 1) // blocks
    counts = jax.random.randint(subkeys[0], (blocks,), 0, ceiling + 1)
    counts = jnp.where(block_ids == blocks - 1, CAP, counts)
    ranked_tokens = jax.vmap(permuted)(jax.random.split(subkeys[1], blocks))
    chosen_tokens = ranked_tokens < counts[:, None]
    return chosen_tokens


def draw_depth(key, part):
    chosen_tokens = continuing_tokens(key)
    subkeys = jax.random.split(jax.random.fold_in(key, 202), 2)
    higher = jax.random.randint(subkeys[0], chosen_tokens.shape, STEP + 1, 5)
    lower = jax.random.randint(subkeys[1], chosen_tokens.shape, 0, STEP + 1)
    return jnp.where(chosen_tokens, higher, lower).reshape(DOCUMENT_TOKENS).astype(jnp.int32)


def draw_norm_gain(key, part):
    values = jax.random.uniform(jax.random.fold_in(key, 404), (D,), jnp.float32, 0.5, 1.5)
    return values.astype(jnp.float32)


def draw_w_query(key, part):
    spread = (8.0 / D) ** 0.5
    values = jax.random.normal(jax.random.fold_in(key, 414), (D, QH * HD), jnp.float32) * spread
    values = jnp.clip(values, -6.0 * spread, 6.0 * spread)
    return values.astype(jnp.bfloat16)


def draw_w_key(key, part):
    spread = (1.0 / D) ** 0.5
    values = jax.random.normal(jax.random.fold_in(key, 424), (D, KVH * HD), jnp.float32) * spread
    values = jnp.clip(values, -6.0 * spread, 6.0 * spread)
    return values.astype(jnp.bfloat16)


def draw_hidden(key, part):
    values = jnp.clip(jax.random.normal(jax.random.fold_in(key, 505), (DOCUMENT_TOKENS, D), jnp.float32), -6.0, 6.0)
    return values.astype(jnp.bfloat16)


def raised(values, key, source, target, shards_of, factor):
    def block_of(position):
        return (jnp.arange(values.shape[position]) // (values.shape[position] // shards_of)).reshape((-1,) + (1,) * (values.ndim - 1 - position))

    first = jax.random.permutation(key, shards_of)[block_of(target)]
    other_side = (block_of(target) + shards_of // 2) % shards_of
    return jnp.where((block_of(source) == first) | (block_of(source) == other_side), factor * values, values)


def shard_levels(own_key, dims, shards, low, high):
    level, own = 1.0, jax.random.fold_in(own_key, 6)
    for axis_at, shards_of in shards:
        heights = jnp.exp(jax.random.uniform(jax.random.fold_in(own, axis_at), (shards_of,), jnp.float32, low / len(shards), high / len(shards)))
        level = level * jnp.repeat(heights, dims[axis_at] // shards_of).reshape([-1 if axis == axis_at else 1 for axis in range(len(dims))])
    return level


def gaussian(rng, dims, scale, bound, shards=(), held_as=jnp.bfloat16):
    result = scale * jax.random.normal(rng, dims, jnp.float32)
    if shards:
        result = result * shard_levels(rng, dims, shards, -0.22, 0.18)
    return jnp.clip(result, -bound, bound).astype(held_as)


def gaussian_with(stream_key, dims, deviation, bound, pieces, heavy, kind=jnp.bfloat16):
    values = deviation * jax.random.normal(stream_key, dims, jnp.float32)
    if pieces:
        values = values * shard_levels(stream_key, dims, pieces, -0.22, 0.18)
    return jnp.clip(raised(values, jax.random.fold_in(stream_key, 3), *heavy), -bound, bound).astype(kind)


def setup_inputs(seed: int = 0) -> dict:
    seeds = jax.random.split(jax.random.key(seed), 8)
    return {
        "hidden": draw_hidden(jax.random.fold_in(seeds[7], 71), 0),
        "depth": draw_depth(jax.random.fold_in(seeds[7], 71), 0),
        "norm_gain": draw_norm_gain(jax.random.fold_in(seeds[7], 71), 0),
        "w_query": draw_w_query(jax.random.fold_in(seeds[7], 71), 0),
        "w_key": draw_w_key(jax.random.fold_in(seeds[7], 71), 0),
        "w_value": gaussian(seeds[5], (D, KVH * HD), D ** -0.5, 0.09375, ((0, 16), (1, 2))),
        "w_out": gaussian_with(seeds[6], (QH * HD, D), (QH * HD) ** -0.5, 0.1875, ((0, 2), (1, 16)), (0, 1, 16, 2.0)),
    }


EPSILON = 1e-05
MASKED_SCORE = -1e+30

def reference(hidden, depth, norm_gain, w_query, w_key, w_value, w_out):
    blocks = DOCUMENT_TOKENS // TOK_DEV
    widened = hidden.astype(jnp.float32)
    inverse = lax.rsqrt(lax.optimization_barrier(jnp.mean(widened * widened, axis=1, keepdims=True)) + EPSILON)
    normed = (widened * inverse * norm_gain[None, :]).astype(jnp.bfloat16)
    queries = jnp.dot(normed, w_query, preferred_element_type=jnp.float32).astype(jnp.bfloat16)
    keys_all = jnp.dot(normed, w_key, preferred_element_type=jnp.float32).astype(jnp.bfloat16)
    values_all = jnp.dot(normed, w_value, preferred_element_type=jnp.float32).astype(jnp.bfloat16)
    living = (depth > STEP).reshape(blocks, TOK_DEV)
    slot_of = jnp.cumsum(living.astype(jnp.int32), axis=1) - 1
    slot_ids = jnp.arange(CAP, dtype=jnp.int32)
    hit_bool = living[:, :, None] & (slot_of[:, :, None] == slot_ids[None, None, :])
    select_tokens = hit_bool.astype(jnp.float32)

    def compact(matrix):
        shaped = matrix.astype(jnp.float32).reshape(blocks, TOK_DEV, -1)
        return jnp.einsum('src,srf->scf', select_tokens, shaped).reshape(blocks * CAP, -1)
    positions = jnp.arange(DOCUMENT_TOKENS, dtype=jnp.int32).reshape(blocks, TOK_DEV)
    slot_pos = lax.optimization_barrier(jnp.sum(jnp.where(hit_bool, positions[:, :, None], 0), axis=1))
    filled = jnp.any(hit_bool, axis=1)
    slot_pos = jnp.where(filled, slot_pos, DOCUMENT_TOKENS).reshape(blocks * CAP).astype(jnp.int32)
    group_size = QH // KVH
    kept_queries = compact(queries).reshape(blocks, CAP, QH, HD)
    kept_keys = jnp.repeat(compact(keys_all).reshape(blocks * CAP, KVH, HD), group_size, axis=1)
    kept_values = jnp.repeat(compact(values_all).reshape(blocks * CAP, KVH, HD), group_size, axis=1)
    scale = 1.0 / math.sqrt(HD)

    def attend(query_block):
        query_rows, query_pos = query_block
        scores = jnp.einsum('qhd,khd->hqk', query_rows, kept_keys) * scale
        visible = slot_pos[None, :] <= query_pos[:, None]
        scores = jnp.where(visible[None], scores, MASKED_SCORE)
        row_peak = lax.optimization_barrier(jnp.max(scores, axis=-1, keepdims=True))
        expons = jnp.exp(scores - row_peak)
        row_total = lax.optimization_barrier(jnp.sum(expons, axis=-1))
        weights = lax.optimization_barrier(expons.astype(jnp.bfloat16)).astype(jnp.float32)
        weighted = jnp.einsum('hqk,khd->qhd', weights, kept_values)
        return (weighted / jnp.transpose(row_total)[:, :, None]).astype(jnp.bfloat16)
    attended_kept = lax.map(attend, (kept_queries, slot_pos.reshape(blocks, CAP)))
    attended = jnp.einsum('src,scf->srf', select_tokens, attended_kept.reshape(blocks, CAP, QH * HD).astype(jnp.float32))
    attended = attended.reshape(DOCUMENT_TOKENS, QH * HD).astype(jnp.bfloat16)
    head_cols = QH * HD // N_TENSOR
    grouped = jnp.transpose(attended.reshape(DOCUMENT_TOKENS, N_TENSOR, head_cols), (1, 0, 2))
    out_groups = w_out.reshape(N_TENSOR, head_cols, D)

    def add_group(prefix_total, group_pair):
        columns, out_rows = group_pair
        partial_term = jnp.dot(columns, out_rows, preferred_element_type=jnp.float32)
        rounded = lax.optimization_barrier(partial_term.astype(jnp.bfloat16)).astype(jnp.float32)
        return (prefix_total + rounded, None)
    summed, _ = lax.scan(add_group, jnp.zeros((DOCUMENT_TOKENS, D), jnp.float32), (grouped, out_groups))
    living_flat = living.reshape(DOCUMENT_TOKENS)
    return jnp.where(living_flat[:, None], summed, 0.0).astype(jnp.bfloat16)
```

```python
import functools

import jax
import jax.numpy as jnp
from jax import lax
from jax.experimental import pallas as pl
from jax.experimental.pallas import tpu as pltpu
from jax.sharding import PartitionSpec as P

HD = 128
STEP = 2
EPSILON = 1e-05
MASKED_SCORE = -1e30


def rolled(pieces, axis, my):
    n = len(pieces)
    if n == 1:
        return pieces[0]
    width = pieces[0].shape[axis]
    twice = jnp.concatenate(pieces + pieces, axis=axis)
    start = lax.rem(n - my, n) * width
    return lax.dynamic_slice_in_dim(twice, start, n * width, axis=axis)


LANES = 128
MESH = pl.DeviceIdType.MESH


def step_kernel(
    Z, J, T, packed, count, gain, w_blocks, w_out, mixed_ref,
    weights, tokens, counts, sq_own, sq_other, queries, kv, outw, att, heads, terms, other,
    ws_z, ws_s, ws_x, wr, cs, cr, qs, qr, ts_up, ts_dn, ts_y, tr, ks_s, ks_x, kr,
    os_up, os_dn, os_s, os_x, orr, hs, hr, ys, yr,
):
    me, t = lax.axis_index("seq"), lax.axis_index("tensor")
    z, j = me // J, lax.rem(me, J)
    slots, width = packed.shape
    part, cols = w_blocks.shape[1:]
    q_cols = cols - 2 * HD
    heads_here = q_cols // HD
    pad = counts.shape[1]
    block = slots + pad
    half = w_out.shape[0] // 2
    share = Z // T
    sib = j + 1 - 2 * lax.rem(j, 2)
    across = lax.rem(j + J // 2, J)
    diag = lax.rem(sib + J // 2, J)
    ty = T - 1 - t
    has_up, has_down = z < Z - 1, z > 0

    def dev(zz, jj):
        return (zz * J + jj, t)

    sib_dev, across_dev, y_dev = dev(z, sib), dev(z, across), (me, ty)
    up, down = dev(z + 1, j), dev(z - 1, j)

    def sides(k, act):
        pl.when(z - k >= 0)(lambda: act(z - k))
        pl.when(z + k < Z)(lambda: act(z + k))

    barrier = pltpu.get_barrier_semaphore()

    def greet(device):
        pl.semaphore_signal(barrier, inc=1, device_id=device, device_id_type=MESH)

    for k in range(1, Z):
        sides(k, lambda zz: greet(dev(zz, j)))
    for device in (sib_dev, across_dev, y_dev):
        greet(device)
    pl.semaphore_wait(barrier, Z + 2)

    def send(src, dst, send_sem, recv_sem, device):
        return pltpu.make_async_remote_copy(
            src_ref=src, dst_ref=dst, send_sem=send_sem, recv_sem=recv_sem,
            device_id=device, device_id_type=MESH,
        )

    def w_at(b):
        return weights.at[pl.ds(pl.multiple_of(b * part, part), part), :]

    def w_z(zz):
        return send(w_blocks.at[zz], w_at(me), ws_z.at[zz], wr.at[me], dev(zz, j))

    def w_cast(b, sems, device, own=False):
        return send(w_blocks.at[z] if own else w_at(b), w_at(b), sems.at[b], wr.at[b], device)

    def w_wait(b):
        w_cast(b, ws_s, sib_dev).wait_recv()

    def c_z(zz):
        return send(count, counts.at[z], cs.at[zz], cr.at[z], dev(zz, j))

    def t_copy(zz, tt, sems, device):
        at = tokens.at[zz, tt]
        return send(at, at, sems.at[zz], tr.at[zz * T + tt], device)

    def k_at(b):
        return kv.at[pl.ds(pl.multiple_of(b * block, 16), block), :]

    def k_cast(b, sems, device):
        return send(k_at(b), k_at(b), sems.at[b], kr.at[b], device)

    def o_copy(zb, jb, h, sems, device, own=False):
        b = zb * J + jb
        rows = pl.ds(h * half, half)
        dst = outw.at[b, rows]
        return send(w_out.at[rows] if own else dst, dst, sems.at[2 * b + h], orr.at[2 * b + h], device)

    def h_copy(zz):
        return send(att.at[zz], heads.at[z], hs.at[zz], hr.at[z], dev(zz, j))

    def y_copy(zb):
        return send(
            terms.at[zb], other.at[lax.rem(zb, share)], ys.at[zb], yr.at[lax.rem(zb, share)], y_dev
        )

    for k in range(1, Z):
        sides(k, lambda zz: c_z(zz).start())
    for k in range(Z - 1, 0, -1):
        sides(k, lambda zz: w_z(zz).start())
    w_cast(me, ws_x, across_dev, True).start()
    w_cast(me, ws_s, sib_dev, True).start()

    wide = packed[...].astype(jnp.float32)
    own_squares = jnp.sum(wide * wide, axis=1, keepdims=True)
    sq_own[...] = jnp.broadcast_to(own_squares, sq_own.shape)
    q_copy = send(sq_own, sq_other, qs.at[0], qr.at[0], y_dev)
    q_copy.start()
    weights[pl.ds(pl.multiple_of(me * part, part), part), :] = w_blocks[z]
    counts[z] = count[...]
    q_copy.wait_recv()
    squares = own_squares + sq_other[:, 0:1]
    inverse = lax.rsqrt(squares / (T * width) + EPSILON)
    tokens[z, t] = (packed[...].astype(jnp.float32) * inverse * gain[t]).astype(jnp.bfloat16)

    def push_t(zz, go_up, go_down):
        if go_up is not None:
            pl.when(go_up)(lambda: t_copy(zz, t, ts_up, up).start())
        if go_down is not None:
            pl.when(go_down)(lambda: t_copy(zz, t, ts_dn, down).start())
        t_copy(zz, t, ts_y, y_dev).start()

    push_t(z, has_up, has_down)

    def own_o(h):
        pl.when(has_up)(lambda: o_copy(z, j, h, os_up, up, True).start())
        pl.when(has_down)(lambda: o_copy(z, j, h, os_dn, down, True).start())

    own_o(0)
    for h in range(2):
        o_copy(z, j, h, os_x, across_dev, True).start()
        o_copy(z, j, h, os_s, sib_dev, True).start()
    outw[me] = w_out[...]

    def relay_t(k):
        @pl.when(z - k >= 0)
        def _():
            t_copy(z - k, t, ts_up, up).wait_recv()
            push_t(z - k, has_up, None)

        @pl.when(z + k < Z)
        def _():
            t_copy(z + k, t, ts_dn, down).wait_recv()
            push_t(z + k, None, has_down)

    def relay_o(k, h):
        def cast(zb):
            o_copy(zb, j, h, os_x, across_dev).start()
            o_copy(zb, j, h, os_s, sib_dev).start()

        @pl.when(z - k >= 0)
        def _():
            o_copy(z - k, j, h, os_up, up).wait_recv()
            pl.when(has_up)(lambda: o_copy(z - k, j, h, os_up, up).start())
            cast(z - k)

        @pl.when(z + k < Z)
        def _():
            o_copy(z + k, j, h, os_dn, down).wait_recv()
            pl.when(has_down)(lambda: o_copy(z + k, j, h, os_dn, down).start())
            cast(z + k)

    def across_o(zb):
        for h in range(2):
            o_copy(zb, across, h, os_s, sib_dev).wait_recv()
            o_copy(zb, across, h, os_s, sib_dev).start()

    def relay_w(zz):
        b = zz * J + j
        w_wait(b)
        w_cast(b, ws_x, across_dev).start()
        w_cast(b, ws_s, sib_dev).start()

    def product(zz):
        t_copy(zz, ty, ts_y, y_dev).wait_recv()
        result = None
        for tt in range(T):
            term = jnp.dot(
                tokens[zz, tt], weights[tt * width : (tt + 1) * width, :],
                preferred_element_type=jnp.float32,
            )
            result = term if result is None else result + term
        for g in range(heads_here):
            queries[zz, g * slots : (g + 1) * slots, :] = result[
                :, g * HD : (g + 1) * HD
            ].astype(jnp.bfloat16)
        b = zz * J + j
        top = pl.multiple_of(b * block, 16)
        kv[pl.ds(top, slots), :] = result[:, q_cols:].astype(jnp.bfloat16)
        kv[pl.ds(pl.multiple_of(top + slots, 16), pad), :] = counts[zz]
        k_cast(b, ks_x, across_dev).start()
        k_cast(b, ks_s, sib_dev).start()

    for k in range(1, Z):
        sides(k, relay_w)
    relay_t(1)
    own_o(1)
    for zz in range(Z):
        w_wait(zz * J + across)
        w_cast(zz * J + across, ws_s, sib_dev).start()
    for k in range(1, Z):
        sides(k, lambda zz: c_z(zz).wait_send())

        @pl.when(z - k >= 0)
        def _():
            send(count, counts.at[z - k], cs.at[0], cr.at[z - k], down).wait_recv()

        @pl.when(z + k < Z)
        def _():
            send(count, counts.at[z + k], cs.at[0], cr.at[z + k], up).wait_recv()

    for zz in range(Z):
        w_wait(zz * J + sib)
        w_wait(zz * J + diag)
    product(z)
    for k in range(2, Z):
        relay_t(k)
        if k == 2:
            relay_o(1, 0)
        sides(k - 1, product)
        if k == 2:
            relay_o(1, 1)
    sides(Z - 1, product)
    across_o(z)

    for zz in range(Z):
        b = zz * J + across
        k_cast(b, ks_s, sib_dev).wait_recv()
        k_cast(b, ks_s, sib_dev).start()
    for zz in range(Z):
        k_cast(zz * J + sib, ks_s, sib_dev).wait_recv()
        k_cast(zz * J + diag, ks_s, sib_dev).wait_recv()

    keys = Z * J * block
    key_pos = lax.broadcasted_iota(jnp.int32, (1, keys), 1)
    seen = jnp.zeros((1, keys), jnp.float32)
    for b in range(Z * J):
        limit = kv[b * block + slots : b * block + slots + 1, 0:1].astype(jnp.float32) + b * block
        inside = (key_pos >= b * block) & (key_pos < (b + 1) * block)
        seen = jnp.where(inside & (key_pos.astype(jnp.float32) < limit), 1.0, seen)
    key_pos = jnp.where(seen > 0, key_pos, keys)
    row = lax.broadcasted_iota(jnp.int32, (slots, 1), 0)
    row = jnp.concatenate([row] * heads_here, axis=0) + j * block

    for zq in range(Z):
        n = (zq + 1) * J * block
        scores = lax.dot_general(
            queries[zq], kv[:n, :HD], (((1,), (1,)), ((), ())), preferred_element_type=jnp.float32
        ) * HD ** (-0.5)
        visible = key_pos[:, :n] <= row + zq * J * block
        scores = jnp.where(visible, scores, MASKED_SCORE)
        expons = jnp.exp(scores - jnp.max(scores, axis=1, keepdims=True))
        row_total = jnp.sum(expons, axis=1, keepdims=True)
        weighted = jnp.dot(
            expons.astype(jnp.bfloat16), kv[:n, HD:], preferred_element_type=jnp.float32
        )
        attended = (weighted / row_total).astype(jnp.bfloat16)
        for g in range(heads_here):
            att[zq, :, g * HD : (g + 1) * HD] = attended[g * slots : (g + 1) * slots]

        @pl.when(z == zq)
        def _():
            heads[z] = att[zq]

        @pl.when(z != zq)
        def _():
            h_copy(zq).start()

    for h in range(2):
        relay_o(2, h)
    sides(1, across_o)
    for k in range(1, Z):
        @pl.when(z - k >= 0)
        def _():
            send(att.at[0], heads.at[z - k], hs.at[0], hr.at[z - k], down).wait_recv()

        @pl.when(z + k < Z)
        def _():
            send(att.at[0], heads.at[z + k], hs.at[0], hr.at[z + k], up).wait_recv()

    def emit(zb):
        every = jnp.concatenate([heads[zz] for zz in range(Z)], axis=1)
        for jb in (sib, diag):
            for h in range(2):
                o_copy(zb, jb, h, os_s, sib_dev).wait_recv()
        for jb in range(J):
            terms[zb, :, jb * part : (jb + 1) * part] = jnp.dot(
                every, outw[zb * J + jb], preferred_element_type=jnp.float32
            ).astype(jnp.bfloat16)

        @pl.when(zb // share != t)
        def _():
            y_copy(zb).start()

    emit(z)
    sides(1, emit)
    for k in range(3, Z + 1):
        if k < Z:
            for h in range(2):
                relay_o(k, h)
        sides(k - 1, across_o)
        sides(k - 1, emit)

    for zl in range(share):
        zb = t * share + zl
        y_copy(zl).wait_recv()
        mixed_ref[:, zl * J * part : (zl + 1) * J * part] = (
            terms[zb].astype(jnp.float32) + other[zl].astype(jnp.float32)
        ).astype(jnp.bfloat16)

    q_copy.wait_send()
    for k in range(1, Z):
        sides(k, lambda zz: w_z(zz).wait_send())
        sides(k, lambda zz: h_copy(zz).wait_send())
    for zz in range(Z):
        t_copy(zz, t, ts_y, y_dev).wait_send()

        @pl.when(has_up & (zz <= z))
        def _():
            t_copy(zz, t, ts_up, up).wait_send()
            for h in range(2):
                o_copy(zz, j, h, os_up, up).wait_send()

        @pl.when(has_down & (zz >= z))
        def _():
            t_copy(zz, t, ts_dn, down).wait_send()
            for h in range(2):
                o_copy(zz, j, h, os_dn, down).wait_send()

        own, far = zz * J + j, zz * J + across
        w_cast(own, ws_x, across_dev).wait_send()
        k_cast(own, ks_x, across_dev).wait_send()
        for h in range(2):
            o_copy(zz, j, h, os_x, across_dev).wait_send()
        for jj in (j, across):
            w_cast(zz * J + jj, ws_s, sib_dev).wait_send()
            k_cast(zz * J + jj, ks_s, sib_dev).wait_send()
            for h in range(2):
                o_copy(zz, jj, h, os_s, sib_dev).wait_send()

        @pl.when(zz // share != t)
        def _():
            y_copy(zz).wait_send()


def stepped(Z, J, T, packed, count, gain, w_blocks, w_out):
    slots, width = packed.shape
    part, cols = w_blocks.shape[1:]
    q_cols = cols - 2 * HD
    pad = count.shape[0]
    n = Z * J
    vmem = pl.BlockSpec(memory_space=pltpu.VMEM)
    dma = pltpu.SemaphoreType.DMA
    bf16, f32 = jnp.bfloat16, jnp.float32
    return pl.pallas_call(
        functools.partial(step_kernel, Z, J, T),
        out_shape=jax.ShapeDtypeStruct((slots, width), bf16),
        in_specs=[vmem] * 5,
        out_specs=vmem,
        scratch_shapes=[
            pltpu.VMEM((n * part, cols), bf16),
            pltpu.VMEM((Z, T, slots, width), bf16),
            pltpu.VMEM((Z,) + count.shape, bf16),
            pltpu.VMEM((slots, LANES), f32),
            pltpu.VMEM((slots, LANES), f32),
            pltpu.VMEM((Z, q_cols // HD * slots, HD), bf16),
            pltpu.VMEM((n * (slots + pad), 2 * HD), bf16),
            pltpu.VMEM((n,) + w_out.shape, bf16),
            pltpu.VMEM((Z, slots, q_cols), bf16),
            pltpu.VMEM((Z, slots, q_cols), bf16),
            pltpu.VMEM((Z, slots, J * part), bf16),
            pltpu.VMEM((Z // T, slots, J * part), bf16),
            dma((Z,)), dma((n,)), dma((n,)), dma((n,)), dma((Z,)), dma((Z,)), dma((1,)), dma((1,)),
            dma((Z,)), dma((Z,)), dma((Z,)), dma((Z * T,)), dma((n,)), dma((n,)), dma((n,)),
            dma((2 * n,)), dma((2 * n,)), dma((2 * n,)), dma((2 * n,)), dma((2 * n,)),
            dma((Z,)), dma((Z,)), dma((Z,)), dma((Z // T,)),
        ],
        compiler_params=pltpu.CompilerParams(
            collective_id=0, has_side_effects=True, vmem_limit_bytes=56 * 1024 * 1024
        ),
    )(packed, count, gain, w_blocks, w_out)


def body(n_seq, n_tensor, hidden, depth, norm_gain, w_query, w_key, w_value, w_out):
    rows, width = hidden.shape
    slots = rows // 2
    d_model = width * n_tensor
    kv_heads = w_key.shape[1] // HD
    group = w_query.shape[1] // w_key.shape[1]
    J = kv_heads
    Z = n_seq // J
    part = w_query.shape[0]
    head_cols = (group + 2) * HD
    me = lax.axis_index("seq")
    t = lax.axis_index("tensor")
    j = lax.rem(me, J)
    z = me // J
    z_groups = [[a * J + b for a in range(Z)] for b in range(J)]

    def shift_j(value, k):
        pairs = [(a * J + b, a * J + (b + k) % J) for a in range(Z) for b in range(J)]
        return lax.ppermute(value, "seq", pairs)

    def shift_t(value, k):
        return lax.ppermute(value, "tensor", [(b, (b + k) % n_tensor) for b in range(n_tensor)])

    def gather_z(value, axis):
        return lax.all_gather(value, "seq", axis=axis, tiled=True, axis_index_groups=z_groups)

    def gather_j(value):
        return [value] + [shift_j(value, J - m) for m in range(1, J)]

    def exchange_j(block_for):
        return [block_for(j)] + [
            shift_j(block_for(lax.rem(j + J - m, J)), J - m) for m in range(1, J)
        ]

    living = depth > STEP
    index = jnp.arange(rows, dtype=jnp.int32)
    rank = jnp.sum(
        jnp.where(living[None, :] & (index[None, :] <= index[:, None]), 1, 0), axis=1
    ) - 1
    slot_ids = jnp.arange(slots, dtype=jnp.int32)
    select = (living[None, :] & (rank[None, :] == slot_ids[:, None])).astype(jnp.bfloat16)
    filled = jnp.sum(select.astype(jnp.float32), axis=1).astype(jnp.bfloat16)
    packed = jnp.dot(select, hidden, preferred_element_type=jnp.float32).astype(jnp.bfloat16)

    def columns_of(i):
        return jnp.concatenate(
            [
                lax.dynamic_slice_in_dim(w_query, i * group * HD, group * HD, axis=1),
                lax.dynamic_slice_in_dim(w_key, i * HD, HD, axis=1),
                lax.dynamic_slice_in_dim(w_value, i * HD, HD, axis=1),
            ],
            axis=1,
        )

    fast = (
        n_tensor == 2 and J == 4 and Z == kv_heads and Z > 2 and Z % n_tensor == 0 and slots % 16 == 0
        and slots <= 256 and part == w_out.shape[1] and part % 128 == 0 and width % 128 == 0
    )
    if fast:
        count = jnp.broadcast_to(jnp.sum(filled.astype(jnp.float32)), (16, 2 * HD)).astype(jnp.bfloat16)
        w_blocks = jnp.stack([columns_of(i) for i in range(kv_heads)])
        mixed = stepped(
            Z, J, n_tensor, packed, count, norm_gain.reshape(n_tensor, 1, width), w_blocks, w_out
        )
        return jnp.einsum(
            "sr,sf->rf", select, mixed, preferred_element_type=jnp.float32
        ).astype(jnp.bfloat16)

    w_rows = rolled(exchange_j(columns_of), 0, j)
    weights = gather_z(w_rows, 0)
    out_rows = group * HD
    twice = jnp.concatenate([w_out, w_out], axis=0) if J > 1 else w_out
    w_out_turned = lax.dynamic_slice_in_dim(twice, j * out_rows, J * out_rows, axis=0)
    out_weights = gather_z(w_out_turned, 1)

    features = rolled([packed] + [shift_t(packed, n_tensor - m) for m in range(1, n_tensor)], 1, t)
    widened = features.astype(jnp.float32)
    inverse = lax.rsqrt(jnp.mean(widened * widened, axis=1, keepdims=True) + EPSILON)
    normed = (widened * inverse * norm_gain[None, :]).astype(jnp.bfloat16)
    block_rows = J * slots
    tokens = jnp.concatenate(gather_j(normed), axis=0)
    flags = jnp.concatenate(gather_j(filled), axis=0)

    qkv = jnp.dot(tokens, weights, preferred_element_type=jnp.float32).astype(jnp.bfloat16)
    queries = qkv[:, : group * HD].reshape(block_rows, group, HD)
    kv = qkv[:, group * HD :]
    flag_rows = -(-block_rows // (2 * HD))
    flag_pad = -(-flag_rows // 16) * 16
    flag_block = jnp.pad(flags, (0, flag_pad * 2 * HD - block_rows)).reshape(flag_pad, 2 * HD)
    arrived = gather_z(jnp.concatenate([kv, flag_block], axis=0), 0).reshape(
        Z, block_rows + flag_pad, 2 * HD
    )
    keys = arrived[:, :block_rows, :HD].reshape(Z * block_rows, HD)
    values = arrived[:, :block_rows, HD:].reshape(Z * block_rows, HD)
    key_flags = arrived[:, block_rows:].reshape(Z, -1)[:, :block_rows].reshape(Z * block_rows)

    local = jnp.arange(block_rows, dtype=jnp.int32)
    turned = lax.rem(local // slots + j, J) * slots + lax.rem(local, slots)
    query_pos = z * block_rows + turned
    key_pos = (jnp.arange(Z, dtype=jnp.int32)[:, None] * block_rows + turned[None, :]).reshape(-1)
    visible = (key_flags[None, :] > 0) & (key_pos[None, :] <= query_pos[:, None])
    scores = jnp.einsum(
        "qgd,kd->gqk", queries, keys, preferred_element_type=jnp.float32
    ) * HD ** (-0.5)
    scores = jnp.where(visible[None], scores, MASKED_SCORE)
    expons = jnp.exp(scores - jnp.max(scores, axis=-1, keepdims=True))
    total = jnp.sum(expons, axis=-1)
    weighted = jnp.einsum(
        "gqk,kd->gqd", expons.astype(jnp.bfloat16), values, preferred_element_type=jnp.float32
    )
    attended = (weighted / total[..., None]).astype(jnp.bfloat16)
    attended = jnp.transpose(attended, (1, 0, 2)).reshape(block_rows, group * HD)
    attended = rolled([attended[m * slots : (m + 1) * slots] for m in range(J)], 0, j)
    heads = jnp.concatenate(gather_j(attended), axis=1)
    terms = jnp.dot(heads, out_weights, preferred_element_type=jnp.float32).astype(jnp.bfloat16)
    own_cols = w_out.shape[1]
    mine = exchange_j(lambda i: lax.dynamic_slice_in_dim(terms, i * slots, slots, axis=0))
    mine = [piece.reshape(slots, Z, 1, own_cols) for piece in mine]
    mine = rolled(mine, 2, j).reshape(slots, d_model)

    def features_of(i):
        return lax.dynamic_slice_in_dim(mine, i * width, width, axis=1)

    owned = features_of(t).astype(jnp.float32)
    for k in range(1, n_tensor):
        owned = owned + shift_t(features_of(lax.rem(t + k, n_tensor)), k).astype(jnp.float32)
    mixed = owned.astype(jnp.bfloat16)
    return jnp.einsum(
        "sr,sf->rf", select, mixed, preferred_element_type=jnp.float32
    ).astype(jnp.bfloat16)


def solution(mesh):
    n_seq, n_tensor = mesh.shape["seq"], mesh.shape["tensor"]

    def step(*args):
        return body(n_seq, n_tensor, *args)

    return jax.shard_map(
        step,
        mesh=mesh,
        in_specs=(
            P("seq", "tensor"),
            P("seq"),
            P(),
            P("seq", "tensor"),
            P("seq", "tensor"),
            P("seq", "tensor"),
            P("tensor", "seq"),
        ),
        out_specs=P("seq", "tensor"),
        check_vma=False,
    )
```

```python
import functools

import jax
import jax.numpy as jnp
from jax import lax
from jax.experimental import pallas as pl
from jax.experimental.pallas import tpu as pltpu
from jax.sharding import PartitionSpec as P

HD = 128
STEP = 2
EPSILON = 1e-05
MASKED_SCORE = -1e30


def rolled(pieces, axis, my):
    n = len(pieces)
    if n == 1:
        return pieces[0]
    width = pieces[0].shape[axis]
    twice = jnp.concatenate(pieces + pieces, axis=axis)
    start = lax.rem(n - my, n) * width
    return lax.dynamic_slice_in_dim(twice, start, n * width, axis=axis)


LANES = 128
MESH = pl.DeviceIdType.MESH


def step_kernel(
    Z, J, T, TC, OC, packed, count, gain, w_blocks, w_out, mixed_ref,
    weights, tokens, counts, sq_own, sq_other, queries, kv, outw, att, heads, terms, away, other,
    ws_z, ws_s, ws_x, wr, cs, cr, qs, qr, ts_up, ts_dn, ts_y, tr, ks_s, ks_x, kr,
    os_up, os_dn, os_s, orr, hs, hs_h, hr, xs, xr, ms, mr, ns, nr, ys, yr,
):
    me, t = lax.axis_index("seq"), lax.axis_index("tensor")
    z, j = me // J, lax.rem(me, J)
    slots, width = packed.shape
    part, cols = w_blocks.shape[1:]
    q_cols = cols - 2 * HD
    heads_here = q_cols // HD
    pad = counts.shape[1]
    block = slots + pad
    t_rows = slots // TC
    o_rows = w_out.shape[0] // OC
    share = Z // T
    x, c = j // 2, lax.rem(j, 2)
    sib = j + 1 - 2 * c
    across = lax.rem(j + J // 2, J)
    diag = lax.rem(sib + J // 2, J)
    has_up, has_down = z < Z - 1, z > 0

    low = 1 - z // (Z // 2)
    depth_in = low * z + (1 - low) * (Z - 1 - z)
    at_end, inside = depth_in == 0, depth_in > 0
    helps = depth_in == 1

    def mirrored(a):
        return low * a + (1 - low) * (Z - 1 - a)

    near = [z] + [mirrored(i - (i <= depth_in).astype(jnp.int32)) for i in range(1, Z)]
    end, far = mirrored(0), mirrored(Z - 1)

    def dev(zz, jj):
        return (zz * J + jj, t)

    sib_dev, across_dev, y_dev = dev(z, sib), dev(z, across), (me, T - 1 - t)
    up, down = dev(z + 1, j), dev(z - 1, j)
    inward, outward = dev(z + 2 * low - 1, j), dev(z + 1 - 2 * low, j)

    def if_(cond, act):
        if cond is None:
            act()
        else:
            pl.when(cond)(lambda: act())

    barrier = pltpu.get_barrier_semaphore()

    def greet(device):
        pl.semaphore_signal(barrier, inc=1, device_id=device, device_id_type=MESH)

    for i in range(1, Z):
        greet(dev(near[i], j))
    for device in (sib_dev, across_dev, y_dev):
        greet(device)
    if_(helps, lambda: greet(dev(end, across)))
    if_(at_end, lambda: greet(dev(mirrored(1), across)))
    pl.semaphore_wait(barrier, Z + 2 + (depth_in < 2).astype(jnp.int32))

    def copy(src, dst, send_sem, recv_sem, device):
        return pltpu.make_async_remote_copy(
            src_ref=src, dst_ref=dst, send_sem=send_sem, recv_sem=recv_sem,
            device_id=device, device_id_type=MESH,
        )

    started = []

    def start(cond, make):
        if_(cond, lambda: make().start())
        started.append((cond, make))

    def arrive(cond, make):
        if_(cond, lambda: make().wait_recv())

    def w_at(b):
        return weights.at[pl.ds(pl.multiple_of(b * part, part), part), :]

    def w_copy(b, sems, device, own=False):
        return copy(w_blocks.at[z] if own else w_at(b), w_at(b), sems.at[b], wr.at[b], device)

    def w_z(zz):
        return copy(w_blocks.at[zz], w_at(me), ws_z.at[zz], wr.at[me], dev(zz, j))

    def c_copy(zz, to):
        return copy(count, counts.at[zz], cs.at[to], cr.at[zz], dev(to, j))

    def t_copy(zz, tt, k, sems, device):
        at = tokens.at[zz, tt, pl.ds(k * t_rows, t_rows)]
        return copy(at, at, sems.at[zz * TC + k], tr.at[(zz * T + tt) * TC + k], device)

    def k_copy(b, sems, device):
        at = kv.at[pl.ds(pl.multiple_of(b * block, 16), block), :]
        return copy(at, at, sems.at[b], kr.at[b], device)

    def o_copy(zb, cc, k, sems, device, own=False):
        b = zb * 2 + cc
        rows = pl.ds(k * o_rows, o_rows)
        dst = outw.at[b, rows]
        return copy(
            w_out.at[rows] if own else dst, dst, sems.at[zb * OC + k], orr.at[b * OC + k], device
        )

    def h_copy(kind, zq, source, to):
        sems = (hs, hs_h)[kind]
        return copy(att.at[zq], heads.at[kind, 0, source], sems.at[zq], hr.at[kind * Z + source], dev(to, j))

    def x_copy(kind, source):
        i = kind * Z + source
        return copy(heads.at[kind, 0, source], heads.at[kind, 1, source], xs.at[i], xr.at[i], across_dev)

    def m_copy(zb, from_x, slot, device):
        return copy(away.at[slot], terms.at[zb, from_x], ms.at[slot], mr.at[zb], device)

    def n_copy():
        return copy(away.at[Z + 1], terms.at[far, x], ns.at[0], nr.at[0], dev(end, j))

    def y_copy(zb, xx):
        zl = lax.rem(zb, share)
        return copy(
            terms.at[zb, xx], other.at[zl, xx], ys.at[zb * 2 + xx], yr.at[zl * 2 + xx], y_dev
        )

    for i in range(1, Z):
        start(None, lambda zz=near[i]: c_copy(z, zz))
    for i in range(1, Z):
        start(None, lambda zz=near[i]: w_z(zz))
    start(None, lambda: w_copy(me, ws_x, across_dev, True))
    start(None, lambda: w_copy(me, ws_s, sib_dev, True))

    wide = packed[...].astype(jnp.float32)
    own_squares = jnp.sum(wide * wide, axis=1, keepdims=True)
    sq_own[...] = jnp.broadcast_to(own_squares, sq_own.shape)
    q_make = lambda: copy(sq_own, sq_other, qs.at[0], qr.at[0], y_dev)
    start(None, q_make)
    weights[pl.ds(pl.multiple_of(me * part, part), part), :] = w_blocks[z]
    counts[z] = count[...]
    arrive(None, q_make)
    squares = own_squares + sq_other[:, 0:1]
    inverse = lax.rsqrt(squares / (T * width) + EPSILON)
    tokens[z, t] = (packed[...].astype(jnp.float32) * inverse * gain[t]).astype(jnp.bfloat16)

    for k in range(TC):
        start(has_up, lambda k=k: t_copy(z, t, k, ts_up, up))
        start(has_down, lambda k=k: t_copy(z, t, k, ts_dn, down))
        start(None, lambda k=k: t_copy(z, t, k, ts_y, y_dev))

    def own_o(cond, sems_low, sems_high, device):
        for k in range(OC):
            start(cond & (low == 1), lambda k=k: o_copy(z, c, k, sems_low, device, True))
            start(cond & (low == 0), lambda k=k: o_copy(z, c, k, sems_high, device, True))

    own_o(at_end, os_up, os_dn, inward)
    for k in range(OC):
        start(None, lambda k=k: o_copy(z, c, k, os_s, sib_dev, True))
    outw[z * 2 + c] = w_out[...]

    def relay_w(i):
        b = near[i] * J + j
        arrive(None, lambda: w_copy(b, ws_s, sib_dev))
        start(None, lambda: w_copy(b, ws_x, across_dev))
        start(None, lambda: w_copy(b, ws_s, sib_dev))

    def relay_t(i, k, cond=None):
        zz = near[i]
        both = lambda more: more if cond is None else cond & more
        arrive(cond, lambda: t_copy(zz, t, k, ts_y, y_dev))
        start(both((zz < z) & has_up), lambda: t_copy(zz, t, k, ts_up, up))
        start(both((zz > z) & has_down), lambda: t_copy(zz, t, k, ts_dn, down))
        start(cond, lambda: t_copy(zz, t, k, ts_y, y_dev))

    def relay_o(i, ks, cond):
        zb = near[i]
        for k in ks:
            arrive(cond, lambda k=k: o_copy(zb, c, k, os_s, sib_dev))
            start(
                cond & (zb < z) & has_up & ~((z + 1 == Z - 1) & (zb == 0)),
                lambda k=k: o_copy(zb, c, k, os_up, up),
            )
            start(
                cond & (zb > z) & has_down & ~((z - 1 == 0) & (zb == Z - 1)),
                lambda k=k: o_copy(zb, c, k, os_dn, down),
            )
            start(cond, lambda k=k: o_copy(zb, c, k, os_s, sib_dev))

    def product(i):
        zz = near[i]
        for k in range(TC):
            arrive(None, lambda k=k: t_copy(zz, T - 1 - t, k, ts_y, y_dev))
        result = None
        for tt in range(T):
            term = jnp.dot(
                tokens[zz, tt], weights[tt * width : (tt + 1) * width, :],
                preferred_element_type=jnp.float32,
            )
            result = term if result is None else result + term
        for g in range(heads_here):
            queries[zz, g * slots : (g + 1) * slots, :] = result[
                :, g * HD : (g + 1) * HD
            ].astype(jnp.bfloat16)
        b = zz * J + j
        top = pl.multiple_of(b * block, 16)
        kv[pl.ds(top, slots), :] = result[:, q_cols:].astype(jnp.bfloat16)
        kv[pl.ds(pl.multiple_of(top + slots, 16), pad), :] = counts[zz]
        start(None, lambda: k_copy(b, ks_x, across_dev))
        start(None, lambda: k_copy(b, ks_s, sib_dev))

    early = min(2, TC)
    relay_w(1)
    for k in range(early):
        relay_t(1, k, at_end)
    for i in range(2, Z):
        relay_w(i)
    for k in range(early):
        relay_t(1, k, inside)
    for k in range(early, TC):
        relay_t(1, k)
    for i in range(2, Z - 1):
        for k in range(TC):
            relay_t(i, k)
    for zz in range(Z):
        b = zz * J + across
        arrive(None, lambda: w_copy(b, ws_s, sib_dev))
        start(None, lambda b=b: w_copy(b, ws_s, sib_dev))
    for i in range(1, Z):
        arrive(None, lambda: c_copy(near[i], z))
    for zz in range(Z):
        for jj in (sib, diag):
            arrive(None, lambda: w_copy(zz * J + jj, ws_s, sib_dev))

    product(0)
    for i in range(1, Z - 1):
        if i <= TC:
            relay_t(Z - 1, i - 1)
        product(i)
    for k in range(Z - 2, TC):
        relay_t(Z - 1, k)
    own_o(inside, os_dn, os_up, outward)
    own_o(inside, os_up, os_dn, inward)
    product(Z - 1)
    relay_o(1, range(0, 2), inside)
    for i in range(Z):
        b = near[i] * J + across
        arrive(None, lambda: k_copy(b, ks_s, sib_dev))
        start(None, lambda b=b: k_copy(b, ks_s, sib_dev))
    for zz in range(Z):
        for jj in (sib, diag):
            arrive(None, lambda: k_copy(zz * J + jj, ks_s, sib_dev))
    relay_o(2, range(0, 1), inside)

    keys = Z * J * block
    key_pos = lax.broadcasted_iota(jnp.int32, (1, keys), 1)
    seen = jnp.zeros((1, keys), jnp.float32)
    for b in range(Z * J):
        limit = kv[b * block + slots : b * block + slots + 1, 0:1].astype(jnp.float32) + b * block
        inside_b = (key_pos >= b * block) & (key_pos < (b + 1) * block)
        seen = jnp.where(inside_b & (key_pos.astype(jnp.float32) < limit), 1.0, seen)
    key_pos = jnp.where(seen > 0, key_pos, keys)
    row = lax.broadcasted_iota(jnp.int32, (slots, 1), 0)
    row = jnp.concatenate([row] * heads_here, axis=0) + j * block

    for zq in range(Z):
        n = (zq + 1) * J * block
        scores = lax.dot_general(
            queries[zq], kv[:n, :HD], (((1,), (1,)), ((), ())), preferred_element_type=jnp.float32
        ) * HD ** (-0.5)
        visible = key_pos[:, :n] <= row + zq * J * block
        scores = jnp.where(visible, scores, MASKED_SCORE)
        expons = jnp.exp(scores - jnp.max(scores, axis=1, keepdims=True))
        row_total = jnp.sum(expons, axis=1, keepdims=True)
        weighted = jnp.dot(
            expons.astype(jnp.bfloat16), kv[:n, HD:], preferred_element_type=jnp.float32
        )
        attended = (weighted / row_total).astype(jnp.bfloat16)
        for g in range(heads_here):
            att[zq, :, g * HD : (g + 1) * HD] = attended[g * slots : (g + 1) * slots]

        @pl.when(z == zq)
        def _():
            heads[0, 0, z] = att[zq]

        start(z != zq, lambda zq=zq: h_copy(0, zq, z, zq))
        if zq in (0, Z - 1):
            helper = 1 if zq == 0 else Z - 2

            @pl.when(z == helper)
            def _():
                heads[1, 0, z] = att[zq]

            start(z != helper, lambda zq=zq, helper=helper: h_copy(1, zq, z, helper))

    start(None, lambda: x_copy(0, z))
    start(helps, lambda: x_copy(1, z))
    relay_o(1, range(2, OC), inside)
    relay_o(2, range(1, OC), inside)
    relay_o(1, range(OC), at_end)
    for kind, cond in ((0, None), (1, helps)):
        for i in range(1, Z):
            arrive(cond, lambda: h_copy(kind, 0, near[i], z))
            start(cond, lambda kind=kind, i=i: x_copy(kind, near[i]))
    relay_o(Z - 1, range(0, 2), inside)
    for zz in range(Z):
        arrive(None, lambda: x_copy(0, zz))

    def emit(kind, zb, own_slot, away_slot):
        every = jnp.concatenate(
            [
                jnp.concatenate([heads[kind, xx, zz] for zz in range(Z)], axis=1)
                for xx in range(2)
            ],
            axis=0,
        )
        if kind == 0:
            for k in range(OC):
                o_copy(zb, 1 - c, k, os_s, sib_dev).wait_recv()
        for cc in range(2):
            result = jnp.dot(
                every, outw[zb * 2 + cc], preferred_element_type=jnp.float32
            ).astype(jnp.bfloat16)
            at = slice(cc * part, (cc + 1) * part)
            if own_slot is None:
                terms[zb, x, :, at] = result[:slots]
            else:
                away[own_slot, :, at] = result[:slots]
            away[away_slot, :, at] = result[slots:]

    def emit_own(zb):
        emit(0, zb, None, zb)
        start(None, lambda: m_copy(zb, x, zb, across_dev))
        start(zb // share != t, lambda: y_copy(zb, x))

    def collect(zb, cond=None):
        arrive(cond, lambda: m_copy(zb, x, zb, across_dev))
        leaves = zb // share != t
        start(leaves if cond is None else cond & leaves, lambda: y_copy(zb, 1 - x))

    emit_own(z)
    emit_own(near[1])
    relay_o(Z - 1, range(2, OC), inside)
    collect(z, inside)

    @pl.when(inside)
    def _():
        emit(0, far, None, far)

    start(inside, lambda: m_copy(far, x, far, across_dev))
    start(inside & (far // share != t), lambda: y_copy(far, x))
    for zz in range(Z):
        arrive(helps, lambda: x_copy(1, zz))

    @pl.when(helps)
    def _():
        emit(1, far, Z + 1, Z)

    start(helps, n_copy)
    start(helps, lambda: m_copy(far, x, Z, dev(end, across)))
    relay_o(2, range(OC), at_end)
    emit_own(near[2])
    collect(z, at_end)
    collect(near[1])
    collect(near[2])
    arrive(at_end, n_copy)
    start(at_end & (far // share != t), lambda: y_copy(far, x))
    collect(far)

    for zl in range(share):
        zb = t * share + zl
        for xx in range(2):
            y_copy(zl, xx).wait_recv()
            top = (zl * 2 + xx) * 2 * part
            mixed_ref[:, top : top + 2 * part] = (
                terms[zb, xx].astype(jnp.float32) + other[zl, xx].astype(jnp.float32)
            ).astype(jnp.bfloat16)

    for cond, make in started:
        if_(cond, lambda: make().wait_send())


def stepped(Z, J, T, packed, count, gain, w_blocks, w_out):
    slots, width = packed.shape
    part, cols = w_blocks.shape[1:]
    q_cols = cols - 2 * HD
    pad = count.shape[0]
    n = Z * J
    TC = slots // 32 if slots % 32 == 0 else 1
    OC = 4
    vmem = pl.BlockSpec(memory_space=pltpu.VMEM)
    dma = pltpu.SemaphoreType.DMA
    bf16, f32 = jnp.bfloat16, jnp.float32
    return pl.pallas_call(
        functools.partial(step_kernel, Z, J, T, TC, OC),
        out_shape=jax.ShapeDtypeStruct((slots, width), bf16),
        in_specs=[vmem] * 5,
        out_specs=vmem,
        scratch_shapes=[
            pltpu.VMEM((n * part, cols), bf16),
            pltpu.VMEM((Z, T, slots, width), bf16),
            pltpu.VMEM((Z,) + count.shape, bf16),
            pltpu.VMEM((slots, LANES), f32),
            pltpu.VMEM((slots, LANES), f32),
            pltpu.VMEM((Z, q_cols // HD * slots, HD), bf16),
            pltpu.VMEM((n * (slots + pad), 2 * HD), bf16),
            pltpu.VMEM((Z * 2,) + w_out.shape, bf16),
            pltpu.VMEM((Z, slots, q_cols), bf16),
            pltpu.VMEM((2, 2, Z, slots, q_cols), bf16),
            pltpu.VMEM((Z, 2, slots, 2 * part), bf16),
            pltpu.VMEM((Z + 2, slots, 2 * part), bf16),
            pltpu.VMEM((Z // T, 2, slots, 2 * part), bf16),
            dma((Z,)), dma((n,)), dma((n,)), dma((n,)), dma((Z,)), dma((Z,)), dma((1,)), dma((1,)),
            dma((Z * TC,)), dma((Z * TC,)), dma((Z * TC,)), dma((Z * T * TC,)),
            dma((n,)), dma((n,)), dma((n,)),
            dma((Z * OC,)), dma((Z * OC,)), dma((Z * OC,)), dma((Z * 2 * OC,)),
            dma((Z,)), dma((Z,)), dma((2 * Z,)), dma((2 * Z,)), dma((2 * Z,)),
            dma((Z + 1,)), dma((Z,)), dma((1,)), dma((1,)), dma((2 * Z,)), dma((Z // T * 2,)),
        ],
        compiler_params=pltpu.CompilerParams(
            collective_id=0, has_side_effects=True, vmem_limit_bytes=32 * 1024 * 1024
        ),
    )(packed, count, gain, w_blocks, w_out)


def body(n_seq, n_tensor, hidden, depth, norm_gain, w_query, w_key, w_value, w_out):
    rows, width = hidden.shape
    slots = rows // 2
    d_model = width * n_tensor
    kv_heads = w_key.shape[1] // HD
    group = w_query.shape[1] // w_key.shape[1]
    J = kv_heads
    Z = n_seq // J
    part = w_query.shape[0]
    head_cols = (group + 2) * HD
    me = lax.axis_index("seq")
    t = lax.axis_index("tensor")
    j = lax.rem(me, J)
    z = me // J
    z_groups = [[a * J + b for a in range(Z)] for b in range(J)]

    def shift_j(value, k):
        pairs = [(a * J + b, a * J + (b + k) % J) for a in range(Z) for b in range(J)]
        return lax.ppermute(value, "seq", pairs)

    def shift_t(value, k):
        return lax.ppermute(value, "tensor", [(b, (b + k) % n_tensor) for b in range(n_tensor)])

    def gather_z(value, axis):
        return lax.all_gather(value, "seq", axis=axis, tiled=True, axis_index_groups=z_groups)

    def gather_j(value):
        return [value] + [shift_j(value, J - m) for m in range(1, J)]

    def exchange_j(block_for):
        return [block_for(j)] + [
            shift_j(block_for(lax.rem(j + J - m, J)), J - m) for m in range(1, J)
        ]

    living = depth > STEP
    index = jnp.arange(rows, dtype=jnp.int32)
    rank = jnp.sum(
        jnp.where(living[None, :] & (index[None, :] <= index[:, None]), 1, 0), axis=1
    ) - 1
    slot_ids = jnp.arange(slots, dtype=jnp.int32)
    select = (living[None, :] & (rank[None, :] == slot_ids[:, None])).astype(jnp.bfloat16)
    filled = jnp.sum(select.astype(jnp.float32), axis=1).astype(jnp.bfloat16)
    packed = jnp.dot(select, hidden, preferred_element_type=jnp.float32).astype(jnp.bfloat16)

    def columns_of(i):
        return jnp.concatenate(
            [
                lax.dynamic_slice_in_dim(w_query, i * group * HD, group * HD, axis=1),
                lax.dynamic_slice_in_dim(w_key, i * HD, HD, axis=1),
                lax.dynamic_slice_in_dim(w_value, i * HD, HD, axis=1),
            ],
            axis=1,
        )

    fast = (
        n_tensor == 2 and J == 4 and Z == kv_heads and Z == J and Z % n_tensor == 0 and slots % 16 == 0
        and slots <= 256 and part == w_out.shape[1] and part % 128 == 0 and width % 128 == 0 and w_out.shape[0] % 64 == 0
    )
    if fast:
        count = jnp.broadcast_to(jnp.sum(filled.astype(jnp.float32)), (16, 2 * HD)).astype(jnp.bfloat16)
        w_blocks = jnp.stack([columns_of(i) for i in range(kv_heads)])
        mixed = stepped(
            Z, J, n_tensor, packed, count, norm_gain.reshape(n_tensor, 1, width), w_blocks, w_out
        )
        return jnp.einsum(
            "sr,sf->rf", select, mixed, preferred_element_type=jnp.float32
        ).astype(jnp.bfloat16)

    w_rows = rolled(exchange_j(columns_of), 0, j)
    weights = gather_z(w_rows, 0)
    out_rows = group * HD
    twice = jnp.concatenate([w_out, w_out], axis=0) if J > 1 else w_out
    w_out_turned = lax.dynamic_slice_in_dim(twice, j * out_rows, J * out_rows, axis=0)
    out_weights = gather_z(w_out_turned, 1)

    features = rolled([packed] + [shift_t(packed, n_tensor - m) for m in range(1, n_tensor)], 1, t)
    widened = features.astype(jnp.float32)
    inverse = lax.rsqrt(jnp.mean(widened * widened, axis=1, keepdims=True) + EPSILON)
    normed = (widened * inverse * norm_gain[None, :]).astype(jnp.bfloat16)
    block_rows = J * slots
    tokens = jnp.concatenate(gather_j(normed), axis=0)
    flags = jnp.concatenate(gather_j(filled), axis=0)

    qkv = jnp.dot(tokens, weights, preferred_element_type=jnp.float32).astype(jnp.bfloat16)
    queries = qkv[:, : group * HD].reshape(block_rows, group, HD)
    kv = qkv[:, group * HD :]
    flag_rows = -(-block_rows // (2 * HD))
    flag_pad = -(-flag_rows // 16) * 16
    flag_block = jnp.pad(flags, (0, flag_pad * 2 * HD - block_rows)).reshape(flag_pad, 2 * HD)
    arrived = gather_z(jnp.concatenate([kv, flag_block], axis=0), 0).reshape(
        Z, block_rows + flag_pad, 2 * HD
    )
    keys = arrived[:, :block_rows, :HD].reshape(Z * block_rows, HD)
    values = arrived[:, :block_rows, HD:].reshape(Z * block_rows, HD)
    key_flags = arrived[:, block_rows:].reshape(Z, -1)[:, :block_rows].reshape(Z * block_rows)

    local = jnp.arange(block_rows, dtype=jnp.int32)
    turned = lax.rem(local // slots + j, J) * slots + lax.rem(local, slots)
    query_pos = z * block_rows + turned
    key_pos = (jnp.arange(Z, dtype=jnp.int32)[:, None] * block_rows + turned[None, :]).reshape(-1)
    visible = (key_flags[None, :] > 0) & (key_pos[None, :] <= query_pos[:, None])
    scores = jnp.einsum(
        "qgd,kd->gqk", queries, keys, preferred_element_type=jnp.float32
    ) * HD ** (-0.5)
    scores = jnp.where(visible[None], scores, MASKED_SCORE)
    expons = jnp.exp(scores - jnp.max(scores, axis=-1, keepdims=True))
    total = jnp.sum(expons, axis=-1)
    weighted = jnp.einsum(
        "gqk,kd->gqd", expons.astype(jnp.bfloat16), values, preferred_element_type=jnp.float32
    )
    attended = (weighted / total[..., None]).astype(jnp.bfloat16)
    attended = jnp.transpose(attended, (1, 0, 2)).reshape(block_rows, group * HD)
    attended = rolled([attended[m * slots : (m + 1) * slots] for m in range(J)], 0, j)
    heads = jnp.concatenate(gather_j(attended), axis=1)
    terms = jnp.dot(heads, out_weights, preferred_element_type=jnp.float32).astype(jnp.bfloat16)
    own_cols = w_out.shape[1]
    mine = exchange_j(lambda i: lax.dynamic_slice_in_dim(terms, i * slots, slots, axis=0))
    mine = [piece.reshape(slots, Z, 1, own_cols) for piece in mine]
    mine = rolled(mine, 2, j).reshape(slots, d_model)

    def features_of(i):
        return lax.dynamic_slice_in_dim(mine, i * width, width, axis=1)

    owned = features_of(t).astype(jnp.float32)
    for k in range(1, n_tensor):
        owned = owned + shift_t(features_of(lax.rem(t + k, n_tensor)), k).astype(jnp.float32)
    mixed = owned.astype(jnp.bfloat16)
    return jnp.einsum(
        "sr,sf->rf", select, mixed, preferred_element_type=jnp.float32
    ).astype(jnp.bfloat16)


def solution(mesh):
    n_seq, n_tensor = mesh.shape["seq"], mesh.shape["tensor"]

    def step(*args):
        return body(n_seq, n_tensor, *args)

    return jax.shard_map(
        step,
        mesh=mesh,
        in_specs=(
            P("seq", "tensor"),
            P("seq"),
            P(),
            P("seq", "tensor"),
            P("seq", "tensor"),
            P("seq", "tensor"),
            P("tensor", "seq"),
        ),
        out_specs=P("seq", "tensor"),
        check_vma=False,
    )
```

```python
import functools

import jax
import jax.numpy as jnp
from jax import lax
from jax.experimental import pallas as pl
from jax.experimental.pallas import tpu as pltpu
from jax.sharding import PartitionSpec as P

HD = 128
STEP = 2
EPSILON = 1e-05
MASKED_SCORE = -1e30


def rolled(pieces, axis, my):
    n = len(pieces)
    if n == 1:
        return pieces[0]
    width = pieces[0].shape[axis]
    twice = jnp.concatenate(pieces + pieces, axis=axis)
    start = lax.rem(n - my, n) * width
    return lax.dynamic_slice_in_dim(twice, start, n * width, axis=axis)


LANES = 128
MESH = pl.DeviceIdType.MESH


def step_kernel(
    Z, J, T, TC, OC, depth, gain, hidden, w_query, w_key, w_value, w_out, mixed_ref, select_ref,
    raw, w_blocks, weights, tokens, counts, sq_own, sq_other, queries, kv, outw, att, heads, terms, away, other,
    ws_z, ws_s, ws_x, wr, cs, cr, qs, qr, ts_up, ts_dn, ts_y, tr, ks_s, ks_x, kr,
    os_up, os_dn, os_s, orr, hs, hs_h, hr, xs, xr, ms, mr, ns, nr, ys, yr, ls, lw,
):
    me, t = lax.axis_index("seq"), lax.axis_index("tensor")
    z, j = me // J, lax.rem(me, J)
    rows, width = hidden.shape
    slots = mixed_ref.shape[0]
    part, cols = w_blocks.shape[1:]
    q_cols = cols - 2 * HD
    heads_here = q_cols // HD
    pad = counts.shape[1]
    block = slots + pad
    t_rows = slots // TC
    o_rows = w_out.shape[0] // OC
    share = Z // T
    x, c = j // 2, lax.rem(j, 2)
    sib = j + 1 - 2 * c
    across = lax.rem(j + J // 2, J)
    diag = lax.rem(sib + J // 2, J)
    has_up, has_down = z < Z - 1, z > 0

    low = 1 - z // (Z // 2)
    depth_in = low * z + (1 - low) * (Z - 1 - z)
    at_end, inside = depth_in == 0, depth_in > 0
    helps = depth_in == 1

    def mirrored(a):
        return low * a + (1 - low) * (Z - 1 - a)

    near = [z] + [mirrored(i - (i <= depth_in).astype(jnp.int32)) for i in range(1, Z)]
    end, far = mirrored(0), mirrored(Z - 1)

    ty = T - 1 - t

    def dev(zz, jj, tt=t):
        return (zz * J + jj, tt)

    sib_dev, across_dev, y_dev = dev(z, sib), dev(z, across), (me, ty)
    mid = mirrored(1)
    up, down = dev(z + 1, j), dev(z - 1, j)
    inward, outward = dev(z + 2 * low - 1, j), dev(z + 1 - 2 * low, j)

    def if_(cond, act):
        if cond is None:
            act()
        else:
            pl.when(cond)(lambda: act())

    barrier = pltpu.get_barrier_semaphore()

    def greet(device):
        pl.semaphore_signal(barrier, inc=1, device_id=device, device_id_type=MESH)

    for i in range(1, Z):
        greet(dev(near[i], j))
    for device in (sib_dev, across_dev, y_dev, dev(z, across, ty)):
        greet(device)
    for jj, tt in ((across, t), (across, ty), (j, ty)):
        if_(helps, lambda: greet(dev(end, jj, tt)))
        if_(at_end, lambda: greet(dev(mid, jj, tt)))

    local = []

    def bring(src, dst, sem):
        moved = pltpu.make_async_copy(src, dst, sem)
        moved.start()
        return moved

    fetched = bring(hidden, raw, ls.at[0])
    own_rows = pl.ds(pl.multiple_of(me * part, part), part)
    for i in range(Z + 1):
        zz = i if i < Z else z
        for n, (w, first, size) in enumerate(
            ((w_query, 0, q_cols), (w_key, q_cols, HD), (w_value, q_cols + HD, HD))
        ):
            to = slice(first, first + size)
            local.append(
                bring(
                    w.at[:, pl.ds(pl.multiple_of(zz * size, HD), size)],
                    w_blocks.at[i, :, to] if i < Z else weights.at[own_rows, to],
                    lw.at[3 * i + n],
                )
            )
    placed = bring(w_out, outw.at[z * 2 + c], ls.at[1])

    living = (depth[...] > STEP).astype(jnp.float32)
    before = lax.broadcasted_iota(jnp.int32, (rows, rows), 0)
    before = before <= lax.broadcasted_iota(jnp.int32, (rows, rows), 1)
    rank = jnp.dot(
        jnp.broadcast_to(living, (16, rows)).astype(jnp.bfloat16),
        before.astype(jnp.bfloat16),
        preferred_element_type=jnp.float32,
    )[0:1]
    slot = lax.broadcasted_iota(jnp.int32, (slots, rows), 0).astype(jnp.float32) + 1.0
    select = jnp.where((rank == slot) & (living > 0), 1.0, 0.0).astype(jnp.bfloat16)
    select_ref[...] = select
    total = jnp.sum(living, axis=1, keepdims=True)
    counts[z] = jnp.broadcast_to(total, counts.shape[1:]).astype(jnp.bfloat16)
    fetched.wait()
    wide = jnp.dot(select, raw[...], preferred_element_type=jnp.float32)
    own_squares = jnp.sum(wide * wide, axis=1, keepdims=True)
    sq_own[...] = jnp.broadcast_to(own_squares, sq_own.shape)
    for moved in local:
        moved.wait()
    pl.semaphore_wait(barrier, Z + 3 + 3 * (depth_in < 2).astype(jnp.int32))

    def copy(src, dst, send_sem, recv_sem, device):
        return pltpu.make_async_remote_copy(
            src_ref=src, dst_ref=dst, send_sem=send_sem, recv_sem=recv_sem,
            device_id=device, device_id_type=MESH,
        )

    started = []

    def start(cond, make):
        if_(cond, lambda: make().start())
        started.append((cond, make))

    def arrive(cond, make):
        if_(cond, lambda: make().wait_recv())

    def w_at(b):
        return weights.at[pl.ds(pl.multiple_of(b * part, part), part), :]

    def w_copy(b, sems, device, own=False):
        return copy(w_blocks.at[z] if own else w_at(b), w_at(b), sems.at[b], wr.at[b], device)

    def w_z(zz):
        return copy(w_blocks.at[zz], w_at(me), ws_z.at[zz], wr.at[me], dev(zz, j))

    def c_copy(zz, to):
        return copy(counts.at[zz], counts.at[zz], cs.at[to], cr.at[zz], dev(to, j))

    def t_copy(zz, tt, k, sems, device):
        at = tokens.at[zz, tt, pl.ds(k * t_rows, t_rows)]
        return copy(at, at, sems.at[zz * TC + k], tr.at[(zz * T + tt) * TC + k], device)

    def k_copy(b, sems, device):
        at = kv.at[pl.ds(pl.multiple_of(b * block, 16), block), :]
        return copy(at, at, sems.at[b], kr.at[b], device)

    def o_copy(zb, cc, k, sems, device):
        b = zb * 2 + cc
        at = outw.at[b, pl.ds(k * o_rows, o_rows)]
        return copy(at, at, sems.at[zb * OC + k], orr.at[b * OC + k], device)

    def h_copy(kind, zq, source, to):
        sems = (hs, hs_h)[kind]
        return copy(att.at[zq], heads.at[kind, 0, source], sems.at[zq], hr.at[kind * Z + source], dev(to, j))

    def x_copy(kind, source):
        i = kind * Z + source
        return copy(heads.at[kind, 0, source], heads.at[kind, 1, source], xs.at[i], xr.at[i], across_dev)

    def m_copy(zb, slot, zz, leaving):
        zl = lax.rem(zb, share)
        if leaving:
            return copy(
                away.at[slot], other.at[zl, x], ms.at[slot], yr.at[zl * 2 + x], dev(zz, across, ty)
            )
        return copy(away.at[slot], terms.at[zb, x], ms.at[slot], mr.at[zb], dev(zz, across))

    def n_copy(leaving):
        zl = lax.rem(far, share)
        if leaving:
            return copy(away.at[Z + 1], other.at[zl, x], ns.at[0], yr.at[zl * 2 + x], dev(end, j, ty))
        return copy(away.at[Z + 1], terms.at[far, x], ns.at[0], nr.at[0], dev(end, j))

    def y_copy(zb, xx):
        zl = lax.rem(zb, share)
        return copy(
            terms.at[zb, xx], other.at[zl, xx], ys.at[zb * 2 + xx], yr.at[zl * 2 + xx], y_dev
        )

    for i in range(1, Z):
        start(None, lambda zz=near[i]: c_copy(z, zz))
    for i in range(1, Z):
        start(None, lambda zz=near[i]: w_z(zz))
    start(None, lambda: w_copy(me, ws_x, across_dev, True))
    start(None, lambda: w_copy(me, ws_s, sib_dev, True))

    q_make = lambda: copy(sq_own, sq_other, qs.at[0], qr.at[0], y_dev)
    start(None, q_make)
    arrive(None, q_make)
    squares = own_squares + sq_other[:, 0:1]
    inverse = lax.rsqrt(squares / (T * width) + EPSILON)
    tokens[z, t] = (wide * inverse * gain[t]).astype(jnp.bfloat16)

    for k in range(TC):
        start(has_up, lambda k=k: t_copy(z, t, k, ts_up, up))
        start(has_down, lambda k=k: t_copy(z, t, k, ts_dn, down))
        start(None, lambda k=k: t_copy(z, t, k, ts_y, y_dev))

    def own_o(cond, sems_low, sems_high, device):
        for k in range(OC):
            start(cond & (low == 1), lambda k=k: o_copy(z, c, k, sems_low, device))
            start(cond & (low == 0), lambda k=k: o_copy(z, c, k, sems_high, device))

    placed.wait()
    own_o(at_end, os_up, os_dn, inward)
    for k in range(OC):
        start(None, lambda k=k: o_copy(z, c, k, os_s, sib_dev))

    def relay_w(i):
        b = near[i] * J + j
        arrive(None, lambda: w_copy(b, ws_s, sib_dev))
        start(None, lambda: w_copy(b, ws_x, across_dev))
        start(None, lambda: w_copy(b, ws_s, sib_dev))

    def relay_t(i, k, cond=None):
        zz = near[i]
        both = lambda more: more if cond is None else cond & more
        arrive(cond, lambda: t_copy(zz, t, k, ts_y, y_dev))
        start(both((zz < z) & has_up), lambda: t_copy(zz, t, k, ts_up, up))
        start(both((zz > z) & has_down), lambda: t_copy(zz, t, k, ts_dn, down))
        start(cond, lambda: t_copy(zz, t, k, ts_y, y_dev))

    def relay_o(i, ks, cond):
        zb = near[i]
        for k in ks:
            arrive(cond, lambda k=k: o_copy(zb, c, k, os_s, sib_dev))
            start(
                cond & (zb < z) & has_up & ~((z + 1 == Z - 1) & (zb == 0)),
                lambda k=k: o_copy(zb, c, k, os_up, up),
            )
            start(
                cond & (zb > z) & has_down & ~((z - 1 == 0) & (zb == Z - 1)),
                lambda k=k: o_copy(zb, c, k, os_dn, down),
            )
            start(cond, lambda k=k: o_copy(zb, c, k, os_s, sib_dev))

    def product(i):
        zz = near[i]
        for k in range(TC):
            arrive(None, lambda k=k: t_copy(zz, T - 1 - t, k, ts_y, y_dev))
        result = None
        for tt in range(T):
            term = jnp.dot(
                tokens[zz, tt], weights[tt * width : (tt + 1) * width, :],
                preferred_element_type=jnp.float32,
            )
            result = term if result is None else result + term
        for g in range(heads_here):
            queries[zz, g * slots : (g + 1) * slots, :] = result[
                :, g * HD : (g + 1) * HD
            ].astype(jnp.bfloat16)
        b = zz * J + j
        top = pl.multiple_of(b * block, 16)
        kv[pl.ds(top, slots), :] = result[:, q_cols:].astype(jnp.bfloat16)
        kv[pl.ds(pl.multiple_of(top + slots, 16), pad), :] = counts[zz]
        start(None, lambda: k_copy(b, ks_x, across_dev))
        start(None, lambda: k_copy(b, ks_s, sib_dev))

    early = min(2, TC)
    relay_w(1)
    for k in range(early):
        relay_t(1, k, at_end)
    for i in range(2, Z):
        relay_w(i)
    for k in range(early):
        relay_t(1, k, inside)
    for k in range(early, TC):
        relay_t(1, k)
    for i in range(2, Z - 1):
        for k in range(TC):
            relay_t(i, k)
    for zz in range(Z):
        b = zz * J + across
        arrive(None, lambda: w_copy(b, ws_s, sib_dev))
        start(None, lambda b=b: w_copy(b, ws_s, sib_dev))
    for i in range(1, Z):
        arrive(None, lambda: c_copy(near[i], z))
    for zz in range(Z):
        for jj in (sib, diag):
            arrive(None, lambda: w_copy(zz * J + jj, ws_s, sib_dev))

    product(0)
    for i in range(1, Z - 1):
        if i <= TC:
            relay_t(Z - 1, i - 1)
        product(i)
    for k in range(Z - 2, TC):
        relay_t(Z - 1, k)
    own_o(inside, os_dn, os_up, outward)
    own_o(inside, os_up, os_dn, inward)
    product(Z - 1)
    relay_o(1, range(0, 2), inside)
    for i in range(Z):
        b = near[i] * J + across
        arrive(None, lambda: k_copy(b, ks_s, sib_dev))
        start(None, lambda b=b: k_copy(b, ks_s, sib_dev))
    for zz in range(Z):
        for jj in (sib, diag):
            arrive(None, lambda: k_copy(zz * J + jj, ks_s, sib_dev))
    relay_o(2, range(0, 1), inside)

    keys = Z * J * block
    key_pos = lax.broadcasted_iota(jnp.int32, (1, keys), 1)
    seen = jnp.zeros((1, keys), jnp.float32)
    for b in range(Z * J):
        limit = kv[b * block + slots : b * block + slots + 1, 0:1].astype(jnp.float32) + b * block
        inside_b = (key_pos >= b * block) & (key_pos < (b + 1) * block)
        seen = jnp.where(inside_b & (key_pos.astype(jnp.float32) < limit), 1.0, seen)
    key_pos = jnp.where(seen > 0, key_pos, keys)
    row = lax.broadcasted_iota(jnp.int32, (slots, 1), 0)
    row = jnp.concatenate([row] * heads_here, axis=0) + j * block

    for zq in range(Z):
        n = (zq + 1) * J * block
        scores = lax.dot_general(
            queries[zq], kv[:n, :HD], (((1,), (1,)), ((), ())), preferred_element_type=jnp.float32
        ) * HD ** (-0.5)
        visible = key_pos[:, :n] <= row + zq * J * block
        scores = jnp.where(visible, scores, MASKED_SCORE)
        expons = jnp.exp(scores - jnp.max(scores, axis=1, keepdims=True))
        row_total = jnp.sum(expons, axis=1, keepdims=True)
        weighted = jnp.dot(
            expons.astype(jnp.bfloat16), kv[:n, HD:], preferred_element_type=jnp.float32
        )
        attended = (weighted / row_total).astype(jnp.bfloat16)
        for g in range(heads_here):
            att[zq, :, g * HD : (g + 1) * HD] = attended[g * slots : (g + 1) * slots]

        @pl.when(z == zq)
        def _():
            heads[0, 0, z] = att[zq]

        start(z != zq, lambda zq=zq: h_copy(0, zq, z, zq))
        if zq in (0, Z - 1):
            helper = 1 if zq == 0 else Z - 2

            @pl.when(z == helper)
            def _():
                heads[1, 0, z] = att[zq]

            start(z != helper, lambda zq=zq, helper=helper: h_copy(1, zq, z, helper))

    start(None, lambda: x_copy(0, z))
    start(helps, lambda: x_copy(1, z))
    relay_o(1, range(2, OC), inside)
    relay_o(2, range(1, OC), inside)
    relay_o(1, range(OC), at_end)
    for kind, cond in ((0, None), (1, helps)):
        for i in range(1, Z):
            arrive(cond, lambda: h_copy(kind, 0, near[i], z))
            start(cond, lambda kind=kind, i=i: x_copy(kind, near[i]))
    relay_o(Z - 1, range(0, 2), inside)
    for zz in range(Z):
        arrive(None, lambda: x_copy(0, zz))

    def emit(kind, zb, own_slot, away_slot):
        every = jnp.concatenate(
            [
                jnp.concatenate([heads[kind, xx, zz] for zz in range(Z)], axis=1)
                for xx in range(2)
            ],
            axis=0,
        )
        if kind == 0:
            for k in range(OC):
                o_copy(zb, 1 - c, k, os_s, sib_dev).wait_recv()
        for cc in range(2):
            result = jnp.dot(
                every, outw[zb * 2 + cc], preferred_element_type=jnp.float32
            ).astype(jnp.bfloat16)
            at = slice(cc * part, (cc + 1) * part)
            if own_slot is None:
                terms[zb, x, :, at] = result[:slots]
            else:
                away[own_slot, :, at] = result[:slots]
            away[away_slot, :, at] = result[slots:]

    def hand_out(zb, slot, zz, cond=None):
        stays = zb // share == t
        leaves = zb // share != t
        if cond is not None:
            stays, leaves = cond & stays, cond & leaves
        start(stays, lambda: m_copy(zb, slot, zz, False))
        start(leaves, lambda: m_copy(zb, slot, zz, True))
        return stays, leaves

    def emit_own(zb, cond=None):
        if_(cond, lambda: emit(0, zb, None, zb))
        _, leaves = hand_out(zb, zb, z, cond)
        start(leaves, lambda: y_copy(zb, x))

    emit_own(z)
    emit_own(near[1])
    relay_o(Z - 1, range(2, OC), inside)
    emit_own(far, inside)
    for zz in range(Z):
        arrive(helps, lambda: x_copy(1, zz))
    if_(helps, lambda: emit(1, far, Z + 1, Z))
    stays, leaves = hand_out(far, Z, end, helps)
    start(stays, lambda: n_copy(False))
    start(leaves, lambda: n_copy(True))
    relay_o(2, range(OC), at_end)
    emit_own(near[2])

    for zl in range(share):
        zb = t * share + zl
        arrive(None, lambda: m_copy(zb, zb, z, False))
        arrive(at_end & (zb == far), lambda: n_copy(False))
        for xx in range(2):
            y_copy(zl, xx).wait_recv()
            top = (zl * 2 + xx) * 2 * part
            mixed_ref[:, top : top + 2 * part] = (
                terms[zb, xx].astype(jnp.float32) + other[zl, xx].astype(jnp.float32)
            ).astype(jnp.bfloat16)

    for cond, make in started:
        if_(cond, lambda: make().wait_send())


def stepped(Z, J, T, slots, depth, gain, hidden, w_query, w_key, w_value, w_out):
    rows, width = hidden.shape
    part = w_query.shape[0]
    q_cols = w_query.shape[1] // Z
    cols = q_cols + 2 * HD
    pad = 16
    n = Z * J
    TC = slots // 32 if slots % 32 == 0 else 1
    OC = 4
    vmem = pl.BlockSpec(memory_space=pltpu.VMEM)
    dma = pltpu.SemaphoreType.DMA
    bf16, f32 = jnp.bfloat16, jnp.float32
    return pl.pallas_call(
        functools.partial(step_kernel, Z, J, T, TC, OC),
        out_shape=(
            jax.ShapeDtypeStruct((slots, width), bf16), jax.ShapeDtypeStruct((slots, rows), bf16)
        ),
        in_specs=[vmem] * 2 + [pl.BlockSpec(memory_space=pltpu.HBM)] * 5,
        out_specs=(vmem, vmem),
        scratch_shapes=[
            pltpu.VMEM((rows, width), bf16),
            pltpu.VMEM((Z, part, cols), bf16),
            pltpu.VMEM((n * part, cols), bf16),
            pltpu.VMEM((Z, T, slots, width), bf16),
            pltpu.VMEM((Z, pad, 2 * HD), bf16),
            pltpu.VMEM((slots, LANES), f32),
            pltpu.VMEM((slots, LANES), f32),
            pltpu.VMEM((Z, q_cols // HD * slots, HD), bf16),
            pltpu.VMEM((n * (slots + pad), 2 * HD), bf16),
            pltpu.VMEM((Z * 2,) + w_out.shape, bf16),
            pltpu.VMEM((Z, slots, q_cols), bf16),
            pltpu.VMEM((2, 2, Z, slots, q_cols), bf16),
            pltpu.VMEM((Z, 2, slots, 2 * part), bf16),
            pltpu.VMEM((Z + 2, slots, 2 * part), bf16),
            pltpu.VMEM((Z // T, 2, slots, 2 * part), bf16),
            dma((Z,)), dma((n,)), dma((n,)), dma((n,)), dma((Z,)), dma((Z,)), dma((1,)), dma((1,)),
            dma((Z * TC,)), dma((Z * TC,)), dma((Z * TC,)), dma((Z * T * TC,)),
            dma((n,)), dma((n,)), dma((n,)),
            dma((Z * OC,)), dma((Z * OC,)), dma((Z * OC,)), dma((Z * 2 * OC,)),
            dma((Z,)), dma((Z,)), dma((2 * Z,)), dma((2 * Z,)), dma((2 * Z,)),
            dma((Z + 1,)), dma((Z,)), dma((1,)), dma((1,)), dma((2 * Z,)), dma((Z // T * 2,)),
            dma((2,)), dma((3 * (Z + 1),)),
        ],
        compiler_params=pltpu.CompilerParams(
            collective_id=0, has_side_effects=True, vmem_limit_bytes=54 * 1024 * 1024
        ),
    )(depth, gain, hidden, w_query, w_key, w_value, w_out)


def body(n_seq, n_tensor, hidden, depth, norm_gain, w_query, w_key, w_value, w_out):
    rows, width = hidden.shape
    slots = rows // 2
    d_model = width * n_tensor
    kv_heads = w_key.shape[1] // HD
    group = w_query.shape[1] // w_key.shape[1]
    J = kv_heads
    Z = n_seq // J
    part = w_query.shape[0]
    head_cols = (group + 2) * HD
    me = lax.axis_index("seq")
    t = lax.axis_index("tensor")
    j = lax.rem(me, J)
    z = me // J
    z_groups = [[a * J + b for a in range(Z)] for b in range(J)]

    def shift_j(value, k):
        pairs = [(a * J + b, a * J + (b + k) % J) for a in range(Z) for b in range(J)]
        return lax.ppermute(value, "seq", pairs)

    def shift_t(value, k):
        return lax.ppermute(value, "tensor", [(b, (b + k) % n_tensor) for b in range(n_tensor)])

    def gather_z(value, axis):
        return lax.all_gather(value, "seq", axis=axis, tiled=True, axis_index_groups=z_groups)

    def gather_j(value):
        return [value] + [shift_j(value, J - m) for m in range(1, J)]

    def exchange_j(block_for):
        return [block_for(j)] + [
            shift_j(block_for(lax.rem(j + J - m, J)), J - m) for m in range(1, J)
        ]

    living = depth > STEP
    index = jnp.arange(rows, dtype=jnp.int32)
    rank = jnp.sum(
        jnp.where(living[None, :] & (index[None, :] <= index[:, None]), 1, 0), axis=1
    ) - 1
    slot_ids = jnp.arange(slots, dtype=jnp.int32)
    select = (living[None, :] & (rank[None, :] == slot_ids[:, None])).astype(jnp.bfloat16)
    filled = jnp.sum(select.astype(jnp.float32), axis=1).astype(jnp.bfloat16)
    packed = jnp.dot(select, hidden, preferred_element_type=jnp.float32).astype(jnp.bfloat16)

    def columns_of(i):
        return jnp.concatenate(
            [
                lax.dynamic_slice_in_dim(w_query, i * group * HD, group * HD, axis=1),
                lax.dynamic_slice_in_dim(w_key, i * HD, HD, axis=1),
                lax.dynamic_slice_in_dim(w_value, i * HD, HD, axis=1),
            ],
            axis=1,
        )

    fast = (
        n_tensor == 2 and J == 4 and Z == kv_heads and Z == J and Z % n_tensor == 0 and slots % 16 == 0
        and slots <= 256 and part == w_out.shape[1] and part % 128 == 0 and width % 128 == 0 and w_out.shape[0] % 64 == 0
    )
    if fast:
        mixed, chosen = stepped(
            Z, J, n_tensor, slots, depth[None, :], norm_gain.reshape(n_tensor, 1, width),
            hidden, w_query, w_key, w_value, w_out,
        )
        return jnp.einsum(
            "sr,sf->rf", chosen, mixed, preferred_element_type=jnp.float32
        ).astype(jnp.bfloat16)

    w_rows = rolled(exchange_j(columns_of), 0, j)
    weights = gather_z(w_rows, 0)
    out_rows = group * HD
    twice = jnp.concatenate([w_out, w_out], axis=0) if J > 1 else w_out
    w_out_turned = lax.dynamic_slice_in_dim(twice, j * out_rows, J * out_rows, axis=0)
    out_weights = gather_z(w_out_turned, 1)

    features = rolled([packed] + [shift_t(packed, n_tensor - m) for m in range(1, n_tensor)], 1, t)
    widened = features.astype(jnp.float32)
    inverse = lax.rsqrt(jnp.mean(widened * widened, axis=1, keepdims=True) + EPSILON)
    normed = (widened * inverse * norm_gain[None, :]).astype(jnp.bfloat16)
    block_rows = J * slots
    tokens = jnp.concatenate(gather_j(normed), axis=0)
    flags = jnp.concatenate(gather_j(filled), axis=0)

    qkv = jnp.dot(tokens, weights, preferred_element_type=jnp.float32).astype(jnp.bfloat16)
    queries = qkv[:, : group * HD].reshape(block_rows, group, HD)
    kv = qkv[:, group * HD :]
    flag_rows = -(-block_rows // (2 * HD))
    flag_pad = -(-flag_rows // 16) * 16
    flag_block = jnp.pad(flags, (0, flag_pad * 2 * HD - block_rows)).reshape(flag_pad, 2 * HD)
    arrived = gather_z(jnp.concatenate([kv, flag_block], axis=0), 0).reshape(
        Z, block_rows + flag_pad, 2 * HD
    )
    keys = arrived[:, :block_rows, :HD].reshape(Z * block_rows, HD)
    values = arrived[:, :block_rows, HD:].reshape(Z * block_rows, HD)
    key_flags = arrived[:, block_rows:].reshape(Z, -1)[:, :block_rows].reshape(Z * block_rows)

    local = jnp.arange(block_rows, dtype=jnp.int32)
    turned = lax.rem(local // slots + j, J) * slots + lax.rem(local, slots)
    query_pos = z * block_rows + turned
    key_pos = (jnp.arange(Z, dtype=jnp.int32)[:, None] * block_rows + turned[None, :]).reshape(-1)
    visible = (key_flags[None, :] > 0) & (key_pos[None, :] <= query_pos[:, None])
    scores = jnp.einsum(
        "qgd,kd->gqk", queries, keys, preferred_element_type=jnp.float32
    ) * HD ** (-0.5)
    scores = jnp.where(visible[None], scores, MASKED_SCORE)
    expons = jnp.exp(scores - jnp.max(scores, axis=-1, keepdims=True))
    total = jnp.sum(expons, axis=-1)
    weighted = jnp.einsum(
        "gqk,kd->gqd", expons.astype(jnp.bfloat16), values, preferred_element_type=jnp.float32
    )
    attended = (weighted / total[..., None]).astype(jnp.bfloat16)
    attended = jnp.transpose(attended, (1, 0, 2)).reshape(block_rows, group * HD)
    attended = rolled([attended[m * slots : (m + 1) * slots] for m in range(J)], 0, j)
    heads = jnp.concatenate(gather_j(attended), axis=1)
    terms = jnp.dot(heads, out_weights, preferred_element_type=jnp.float32).astype(jnp.bfloat16)
    own_cols = w_out.shape[1]
    mine = exchange_j(lambda i: lax.dynamic_slice_in_dim(terms, i * slots, slots, axis=0))
    mine = [piece.reshape(slots, Z, 1, own_cols) for piece in mine]
    mine = rolled(mine, 2, j).reshape(slots, d_model)

    def features_of(i):
        return lax.dynamic_slice_in_dim(mine, i * width, width, axis=1)

    owned = features_of(t).astype(jnp.float32)
    for k in range(1, n_tensor):
        owned = owned + shift_t(features_of(lax.rem(t + k, n_tensor)), k).astype(jnp.float32)
    mixed = owned.astype(jnp.bfloat16)
    return jnp.einsum(
        "sr,sf->rf", select, mixed, preferred_element_type=jnp.float32
    ).astype(jnp.bfloat16)


def solution(mesh):
    n_seq, n_tensor = mesh.shape["seq"], mesh.shape["tensor"]

    def step(*args):
        return body(n_seq, n_tensor, *args)

    return jax.shard_map(
        step,
        mesh=mesh,
        in_specs=(
            P("seq", "tensor"),
            P("seq"),
            P(),
            P("seq", "tensor"),
            P("seq", "tensor"),
            P("seq", "tensor"),
            P("tensor", "seq"),
        ),
        out_specs=P("seq", "tensor"),
        check_vma=False,
    )
```

```python
import functools

import jax
import jax.numpy as jnp
from jax import lax
from jax.experimental import pallas as pl
from jax.experimental.pallas import tpu as pltpu
from jax.sharding import PartitionSpec as P

HD = 128
STEP = 2
EPSILON = 1e-05
MASKED_SCORE = -1e30


def rolled(pieces, axis, my):
    n = len(pieces)
    if n == 1:
        return pieces[0]
    width = pieces[0].shape[axis]
    twice = jnp.concatenate(pieces + pieces, axis=axis)
    start = lax.rem(n - my, n) * width
    return lax.dynamic_slice_in_dim(twice, start, n * width, axis=axis)


LANES = 128
ORDER = {
    (0, 0): (
        "W1", "T10", "T11", "X", "W2", "W3", "T12", "T20", "T21", "T22", "WA", "P0",
        "T30", "P1", "T31", "P2", "T32", "P3", "KV", "F0", "ATT", "A0", "A1", "A2",
        "A3", "HR", "HH", "L0", "HX", "S1", "S2", "HP", "B0", "B1", "B2", "B3",
        "S3", "END",
    ),
    (0, 1): (
        "W1", "T10", "T11", "X", "W2", "W3", "T12", "T20", "T21", "T22", "WA", "P0",
        "T30", "P1", "T31", "P2", "T32", "P3", "KV", "F0", "ATT", "B0", "B1", "B2",
        "B3", "HR", "HH", "L0", "HX", "S1", "S2", "HP", "A0", "A1", "A2", "A3",
        "S3", "END",
    ),
    (1, 0): (
        "W1", "X", "W2", "W3", "T10", "T11", "T12", "T20", "T21", "T22", "WA", "P0",
        "T30", "P1", "T31", "P2", "T32", "O0", "O1", "O2", "O3", "I0", "I1", "I2",
        "I3", "P3", "A0", "A1", "KV", "F0", "B0", "ATT", "A2", "A3", "B1", "B2",
        "B3", "HR", "HH", "L0", "C0", "C1", "HX", "S1", "C2", "C3", "S2", "HP",
        "S3", "END",
    ),
    (1, 1): (
        "W1", "X", "W2", "W3", "T10", "T11", "T12", "T20", "T21", "T22", "WA", "P0",
        "T30", "P1", "T31", "P2", "T32", "I0", "I1", "I2", "I3", "P3", "B0", "B1",
        "A0", "A1", "KV", "F0", "B2", "ATT", "A2", "A3", "B3", "O0", "O1", "O2",
        "O3", "HR", "HH", "L0", "C0", "C1", "HX", "S1", "C2", "C3", "S2", "HP",
        "S3", "END",
    ),
}
STEPS = ("P0", "P1", "P2", "P3", "KV", "ATT", "HR", "HH", "L0", "HX", "S1", "S2", "HP", "S3", "END")
MESH = pl.DeviceIdType.MESH


def step_kernel(
    Z, J, T, TC, OC, depth, gain, hidden, w_query, w_key, w_value, w_out, mixed_ref, select_ref,
    depth_here, gain_here, raw, w_blocks, weights, tokens, counts, sq_own, sq_other, queries, kv, outw, outx, att, heads, terms, away, other,
    ws_z, ws_s, ws_x, wr, cs, cr, qs, qr, ts_up, ts_dn, ts_y, tr, ks_s, ks_x, kr,
    os_up, os_dn, os_s, orr, hs, hs_h, hr, xs, xr, ms, mr, ns, nr, ys, yr, ls, lw,
    ox_x, ox_s, oxr,
):
    me, t = lax.axis_index("seq"), lax.axis_index("tensor")
    z, j = me // J, lax.rem(me, J)
    rows, width = hidden.shape
    slots = mixed_ref.shape[0]
    part, cols = w_blocks.shape[1:]
    q_cols = cols - 2 * HD
    heads_here = q_cols // HD
    pad = counts.shape[1]
    block = slots + pad
    t_rows = slots // TC
    o_rows = w_out.shape[0] // OC
    share = Z // T
    x, c = j // 2, lax.rem(j, 2)
    sib = j + 1 - 2 * c
    across = lax.rem(j + J // 2, J)
    diag = lax.rem(sib + J // 2, J)
    has_up, has_down = z < Z - 1, z > 0

    low = 1 - z // (Z // 2)
    depth_in = low * z + (1 - low) * (Z - 1 - z)
    at_end, inside = depth_in == 0, depth_in > 0
    helps = depth_in == 1

    def mirrored(a):
        return low * a + (1 - low) * (Z - 1 - a)

    near = [z] + [mirrored(i - (i <= depth_in).astype(jnp.int32)) for i in range(1, Z)]
    end, far = mirrored(0), mirrored(Z - 1)
    keeps = (t == z // share).astype(jnp.int32)

    ty = T - 1 - t

    def dev(zz, jj, tt=t):
        return (zz * J + jj, tt)

    sib_dev, across_dev, y_dev = dev(z, sib), dev(z, across), (me, ty)
    mid = mirrored(1)
    up, down = dev(z + 1, j), dev(z - 1, j)
    inward, outward = dev(z + 2 * low - 1, j), dev(z + 1 - 2 * low, j)

    def if_(cond, act):
        if cond is None:
            act()
        else:
            pl.when(cond)(lambda: act())

    barrier = pltpu.get_barrier_semaphore()

    def greet(device):
        pl.semaphore_signal(barrier, inc=1, device_id=device, device_id_type=MESH)

    for i in range(1, Z):
        greet(dev(near[i], j))
    for device in (sib_dev, across_dev, y_dev, dev(z, across, ty)):
        greet(device)
    for jj, tt in ((across, t), (across, ty), (j, ty)):
        if_(helps, lambda: greet(dev(end, jj, tt)))
        if_(at_end, lambda: greet(dev(mid, jj, tt)))

    local = []

    def bring(src, dst, sem):
        moved = pltpu.make_async_copy(src, dst, sem)
        moved.start()
        return moved

    fetched = bring(hidden, raw, ls.at[0])
    depths = bring(depth, depth_here, ls.at[2])
    gains = bring(gain.at[t], gain_here, ls.at[3])
    own_rows = pl.ds(pl.multiple_of(me * part, part), part)
    for i in range(Z + 1):
        zz = i if i < Z else z
        for n, (w, first, size) in enumerate(
            ((w_query, 0, q_cols), (w_key, q_cols, HD), (w_value, q_cols + HD, HD))
        ):
            to = slice(first, first + size)
            local.append(
                bring(
                    w.at[:, pl.ds(pl.multiple_of(zz * size, HD), size)],
                    w_blocks.at[i, :, to] if i < Z else weights.at[own_rows, to],
                    lw.at[3 * i + n],
                )
            )
    placed = bring(w_out, outw.at[z * 2 + c], ls.at[1])

    depths.wait()
    living = (depth_here[...] > STEP).astype(jnp.float32)
    before = lax.broadcasted_iota(jnp.int32, (rows, rows), 0)
    before = before <= lax.broadcasted_iota(jnp.int32, (rows, rows), 1)
    rank = jnp.dot(
        jnp.broadcast_to(living, (16, rows)).astype(jnp.bfloat16),
        before.astype(jnp.bfloat16),
        preferred_element_type=jnp.float32,
    )[0:1]
    slot = lax.broadcasted_iota(jnp.int32, (slots, rows), 0).astype(jnp.float32) + 1.0
    select = jnp.where((rank == slot) & (living > 0), 1.0, 0.0).astype(jnp.bfloat16)
    select_ref[...] = select
    total = jnp.sum(living, axis=1, keepdims=True)
    counts[z] = jnp.broadcast_to(total, counts.shape[1:]).astype(jnp.bfloat16)
    fetched.wait()
    wide = jnp.dot(select, raw[...], preferred_element_type=jnp.float32)
    own_squares = jnp.sum(wide * wide, axis=1, keepdims=True)
    sq_own[...] = jnp.broadcast_to(own_squares, sq_own.shape)
    gains.wait()
    for moved in local:
        moved.wait()
    pl.semaphore_wait(barrier, Z + 3 + 3 * (depth_in < 2).astype(jnp.int32))

    def copy(src, dst, send_sem, recv_sem, device):
        return pltpu.make_async_remote_copy(
            src_ref=src, dst_ref=dst, send_sem=send_sem, recv_sem=recv_sem,
            device_id=device, device_id_type=MESH,
        )

    started = []

    def start(cond, make):
        if_(cond, lambda: make().start())
        started.append((cond, make))

    def arrive(cond, make):
        if_(cond, lambda: make().wait_recv())

    def w_at(b):
        return weights.at[pl.ds(pl.multiple_of(b * part, part), part), :]

    def w_copy(b, sems, device, own=False):
        return copy(w_blocks.at[z] if own else w_at(b), w_at(b), sems.at[b], wr.at[b], device)

    def w_z(zz):
        return copy(w_blocks.at[zz], w_at(me), ws_z.at[zz], wr.at[me], dev(zz, j))

    def c_copy(zz, to):
        return copy(counts.at[zz], counts.at[zz], cs.at[to], cr.at[zz], dev(to, j))

    def t_copy(zz, tt, k, sems, device):
        at = tokens.at[zz, tt, pl.ds(k * t_rows, t_rows)]
        return copy(at, at, sems.at[zz * TC + k], tr.at[(zz * T + tt) * TC + k], device)

    def k_copy(b, sems, device):
        at = kv.at[pl.ds(pl.multiple_of(b * block, 16), block), :]
        return copy(at, at, sems.at[b], kr.at[b], device)

    def o_copy(zb, cc, k, sems, device):
        b = zb * 2 + cc
        at = outw.at[b, pl.ds(k * o_rows, o_rows)]
        return copy(at, at, sems.at[zb * OC + k], orr.at[b * OC + k], device)

    def q_copy(cc, k, sems, device, first=False):
        rows_k = pl.ds(k * o_rows, o_rows)
        dst = outx.at[cc, rows_k]
        src = outw.at[z * 2 + c, rows_k] if first else dst
        return copy(src, dst, sems.at[k], oxr.at[cc * OC + k], device)

    def h_copy(kind, zq, source, to):
        sems = (hs, hs_h)[kind]
        return copy(att.at[zq], heads.at[kind, 0, source], sems.at[zq], hr.at[kind * Z + source], dev(to, j))

    def x_copy(kind, source):
        i = kind * Z + source
        return copy(heads.at[kind, 0, source], heads.at[kind, 1, source], xs.at[i], xr.at[i], across_dev)

    def m_copy(zb, slot, zz, leaving):
        zl = lax.rem(zb, share)
        if leaving:
            return copy(
                away.at[slot], other.at[zl, x], ms.at[slot], yr.at[zl * 2 + x], dev(zz, across, ty)
            )
        return copy(away.at[slot], terms.at[zb, x], ms.at[slot], mr.at[zb], dev(zz, across))

    def n_copy(leaving):
        zl = lax.rem(far, share)
        if leaving:
            return copy(away.at[Z + 1], other.at[zl, x], ns.at[0], yr.at[zl * 2 + x], dev(end, j, ty))
        return copy(away.at[Z + 1], terms.at[far, x], ns.at[0], nr.at[0], dev(end, j))

    def y_copy(zb, xx):
        zl = lax.rem(zb, share)
        return copy(
            terms.at[zb, xx], other.at[zl, xx], ys.at[zb * 2 + xx], yr.at[zl * 2 + xx], y_dev
        )

    for i in range(1, Z):
        start(None, lambda zz=near[i]: c_copy(z, zz))
    for i in range(1, Z):
        start(None, lambda zz=near[i]: w_z(zz))
    start(None, lambda: w_copy(me, ws_x, across_dev, True))
    start(None, lambda: w_copy(me, ws_s, sib_dev, True))

    q_make = lambda: copy(sq_own, sq_other, qs.at[0], qr.at[0], y_dev)
    start(None, q_make)
    arrive(None, q_make)
    squares = own_squares + sq_other[:, 0:1]
    inverse = lax.rsqrt(squares / (T * width) + EPSILON)
    tokens[z, t] = (wide * inverse * gain_here[...]).astype(jnp.bfloat16)

    for k in range(TC):
        start(has_up, lambda k=k: t_copy(z, t, k, ts_up, up))
        start(has_down, lambda k=k: t_copy(z, t, k, ts_dn, down))
        start(None, lambda k=k: t_copy(z, t, k, ts_y, y_dev))

    def own_o(k, in_):
        device = inward if in_ else outward
        ups = low if in_ else 1 - low
        return [
            (ups == 1, lambda: o_copy(z, c, k, os_up, device)),
            (ups == 0, lambda: o_copy(z, c, k, os_dn, device)),
        ]

    def cast_w(b):
        return [
            (None, lambda: w_copy(b, ws_x, across_dev)), (None, lambda: w_copy(b, ws_s, sib_dev))
        ]

    def pass_t(zz, k):
        return [
            ((zz < z) & has_up, lambda: t_copy(zz, t, k, ts_up, up)),
            ((zz > z) & has_down, lambda: t_copy(zz, t, k, ts_dn, down)),
            (None, lambda: t_copy(zz, t, k, ts_y, y_dev)),
        ]

    def pass_o(zb, k):
        return [
            (
                (zb < z) & has_up & ~((z + 1 == Z - 1) & (zb == 0)),
                lambda: o_copy(zb, c, k, os_up, up),
            ),
            (
                (zb > z) & has_down & ~((z - 1 == 0) & (zb == Z - 1)),
                lambda: o_copy(zb, c, k, os_dn, down),
            ),
            (None, lambda: o_copy(zb, c, k, os_s, sib_dev)),
        ]

    def moves(op):
        kind, last = op[0], op[-1]
        if op == "WA":
            return [
                (
                    lambda b=zz * J + across: w_copy(b, ws_s, sib_dev),
                    [(None, lambda b=zz * J + across: w_copy(b, ws_s, sib_dev))],
                )
                for zz in range(Z)
            ]
        if kind == "X":
            return [
                (None, [(None, lambda k=k: q_copy(c, k, ox_x, across_dev, True))]) for k in range(OC)
            ]
        if kind == "F":
            return [
                (
                    lambda k=k: q_copy(c, k, ox_s, sib_dev),
                    [(None, lambda k=k: q_copy(c, k, ox_s, sib_dev))],
                )
                for k in range(OC)
            ]
        n = int(last)
        if kind == "W":
            b = near[n] * J + j
            return [(lambda: w_copy(b, ws_s, sib_dev), cast_w(b))]
        if kind == "T":
            zz = near[int(op[1])]
            return [(lambda: t_copy(zz, t, n, ts_y, y_dev), pass_t(zz, n))]
        if kind in "IO":
            return [(None, own_o(n, kind == "I"))]
        zb = near["ABC".index(kind) + 1]
        return [(lambda: o_copy(zb, c, n, os_s, sib_dev), pass_o(zb, n))]

    def act(op):
        for awaited, copies in moves(op):
            if awaited is not None:
                awaited().wait_recv()
            for cond, make in copies:
                if_(cond, lambda: make().start())

    def between(step):
        for (place, stays), order in ORDER.items():
            first = 0
            for i, op in enumerate(order):
                if op == step:
                    break
                if op in STEPS:
                    first = i + 1
            todo = order[first:i]
            if todo:
                mine = (inside if place else at_end) & (keeps == stays)

                def run():
                    for op in todo:
                        act(op)

                pl.when(mine)(run)

    everyone = (
        ["W1", "W2", "W3", "X", "F0", "WA"]
        + ["T%d%d" % (i, k) for i in range(1, Z) for k in range(TC)]
        + ["%s%d" % (f, k) for f in "AB" for k in range(OC)]
    )
    within = ["%s%d" % (f, k) for f in "IOC" for k in range(OC)]
    for ops, base_cond in ((everyone, None), (within, inside)):
        for op in ops:
            for _, copies in moves(op):
                for cond, make in copies:
                    if base_cond is not None:
                        cond = base_cond if cond is None else base_cond & cond
                    started.append((cond, make))

    placed.wait()
    for k in range(OC):
        for cond, make in own_o(k, True):
            start(at_end & cond, make)
    for k in range(OC):
        start(None, lambda k=k: o_copy(z, c, k, os_s, sib_dev))

    def product(i):
        zz = near[i]
        for k in range(TC):
            arrive(None, lambda k=k: t_copy(zz, T - 1 - t, k, ts_y, y_dev))
        result = None
        for tt in range(T):
            term = jnp.dot(
                tokens[zz, tt], weights[tt * width : (tt + 1) * width, :],
                preferred_element_type=jnp.float32,
            )
            result = term if result is None else result + term
        for g in range(heads_here):
            queries[zz, g * slots : (g + 1) * slots, :] = result[
                :, g * HD : (g + 1) * HD
            ].astype(jnp.bfloat16)
        b = zz * J + j
        top = pl.multiple_of(b * block, 16)
        kv[pl.ds(top, slots), :] = result[:, q_cols:].astype(jnp.bfloat16)
        kv[pl.ds(pl.multiple_of(top + slots, 16), pad), :] = counts[zz]
        start(None, lambda: k_copy(b, ks_x, across_dev))
        start(None, lambda: k_copy(b, ks_s, sib_dev))

    between("P0")
    for i in range(1, Z):
        arrive(None, lambda: c_copy(near[i], z))
    for zz in range(Z):
        for jj in (sib, diag):
            arrive(None, lambda: w_copy(zz * J + jj, ws_s, sib_dev))
    product(0)
    for i in range(1, Z):
        between("P%d" % i)
        product(i)
    between("KV")
    for i in range(Z):
        b = near[i] * J + across
        arrive(None, lambda: k_copy(b, ks_s, sib_dev))
        start(None, lambda b=b: k_copy(b, ks_s, sib_dev))
    for zz in range(Z):
        for jj in (sib, diag):
            arrive(None, lambda: k_copy(zz * J + jj, ks_s, sib_dev))
    between("ATT")

    keys = Z * J * block
    key_pos = lax.broadcasted_iota(jnp.int32, (1, keys), 1)
    seen = jnp.zeros((1, keys), jnp.float32)
    for b in range(Z * J):
        limit = kv[b * block + slots : b * block + slots + 1, 0:1].astype(jnp.float32) + b * block
        inside_b = (key_pos >= b * block) & (key_pos < (b + 1) * block)
        seen = jnp.where(inside_b & (key_pos.astype(jnp.float32) < limit), 1.0, seen)
    key_pos = jnp.where(seen > 0, key_pos, keys)
    row = lax.broadcasted_iota(jnp.int32, (slots, 1), 0)
    row = jnp.concatenate([row] * heads_here, axis=0) + j * block

    for zq in range(Z):
        n = (zq + 1) * J * block
        scores = lax.dot_general(
            queries[zq], kv[:n, :HD], (((1,), (1,)), ((), ())), preferred_element_type=jnp.float32
        ) * HD ** (-0.5)
        visible = key_pos[:, :n] <= row + zq * J * block
        scores = jnp.where(visible, scores, MASKED_SCORE)
        expons = jnp.exp(scores - jnp.max(scores, axis=1, keepdims=True))
        row_total = jnp.sum(expons, axis=1, keepdims=True)
        weighted = jnp.dot(
            expons.astype(jnp.bfloat16), kv[:n, HD:], preferred_element_type=jnp.float32
        )
        attended = (weighted / row_total).astype(jnp.bfloat16)
        for g in range(heads_here):
            att[zq, :, g * HD : (g + 1) * HD] = attended[g * slots : (g + 1) * slots]

        @pl.when(z == zq)
        def _():
            heads[0, 0, z] = att[zq]

        start(z != zq, lambda zq=zq: h_copy(0, zq, z, zq))
        if zq in (0, Z - 1):
            helper = 1 if zq == 0 else Z - 2

            @pl.when(z == helper)
            def _():
                heads[1, 0, z] = att[zq]

            start(z != helper, lambda zq=zq, helper=helper: h_copy(1, zq, z, helper))

    start(None, lambda: x_copy(0, z))
    start(helps, lambda: x_copy(1, z))
    between("HR")
    for kind, cond in ((0, None), (1, helps)):
        if kind:
            between("HH")
        for i in range(1, Z):
            arrive(cond, lambda: h_copy(kind, 0, near[i], z))
            start(cond, lambda kind=kind, i=i: x_copy(kind, near[i]))

    between("L0")
    for k in range(OC):
        arrive(None, lambda: o_copy(z, 1 - c, k, os_s, sib_dev))
        arrive(None, lambda: q_copy(1 - c, k, ox_s, sib_dev))
    every = jnp.concatenate([heads[0, 0, zz] for zz in range(Z)], axis=1)
    for cc in range(2):
        at = slice(cc * part, (cc + 1) * part)
        for to, block_of in ((x, outw.at[z * 2 + cc]), (1 - x, outx.at[cc])):
            terms[z, to, :, at] = jnp.dot(
                every, block_of[...], preferred_element_type=jnp.float32
            ).astype(jnp.bfloat16)
    for xx in (1 - x, x):
        start(z // share != t, lambda xx=xx: y_copy(z, xx))

    between("HX")
    for zz in range(Z):
        arrive(None, lambda: x_copy(0, zz))

    def emit(kind, zb, own_slot, away_slot):
        every = jnp.concatenate(
            [
                jnp.concatenate([heads[kind, xx, zz] for zz in range(Z)], axis=1)
                for xx in range(2)
            ],
            axis=0,
        )
        if kind == 0:
            for k in range(OC):
                o_copy(zb, 1 - c, k, os_s, sib_dev).wait_recv()
        for cc in range(2):
            result = jnp.dot(
                every, outw[zb * 2 + cc], preferred_element_type=jnp.float32
            ).astype(jnp.bfloat16)
            at = slice(cc * part, (cc + 1) * part)
            if own_slot is None:
                terms[zb, x, :, at] = result[:slots]
            else:
                away[own_slot, :, at] = result[:slots]
            away[away_slot, :, at] = result[slots:]

    def hand_out(zb, slot, zz, cond=None):
        stays = zb // share == t
        leaves = zb // share != t
        if cond is not None:
            stays, leaves = cond & stays, cond & leaves
        start(stays, lambda: m_copy(zb, slot, zz, False))
        start(leaves, lambda: m_copy(zb, slot, zz, True))
        return stays, leaves

    def emit_own(zb, cond=None):
        if_(cond, lambda: emit(0, zb, None, zb))
        _, leaves = hand_out(zb, zb, z, cond)
        start(leaves, lambda: y_copy(zb, x))

    early = keeps * near[2] + (1 - keeps) * near[1]
    late = keeps * near[1] + (1 - keeps) * near[2]
    between("S1")
    emit_own(early)
    between("S2")
    emit_own(far, inside)
    between("HP")
    for zz in range(Z):
        arrive(helps, lambda: x_copy(1, zz))
    if_(helps, lambda: emit(1, far, Z + 1, Z))
    stays, leaves = hand_out(far, Z, end, helps)
    start(stays, lambda: n_copy(False))
    start(leaves, lambda: n_copy(True))
    between("S3")
    emit_own(late)

    for zl in range(share):
        zb = t * share + zl
        arrive(zb != z, lambda: m_copy(zb, zb, z, False))
        arrive(at_end & (zb == far), lambda: n_copy(False))
        for xx in range(2):
            y_copy(zl, xx).wait_recv()
            top = (zl * 2 + xx) * 2 * part
            mixed_ref[:, top : top + 2 * part] = (
                terms[zb, xx].astype(jnp.float32) + other[zl, xx].astype(jnp.float32)
            ).astype(jnp.bfloat16)

    for cond, make in started:
        if_(cond, lambda: make().wait_send())


def stepped(Z, J, T, slots, depth, gain, hidden, w_query, w_key, w_value, w_out):
    rows, width = hidden.shape
    part = w_query.shape[0]
    q_cols = w_query.shape[1] // Z
    cols = q_cols + 2 * HD
    pad = 16
    n = Z * J
    TC, OC = 3, 4
    vmem = pl.BlockSpec(memory_space=pltpu.VMEM)
    dma = pltpu.SemaphoreType.DMA
    bf16, f32 = jnp.bfloat16, jnp.float32
    return pl.pallas_call(
        functools.partial(step_kernel, Z, J, T, TC, OC),
        out_shape=(
            jax.ShapeDtypeStruct((slots, width), bf16), jax.ShapeDtypeStruct((slots, rows), bf16)
        ),
        in_specs=[pl.BlockSpec(memory_space=pltpu.HBM)] * 7,
        out_specs=(vmem, vmem),
        scratch_shapes=[
            pltpu.VMEM((1, rows), jnp.int32),
            pltpu.VMEM((1, width), f32),
            pltpu.VMEM((rows, width), bf16),
            pltpu.VMEM((Z, part, cols), bf16),
            pltpu.VMEM((n * part, cols), bf16),
            pltpu.VMEM((Z, T, slots, width), bf16),
            pltpu.VMEM((Z, pad, 2 * HD), bf16),
            pltpu.VMEM((slots, LANES), f32),
            pltpu.VMEM((slots, LANES), f32),
            pltpu.VMEM((Z, q_cols // HD * slots, HD), bf16),
            pltpu.VMEM((n * (slots + pad), 2 * HD), bf16),
            pltpu.VMEM((Z * 2,) + w_out.shape, bf16),
            pltpu.VMEM((2,) + w_out.shape, bf16),
            pltpu.VMEM((Z, slots, q_cols), bf16),
            pltpu.VMEM((2, 2, Z, slots, q_cols), bf16),
            pltpu.VMEM((Z, 2, slots, 2 * part), bf16),
            pltpu.VMEM((Z + 2, slots, 2 * part), bf16),
            pltpu.VMEM((Z // T, 2, slots, 2 * part), bf16),
            dma((Z,)), dma((n,)), dma((n,)), dma((n,)), dma((Z,)), dma((Z,)), dma((1,)), dma((1,)),
            dma((Z * TC,)), dma((Z * TC,)), dma((Z * TC,)), dma((Z * T * TC,)),
            dma((n,)), dma((n,)), dma((n,)),
            dma((Z * OC,)), dma((Z * OC,)), dma((Z * OC,)), dma((Z * 2 * OC,)),
            dma((Z,)), dma((Z,)), dma((2 * Z,)), dma((2 * Z,)), dma((2 * Z,)),
            dma((Z + 1,)), dma((Z,)), dma((1,)), dma((1,)), dma((2 * Z,)), dma((Z // T * 2,)),
            dma((4,)), dma((3 * (Z + 1),)),
            dma((OC,)), dma((OC,)), dma((2 * OC,)),
        ],
        compiler_params=pltpu.CompilerParams(
            collective_id=0, has_side_effects=True, vmem_limit_bytes=32 * 1024 * 1024
        ),
    )(depth, gain, hidden, w_query, w_key, w_value, w_out)


def body(n_seq, n_tensor, hidden, depth, norm_gain, w_query, w_key, w_value, w_out):
    rows, width = hidden.shape
    slots = rows // 2
    d_model = width * n_tensor
    kv_heads = w_key.shape[1] // HD
    group = w_query.shape[1] // w_key.shape[1]
    J = kv_heads
    Z = n_seq // J
    part = w_query.shape[0]
    head_cols = (group + 2) * HD
    me = lax.axis_index("seq")
    t = lax.axis_index("tensor")
    j = lax.rem(me, J)
    z = me // J
    z_groups = [[a * J + b for a in range(Z)] for b in range(J)]

    def shift_j(value, k):
        pairs = [(a * J + b, a * J + (b + k) % J) for a in range(Z) for b in range(J)]
        return lax.ppermute(value, "seq", pairs)

    def shift_t(value, k):
        return lax.ppermute(value, "tensor", [(b, (b + k) % n_tensor) for b in range(n_tensor)])

    def gather_z(value, axis):
        return lax.all_gather(value, "seq", axis=axis, tiled=True, axis_index_groups=z_groups)

    def gather_j(value):
        return [value] + [shift_j(value, J - m) for m in range(1, J)]

    def exchange_j(block_for):
        return [block_for(j)] + [
            shift_j(block_for(lax.rem(j + J - m, J)), J - m) for m in range(1, J)
        ]

    living = depth > STEP
    index = jnp.arange(rows, dtype=jnp.int32)
    rank = jnp.sum(
        jnp.where(living[None, :] & (index[None, :] <= index[:, None]), 1, 0), axis=1
    ) - 1
    slot_ids = jnp.arange(slots, dtype=jnp.int32)
    select = (living[None, :] & (rank[None, :] == slot_ids[:, None])).astype(jnp.bfloat16)
    filled = jnp.sum(select.astype(jnp.float32), axis=1).astype(jnp.bfloat16)
    packed = jnp.dot(select, hidden, preferred_element_type=jnp.float32).astype(jnp.bfloat16)

    def columns_of(i):
        return jnp.concatenate(
            [
                lax.dynamic_slice_in_dim(w_query, i * group * HD, group * HD, axis=1),
                lax.dynamic_slice_in_dim(w_key, i * HD, HD, axis=1),
                lax.dynamic_slice_in_dim(w_value, i * HD, HD, axis=1),
            ],
            axis=1,
        )

    fast = (
        n_tensor == 2 and J == 4 and Z == kv_heads and Z == J and Z % n_tensor == 0 and slots % 48 == 0
        and slots <= 256 and part == w_out.shape[1] and part % 128 == 0 and width % 128 == 0 and w_out.shape[0] % 64 == 0
    )
    if fast:
        operands = (
            depth[None, :], norm_gain.reshape(n_tensor, 1, width),
            hidden, w_query, w_key, w_value, w_out,
        )
        mixed, chosen = stepped(
            Z, J, n_tensor, slots,
            *(pltpu.with_memory_space_constraint(a, pltpu.HBM) for a in operands),
        )
        return jnp.einsum(
            "sr,sf->rf", chosen, mixed, preferred_element_type=jnp.float32
        ).astype(jnp.bfloat16)

    w_rows = rolled(exchange_j(columns_of), 0, j)
    weights = gather_z(w_rows, 0)
    out_rows = group * HD
    twice = jnp.concatenate([w_out, w_out], axis=0) if J > 1 else w_out
    w_out_turned = lax.dynamic_slice_in_dim(twice, j * out_rows, J * out_rows, axis=0)
    out_weights = gather_z(w_out_turned, 1)

    features = rolled([packed] + [shift_t(packed, n_tensor - m) for m in range(1, n_tensor)], 1, t)
    widened = features.astype(jnp.float32)
    inverse = lax.rsqrt(jnp.mean(widened * widened, axis=1, keepdims=True) + EPSILON)
    normed = (widened * inverse * norm_gain[None, :]).astype(jnp.bfloat16)
    block_rows = J * slots
    tokens = jnp.concatenate(gather_j(normed), axis=0)
    flags = jnp.concatenate(gather_j(filled), axis=0)

    qkv = jnp.dot(tokens, weights, preferred_element_type=jnp.float32).astype(jnp.bfloat16)
    queries = qkv[:, : group * HD].reshape(block_rows, group, HD)
    kv = qkv[:, group * HD :]
    flag_rows = -(-block_rows // (2 * HD))
    flag_pad = -(-flag_rows // 16) * 16
    flag_block = jnp.pad(flags, (0, flag_pad * 2 * HD - block_rows)).reshape(flag_pad, 2 * HD)
    arrived = gather_z(jnp.concatenate([kv, flag_block], axis=0), 0).reshape(
        Z, block_rows + flag_pad, 2 * HD
    )
    keys = arrived[:, :block_rows, :HD].reshape(Z * block_rows, HD)
    values = arrived[:, :block_rows, HD:].reshape(Z * block_rows, HD)
    key_flags = arrived[:, block_rows:].reshape(Z, -1)[:, :block_rows].reshape(Z * block_rows)

    local = jnp.arange(block_rows, dtype=jnp.int32)
    turned = lax.rem(local // slots + j, J) * slots + lax.rem(local, slots)
    query_pos = z * block_rows + turned
    key_pos = (jnp.arange(Z, dtype=jnp.int32)[:, None] * block_rows + turned[None, :]).reshape(-1)
    visible = (key_flags[None, :] > 0) & (key_pos[None, :] <= query_pos[:, None])
    scores = jnp.einsum(
        "qgd,kd->gqk", queries, keys, preferred_element_type=jnp.float32
    ) * HD ** (-0.5)
    scores = jnp.where(visible[None], scores, MASKED_SCORE)
    expons = jnp.exp(scores - jnp.max(scores, axis=-1, keepdims=True))
    total = jnp.sum(expons, axis=-1)
    weighted = jnp.einsum(
        "gqk,kd->gqd", expons.astype(jnp.bfloat16), values, preferred_element_type=jnp.float32
    )
    attended = (weighted / total[..., None]).astype(jnp.bfloat16)
    attended = jnp.transpose(attended, (1, 0, 2)).reshape(block_rows, group * HD)
    attended = rolled([attended[m * slots : (m + 1) * slots] for m in range(J)], 0, j)
    heads = jnp.concatenate(gather_j(attended), axis=1)
    terms = jnp.dot(heads, out_weights, preferred_element_type=jnp.float32).astype(jnp.bfloat16)
    own_cols = w_out.shape[1]
    mine = exchange_j(lambda i: lax.dynamic_slice_in_dim(terms, i * slots, slots, axis=0))
    mine = [piece.reshape(slots, Z, 1, own_cols) for piece in mine]
    mine = rolled(mine, 2, j).reshape(slots, d_model)

    def features_of(i):
        return lax.dynamic_slice_in_dim(mine, i * width, width, axis=1)

    owned = features_of(t).astype(jnp.float32)
    for k in range(1, n_tensor):
        owned = owned + shift_t(features_of(lax.rem(t + k, n_tensor)), k).astype(jnp.float32)
    mixed = owned.astype(jnp.bfloat16)
    return jnp.einsum(
        "sr,sf->rf", select, mixed, preferred_element_type=jnp.float32
    ).astype(jnp.bfloat16)


def solution(mesh):
    n_seq, n_tensor = mesh.shape["seq"], mesh.shape["tensor"]

    def step(*args):
        return body(n_seq, n_tensor, *args)

    return jax.shard_map(
        step,
        mesh=mesh,
        in_specs=(
            P("seq", "tensor"),
            P("seq"),
            P(),
            P("seq", "tensor"),
            P("seq", "tensor"),
            P("seq", "tensor"),
            P("tensor", "seq"),
        ),
        out_specs=P("seq", "tensor"),
        check_vma=False,
    )
```

```python
import functools

import jax
import jax.numpy as jnp
from jax import lax
from jax.experimental import pallas as pl
from jax.experimental.pallas import tpu as pltpu
from jax.sharding import PartitionSpec as P

HD = 128
STEP = 2
EPSILON = 1e-05
MASKED_SCORE = -1e30


def rolled(pieces, axis, my):
    n = len(pieces)
    if n == 1:
        return pieces[0]
    width = pieces[0].shape[axis]
    twice = jnp.concatenate(pieces + pieces, axis=axis)
    start = lax.rem(n - my, n) * width
    return lax.dynamic_slice_in_dim(twice, start, n * width, axis=axis)


LANES = 128
ORDER = {
    (0, 0): (
        "T10", "W1", "T11", "T12", "W3", "T13", "T20", "T21", "T14", "T15", "W2", "T22",
        "T23", "X", "T24", "WA", "T25", "T30", "P0", "T31", "P1", "T32", "T33", "P2",
        "T34", "T35", "P3", "F0", "KV", "A0", "A1", "ATT", "A2", "A3", "HR", "HH",
        "L0", "HX", "S1", "S2", "B0", "HP", "B1", "B2", "B3", "S3", "END",
    ),
    (0, 1): (
        "W1", "T10", "X", "W3", "T11", "T12", "T13", "T20", "W2", "T14", "T21", "T22",
        "T23", "T15", "T30", "T31", "T24", "T25", "WA", "T32", "P0", "P1", "T33", "F0",
        "T34", "P2", "T35", "P3", "KV", "ATT", "B0", "B1", "B2", "HR", "HH", "L0",
        "B3", "A0", "HX", "S1", "S2", "HP", "A1", "A2", "A3", "S3", "END",
    ),
    (1, 0): (
        "W3", "W2", "T10", "T11", "W1", "T12", "T13", "T20", "T14", "T21", "X", "T22",
        "T23", "T24", "T25", "T15", "WA", "I0", "T30", "T31", "P0", "A0", "P1", "T32",
        "T33", "T34", "P2", "T35", "O0", "O1", "O2", "I1", "I2", "P3", "O3", "I3",
        "KV", "ATT", "A1", "B0", "C0", "A2", "B1", "B2", "B3", "HR", "HH", "A3",
        "F0", "L0", "C1", "HX", "S1", "C2", "C3", "S2", "HP", "S3", "END",
    ),
    (1, 1): (
        "W1", "T10", "W3", "T11", "W2", "T12", "T13", "T14", "T20", "X", "T21", "T22",
        "T23", "T24", "T30", "T15", "WA", "T31", "I0", "P0", "T25", "P1", "A0", "T32",
        "T33", "P2", "T34", "A1", "T35", "I1", "P3", "B0", "I2", "B1", "I3", "KV",
        "B2", "ATT", "A2", "B3", "F0", "O0", "O1", "HR", "HH", "O2", "L0", "C0",
        "C1", "A3", "O3", "HX", "S1", "C2", "C3", "S2", "HP", "S3", "END",
    ),
}
STEPS = ("P0", "P1", "P2", "P3", "KV", "ATT", "HR", "HH", "L0", "HX", "S1", "S2", "HP", "S3", "END")
MESH = pl.DeviceIdType.MESH


def step_kernel(
    Z, J, T, TC, OC, depth, gain, hidden, w_query, w_key, w_value, w_out, mixed_ref, select_ref,
    depth_here, gain_here, raw, w_blocks, weights, tokens, counts, sq_own, sq_other, queries, kv, outw, outx, att, heads, terms, away, other,
    ws_z, ws_s, ws_x, wr, cs, cr, qs, qr, ts_up, ts_dn, ts_y, tr, ks_s, ks_x, kr,
    os_up, os_dn, os_s, orr, hs, hs_h, hr, xs, xr, ms, mr, ns, nr, ys, yr, ls, lw,
    ox_x, ox_s, oxr,
):
    me, t = lax.axis_index("seq"), lax.axis_index("tensor")
    z, j = me // J, lax.rem(me, J)
    rows, width = hidden.shape
    slots = mixed_ref.shape[0]
    part, cols = w_blocks.shape[1:]
    q_cols = cols - 2 * HD
    heads_here = q_cols // HD
    pad = counts.shape[1]
    block = slots + pad
    t_rows = slots // TC
    o_rows = w_out.shape[0] // OC
    share = Z // T
    x, c = j // 2, lax.rem(j, 2)
    sib = j + 1 - 2 * c
    across = lax.rem(j + J // 2, J)
    diag = lax.rem(sib + J // 2, J)
    has_up, has_down = z < Z - 1, z > 0

    low = 1 - z // (Z // 2)
    depth_in = low * z + (1 - low) * (Z - 1 - z)
    at_end, inside = depth_in == 0, depth_in > 0
    helps = depth_in == 1

    def mirrored(a):
        return low * a + (1 - low) * (Z - 1 - a)

    near = [z] + [mirrored(i - (i <= depth_in).astype(jnp.int32)) for i in range(1, Z)]
    end, far = mirrored(0), mirrored(Z - 1)
    keeps = (t == z // share).astype(jnp.int32)

    ty = T - 1 - t

    def dev(zz, jj, tt=t):
        return (zz * J + jj, tt)

    sib_dev, across_dev, y_dev = dev(z, sib), dev(z, across), (me, ty)
    mid = mirrored(1)
    up, down = dev(z + 1, j), dev(z - 1, j)
    inward, outward = dev(z + 2 * low - 1, j), dev(z + 1 - 2 * low, j)

    def if_(cond, act):
        if cond is None:
            act()
        else:
            pl.when(cond)(lambda: act())

    barrier = pltpu.get_barrier_semaphore()

    def greet(device):
        pl.semaphore_signal(barrier, inc=1, device_id=device, device_id_type=MESH)

    for i in range(1, Z):
        greet(dev(near[i], j))
    for device in (sib_dev, across_dev, y_dev, dev(z, across, ty)):
        greet(device)
    for jj, tt in ((across, t), (across, ty), (j, ty)):
        if_(helps, lambda: greet(dev(end, jj, tt)))
        if_(at_end, lambda: greet(dev(mid, jj, tt)))

    local = []

    def bring(src, dst, sem):
        moved = pltpu.make_async_copy(src, dst, sem)
        moved.start()
        return moved

    fetched = bring(hidden, raw, ls.at[0])
    depths = bring(depth, depth_here, ls.at[2])
    gains = bring(gain.at[t], gain_here, ls.at[3])
    own_rows = pl.ds(pl.multiple_of(me * part, part), part)
    for i in range(Z + 1):
        zz = i if i < Z else z
        for n, (w, first, size) in enumerate(
            ((w_query, 0, q_cols), (w_key, q_cols, HD), (w_value, q_cols + HD, HD))
        ):
            to = slice(first, first + size)
            local.append(
                bring(
                    w.at[:, pl.ds(pl.multiple_of(zz * size, HD), size)],
                    w_blocks.at[i, :, to] if i < Z else weights.at[own_rows, to],
                    lw.at[3 * i + n],
                )
            )
    placed = bring(w_out, outw.at[z * 2 + c], ls.at[1])

    depths.wait()
    living = (depth_here[...] > STEP).astype(jnp.float32)
    before = lax.broadcasted_iota(jnp.int32, (rows, rows), 0)
    before = before <= lax.broadcasted_iota(jnp.int32, (rows, rows), 1)
    rank = jnp.dot(
        jnp.broadcast_to(living, (16, rows)).astype(jnp.bfloat16),
        before.astype(jnp.bfloat16),
        preferred_element_type=jnp.float32,
    )[0:1]
    slot = lax.broadcasted_iota(jnp.int32, (slots, rows), 0).astype(jnp.float32) + 1.0
    select = jnp.where((rank == slot) & (living > 0), 1.0, 0.0).astype(jnp.bfloat16)
    select_ref[...] = select
    total = jnp.sum(living, axis=1, keepdims=True)
    counts[z] = jnp.broadcast_to(total, counts.shape[1:]).astype(jnp.bfloat16)
    fetched.wait()
    wide = jnp.dot(select, raw[...], preferred_element_type=jnp.float32)
    own_squares = jnp.sum(wide * wide, axis=1, keepdims=True)
    sq_own[...] = jnp.broadcast_to(own_squares, sq_own.shape)
    gains.wait()
    for moved in local:
        moved.wait()
    pl.semaphore_wait(barrier, Z + 3 + 3 * (depth_in < 2).astype(jnp.int32))

    def copy(src, dst, send_sem, recv_sem, device):
        return pltpu.make_async_remote_copy(
            src_ref=src, dst_ref=dst, send_sem=send_sem, recv_sem=recv_sem,
            device_id=device, device_id_type=MESH,
        )

    started = []

    def start(cond, make):
        if_(cond, lambda: make().start())
        started.append((cond, make))

    def arrive(cond, make):
        if_(cond, lambda: make().wait_recv())

    def w_at(b):
        return weights.at[pl.ds(pl.multiple_of(b * part, part), part), :]

    def w_copy(b, sems, device, own=False):
        return copy(w_blocks.at[z] if own else w_at(b), w_at(b), sems.at[b], wr.at[b], device)

    def w_z(zz):
        return copy(w_blocks.at[zz], w_at(me), ws_z.at[zz], wr.at[me], dev(zz, j))

    def c_copy(zz, to):
        return copy(counts.at[zz], counts.at[zz], cs.at[to], cr.at[zz], dev(to, j))

    def t_copy(zz, tt, k, sems, device):
        at = tokens.at[zz, tt, pl.ds(k * t_rows, t_rows)]
        return copy(at, at, sems.at[zz * TC + k], tr.at[(zz * T + tt) * TC + k], device)

    def k_copy(b, sems, device):
        at = kv.at[pl.ds(pl.multiple_of(b * block, 16), block), :]
        return copy(at, at, sems.at[b], kr.at[b], device)

    def o_copy(zb, cc, k, sems, device):
        b = zb * 2 + cc
        at = outw.at[b, pl.ds(k * o_rows, o_rows)]
        return copy(at, at, sems.at[zb * OC + k], orr.at[b * OC + k], device)

    def q_copy(cc, k, sems, device, first=False):
        rows_k = pl.ds(k * o_rows, o_rows)
        dst = outx.at[cc, rows_k]
        src = outw.at[z * 2 + c, rows_k] if first else dst
        return copy(src, dst, sems.at[k], oxr.at[cc * OC + k], device)

    def h_copy(kind, zq, source, to):
        sems = (hs, hs_h)[kind]
        return copy(att.at[zq], heads.at[kind, 0, source], sems.at[zq], hr.at[kind * Z + source], dev(to, j))

    def x_copy(kind, source):
        i = kind * Z + source
        return copy(heads.at[kind, 0, source], heads.at[kind, 1, source], xs.at[i], xr.at[i], across_dev)

    def m_copy(zb, slot, zz, leaving):
        zl = lax.rem(zb, share)
        if leaving:
            return copy(
                away.at[slot], other.at[zl, x], ms.at[slot], yr.at[zl * 2 + x], dev(zz, across, ty)
            )
        return copy(away.at[slot], terms.at[zb, x], ms.at[slot], mr.at[zb], dev(zz, across))

    def n_copy(leaving):
        zl = lax.rem(far, share)
        if leaving:
            return copy(away.at[Z + 1], other.at[zl, x], ns.at[0], yr.at[zl * 2 + x], dev(end, j, ty))
        return copy(away.at[Z + 1], terms.at[far, x], ns.at[0], nr.at[0], dev(end, j))

    def y_copy(zb, xx):
        zl = lax.rem(zb, share)
        return copy(
            terms.at[zb, xx], other.at[zl, xx], ys.at[zb * 2 + xx], yr.at[zl * 2 + xx], y_dev
        )

    for i in range(1, Z):
        start(None, lambda zz=near[i]: c_copy(z, zz))
    for i in range(1, Z):
        start(None, lambda zz=near[i]: w_z(zz))
    start(None, lambda: w_copy(me, ws_x, across_dev, True))
    start(None, lambda: w_copy(me, ws_s, sib_dev, True))

    q_make = lambda: copy(sq_own, sq_other, qs.at[0], qr.at[0], y_dev)
    start(None, q_make)
    arrive(None, q_make)
    squares = own_squares + sq_other[:, 0:1]
    inverse = lax.rsqrt(squares / (T * width) + EPSILON)
    tokens[z, t] = (wide * inverse * gain_here[...]).astype(jnp.bfloat16)

    for k in range(TC):
        start(has_up, lambda k=k: t_copy(z, t, k, ts_up, up))
        start(has_down, lambda k=k: t_copy(z, t, k, ts_dn, down))
        start(None, lambda k=k: t_copy(z, t, k, ts_y, y_dev))

    def own_o(k, in_):
        device = inward if in_ else outward
        ups = low if in_ else 1 - low
        return [
            (ups == 1, lambda: o_copy(z, c, k, os_up, device)),
            (ups == 0, lambda: o_copy(z, c, k, os_dn, device)),
        ]

    def cast_w(b):
        return [
            (None, lambda: w_copy(b, ws_x, across_dev)), (None, lambda: w_copy(b, ws_s, sib_dev))
        ]

    def pass_t(zz, k):
        return [
            ((zz < z) & has_up, lambda: t_copy(zz, t, k, ts_up, up)),
            ((zz > z) & has_down, lambda: t_copy(zz, t, k, ts_dn, down)),
            (None, lambda: t_copy(zz, t, k, ts_y, y_dev)),
        ]

    def pass_o(zb, k):
        return [
            (
                (zb < z) & has_up & ~((z + 1 == Z - 1) & (zb == 0)),
                lambda: o_copy(zb, c, k, os_up, up),
            ),
            (
                (zb > z) & has_down & ~((z - 1 == 0) & (zb == Z - 1)),
                lambda: o_copy(zb, c, k, os_dn, down),
            ),
            (None, lambda: o_copy(zb, c, k, os_s, sib_dev)),
        ]

    def moves(op):
        kind, last = op[0], op[-1]
        if op == "WA":
            return [
                (
                    lambda b=zz * J + across: w_copy(b, ws_s, sib_dev),
                    [(None, lambda b=zz * J + across: w_copy(b, ws_s, sib_dev))],
                )
                for zz in range(Z)
            ]
        if kind == "X":
            return [
                (None, [(None, lambda k=k: q_copy(c, k, ox_x, across_dev, True))]) for k in range(OC)
            ]
        if kind == "F":
            return [
                (
                    lambda k=k: q_copy(c, k, ox_s, sib_dev),
                    [(None, lambda k=k: q_copy(c, k, ox_s, sib_dev))],
                )
                for k in range(OC)
            ]
        n = int(last)
        if kind == "W":
            b = near[n] * J + j
            return [(lambda: w_copy(b, ws_s, sib_dev), cast_w(b))]
        if kind == "T":
            zz = near[int(op[1])]
            return [(lambda: t_copy(zz, t, n, ts_y, y_dev), pass_t(zz, n))]
        if kind in "IO":
            return [(None, own_o(n, kind == "I"))]
        zb = near["ABC".index(kind) + 1]
        return [(lambda: o_copy(zb, c, n, os_s, sib_dev), pass_o(zb, n))]

    def act(op):
        for awaited, copies in moves(op):
            if awaited is not None:
                awaited().wait_recv()
            for cond, make in copies:
                if_(cond, lambda: make().start())

    def between(step):
        for (place, stays), order in ORDER.items():
            first = 0
            for i, op in enumerate(order):
                if op == step:
                    break
                if op in STEPS:
                    first = i + 1
            todo = order[first:i]
            if todo:
                mine = (inside if place else at_end) & (keeps == stays)

                def run():
                    for op in todo:
                        act(op)

                pl.when(mine)(run)

    everyone = (
        ["W1", "W2", "W3", "X", "F0", "WA"]
        + ["T%d%d" % (i, k) for i in range(1, Z) for k in range(TC)]
        + ["%s%d" % (f, k) for f in "AB" for k in range(OC)]
    )
    within = ["%s%d" % (f, k) for f in "IOC" for k in range(OC)]
    for ops, base_cond in ((everyone, None), (within, inside)):
        for op in ops:
            for _, copies in moves(op):
                for cond, make in copies:
                    if base_cond is not None:
                        cond = base_cond if cond is None else base_cond & cond
                    started.append((cond, make))

    placed.wait()
    for k in range(OC):
        for cond, make in own_o(k, True):
            start(at_end & cond, make)
    for k in range(OC):
        start(None, lambda k=k: o_copy(z, c, k, os_s, sib_dev))

    def product(i):
        zz = near[i]
        for k in range(TC):
            arrive(None, lambda k=k: t_copy(zz, T - 1 - t, k, ts_y, y_dev))
        result = None
        for tt in range(T):
            term = jnp.dot(
                tokens[zz, tt], weights[tt * width : (tt + 1) * width, :],
                preferred_element_type=jnp.float32,
            )
            result = term if result is None else result + term
        for g in range(heads_here):
            queries[zz, g * slots : (g + 1) * slots, :] = result[
                :, g * HD : (g + 1) * HD
            ].astype(jnp.bfloat16)
        b = zz * J + j
        top = pl.multiple_of(b * block, 16)
        kv[pl.ds(top, slots), :] = result[:, q_cols:].astype(jnp.bfloat16)
        kv[pl.ds(pl.multiple_of(top + slots, 16), pad), :] = counts[zz]
        start(None, lambda: k_copy(b, ks_x, across_dev))
        start(None, lambda: k_copy(b, ks_s, sib_dev))

    between("P0")
    for i in range(1, Z):
        arrive(None, lambda: c_copy(near[i], z))
    for zz in range(Z):
        for jj in (sib, diag):
            arrive(None, lambda: w_copy(zz * J + jj, ws_s, sib_dev))
    product(0)
    for i in range(1, Z):
        between("P%d" % i)
        product(i)
    between("KV")
    for i in range(Z):
        b = near[i] * J + across
        arrive(None, lambda: k_copy(b, ks_s, sib_dev))
        start(None, lambda b=b: k_copy(b, ks_s, sib_dev))
    for zz in range(Z):
        for jj in (sib, diag):
            arrive(None, lambda: k_copy(zz * J + jj, ks_s, sib_dev))
    between("ATT")

    keys = Z * J * block
    key_pos = lax.broadcasted_iota(jnp.int32, (1, keys), 1)
    seen = jnp.zeros((1, keys), jnp.float32)
    for b in range(Z * J):
        limit = kv[b * block + slots : b * block + slots + 1, 0:1].astype(jnp.float32) + b * block
        inside_b = (key_pos >= b * block) & (key_pos < (b + 1) * block)
        seen = jnp.where(inside_b & (key_pos.astype(jnp.float32) < limit), 1.0, seen)
    key_pos = jnp.where(seen > 0, key_pos, keys)
    row = lax.broadcasted_iota(jnp.int32, (slots, 1), 0)
    row = jnp.concatenate([row] * heads_here, axis=0) + j * block

    for zq in range(Z):
        n = (zq + 1) * J * block
        scores = lax.dot_general(
            queries[zq], kv[:n, :HD], (((1,), (1,)), ((), ())), preferred_element_type=jnp.float32
        ) * HD ** (-0.5)
        visible = key_pos[:, :n] <= row + zq * J * block
        scores = jnp.where(visible, scores, MASKED_SCORE)
        expons = jnp.exp(scores - jnp.max(scores, axis=1, keepdims=True))
        row_total = jnp.sum(expons, axis=1, keepdims=True)
        weighted = jnp.dot(
            expons.astype(jnp.bfloat16), kv[:n, HD:], preferred_element_type=jnp.float32
        )
        attended = (weighted / row_total).astype(jnp.bfloat16)
        for g in range(heads_here):
            att[zq, :, g * HD : (g + 1) * HD] = attended[g * slots : (g + 1) * slots]

        @pl.when(z == zq)
        def _():
            heads[0, 0, z] = att[zq]

        start(z != zq, lambda zq=zq: h_copy(0, zq, z, zq))
        if zq in (0, Z - 1):
            helper = 1 if zq == 0 else Z - 2

            @pl.when(z == helper)
            def _():
                heads[1, 0, z] = att[zq]

            start(z != helper, lambda zq=zq, helper=helper: h_copy(1, zq, z, helper))

    start(None, lambda: x_copy(0, z))
    start(helps, lambda: x_copy(1, z))
    between("HR")
    for kind, cond in ((0, None), (1, helps)):
        if kind:
            between("HH")
        for i in range(1, Z):
            arrive(cond, lambda: h_copy(kind, 0, near[i], z))
            start(cond, lambda kind=kind, i=i: x_copy(kind, near[i]))

    begun = len(started)

    between("L0")
    for k in range(OC):
        arrive(None, lambda: o_copy(z, 1 - c, k, os_s, sib_dev))
        arrive(None, lambda: q_copy(1 - c, k, ox_s, sib_dev))
    every = jnp.concatenate([heads[0, 0, zz] for zz in range(Z)], axis=1)
    for cc in range(2):
        at = slice(cc * part, (cc + 1) * part)
        for to, block_of in ((x, outw.at[z * 2 + cc]), (1 - x, outx.at[cc])):
            terms[z, to, :, at] = jnp.dot(
                every, block_of[...], preferred_element_type=jnp.float32
            ).astype(jnp.bfloat16)
    for xx in (1 - x, x):
        start(z // share != t, lambda xx=xx: y_copy(z, xx))

    between("HX")
    for zz in range(Z):
        arrive(None, lambda: x_copy(0, zz))

    def emit(kind, zb, own_slot, away_slot):
        every = jnp.concatenate(
            [
                jnp.concatenate([heads[kind, xx, zz] for zz in range(Z)], axis=1)
                for xx in range(2)
            ],
            axis=0,
        )
        if kind == 0:
            for k in range(OC):
                o_copy(zb, 1 - c, k, os_s, sib_dev).wait_recv()
        for cc in range(2):
            result = jnp.dot(
                every, outw[zb * 2 + cc], preferred_element_type=jnp.float32
            ).astype(jnp.bfloat16)
            at = slice(cc * part, (cc + 1) * part)
            if own_slot is None:
                terms[zb, x, :, at] = result[:slots]
            else:
                away[own_slot, :, at] = result[:slots]
            away[away_slot, :, at] = result[slots:]

    def hand_out(zb, slot, zz, cond=None):
        stays = zb // share == t
        leaves = zb // share != t
        if cond is not None:
            stays, leaves = cond & stays, cond & leaves
        start(stays, lambda: m_copy(zb, slot, zz, False))
        start(leaves, lambda: m_copy(zb, slot, zz, True))
        return stays, leaves

    def emit_own(zb, cond=None):
        if_(cond, lambda: emit(0, zb, None, zb))
        _, leaves = hand_out(zb, zb, z, cond)
        start(leaves, lambda: y_copy(zb, x))

    early = keeps * near[2] + (1 - keeps) * near[1]
    late = keeps * near[1] + (1 - keeps) * near[2]
    between("S1")
    emit_own(early)
    between("S2")
    emit_own(far, inside)
    between("HP")
    for zz in range(Z):
        arrive(helps, lambda: x_copy(1, zz))
    if_(helps, lambda: emit(1, far, Z + 1, Z))
    stays, leaves = hand_out(far, Z, end, helps)
    start(stays, lambda: n_copy(False))
    start(leaves, lambda: n_copy(True))
    between("S3")
    emit_own(late)
    for cond, make in started[:begun]:
        if_(cond, lambda: make().wait_send())

    for zl in range(share):
        zb = t * share + zl
        arrive(zb != z, lambda: m_copy(zb, zb, z, False))
        arrive(at_end & (zb == far), lambda: n_copy(False))
        for xx in range(2):
            y_copy(zl, xx).wait_recv()
            top = (zl * 2 + xx) * 2 * part
            mixed_ref[:, top : top + 2 * part] = (
                terms[zb, xx].astype(jnp.float32) + other[zl, xx].astype(jnp.float32)
            ).astype(jnp.bfloat16)

    for cond, make in started[begun:]:
        if_(cond, lambda: make().wait_send())


def stepped(Z, J, T, slots, depth, gain, hidden, w_query, w_key, w_value, w_out):
    rows, width = hidden.shape
    part = w_query.shape[0]
    q_cols = w_query.shape[1] // Z
    cols = q_cols + 2 * HD
    pad = 16
    n = Z * J
    TC, OC = 6, 4
    vmem = pl.BlockSpec(memory_space=pltpu.VMEM)
    dma = pltpu.SemaphoreType.DMA
    bf16, f32 = jnp.bfloat16, jnp.float32
    return pl.pallas_call(
        functools.partial(step_kernel, Z, J, T, TC, OC),
        out_shape=(
            jax.ShapeDtypeStruct((slots, width), bf16), jax.ShapeDtypeStruct((slots, rows), bf16)
        ),
        in_specs=[pl.BlockSpec(memory_space=pltpu.HBM)] * 7,
        out_specs=(vmem, vmem),
        scratch_shapes=[
            pltpu.VMEM((1, rows), jnp.int32),
            pltpu.VMEM((1, width), f32),
            pltpu.VMEM((rows, width), bf16),
            pltpu.VMEM((Z, part, cols), bf16),
            pltpu.VMEM((n * part, cols), bf16),
            pltpu.VMEM((Z, T, slots, width), bf16),
            pltpu.VMEM((Z, pad, 2 * HD), bf16),
            pltpu.VMEM((slots, LANES), f32),
            pltpu.VMEM((slots, LANES), f32),
            pltpu.VMEM((Z, q_cols // HD * slots, HD), bf16),
            pltpu.VMEM((n * (slots + pad), 2 * HD), bf16),
            pltpu.VMEM((Z * 2,) + w_out.shape, bf16),
            pltpu.VMEM((2,) + w_out.shape, bf16),
            pltpu.VMEM((Z, slots, q_cols), bf16),
            pltpu.VMEM((2, 2, Z, slots, q_cols), bf16),
            pltpu.VMEM((Z, 2, slots, 2 * part), bf16),
            pltpu.VMEM((Z + 2, slots, 2 * part), bf16),
            pltpu.VMEM((Z // T, 2, slots, 2 * part), bf16),
            dma((Z,)), dma((n,)), dma((n,)), dma((n,)), dma((Z,)), dma((Z,)), dma((1,)), dma((1,)),
            dma((Z * TC,)), dma((Z * TC,)), dma((Z * TC,)), dma((Z * T * TC,)),
            dma((n,)), dma((n,)), dma((n,)),
            dma((Z * OC,)), dma((Z * OC,)), dma((Z * OC,)), dma((Z * 2 * OC,)),
            dma((Z,)), dma((Z,)), dma((2 * Z,)), dma((2 * Z,)), dma((2 * Z,)),
            dma((Z + 1,)), dma((Z,)), dma((1,)), dma((1,)), dma((2 * Z,)), dma((Z // T * 2,)),
            dma((4,)), dma((3 * (Z + 1),)),
            dma((OC,)), dma((OC,)), dma((2 * OC,)),
        ],
        compiler_params=pltpu.CompilerParams(
            collective_id=0, has_side_effects=True, vmem_limit_bytes=32 * 1024 * 1024
        ),
    )(depth, gain, hidden, w_query, w_key, w_value, w_out)


def body(n_seq, n_tensor, hidden, depth, norm_gain, w_query, w_key, w_value, w_out):
    rows, width = hidden.shape
    slots = rows // 2
    d_model = width * n_tensor
    kv_heads = w_key.shape[1] // HD
    group = w_query.shape[1] // w_key.shape[1]
    J = kv_heads
    Z = n_seq // J
    part = w_query.shape[0]
    head_cols = (group + 2) * HD
    me = lax.axis_index("seq")
    t = lax.axis_index("tensor")
    j = lax.rem(me, J)
    z = me // J
    z_groups = [[a * J + b for a in range(Z)] for b in range(J)]

    def shift_j(value, k):
        pairs = [(a * J + b, a * J + (b + k) % J) for a in range(Z) for b in range(J)]
        return lax.ppermute(value, "seq", pairs)

    def shift_t(value, k):
        return lax.ppermute(value, "tensor", [(b, (b + k) % n_tensor) for b in range(n_tensor)])

    def gather_z(value, axis):
        return lax.all_gather(value, "seq", axis=axis, tiled=True, axis_index_groups=z_groups)

    def gather_j(value):
        return [value] + [shift_j(value, J - m) for m in range(1, J)]

    def exchange_j(block_for):
        return [block_for(j)] + [
            shift_j(block_for(lax.rem(j + J - m, J)), J - m) for m in range(1, J)
        ]

    living = depth > STEP
    index = jnp.arange(rows, dtype=jnp.int32)
    rank = jnp.sum(
        jnp.where(living[None, :] & (index[None, :] <= index[:, None]), 1, 0), axis=1
    ) - 1
    slot_ids = jnp.arange(slots, dtype=jnp.int32)
    select = (living[None, :] & (rank[None, :] == slot_ids[:, None])).astype(jnp.bfloat16)
    filled = jnp.sum(select.astype(jnp.float32), axis=1).astype(jnp.bfloat16)
    packed = jnp.dot(select, hidden, preferred_element_type=jnp.float32).astype(jnp.bfloat16)

    def columns_of(i):
        return jnp.concatenate(
            [
                lax.dynamic_slice_in_dim(w_query, i * group * HD, group * HD, axis=1),
                lax.dynamic_slice_in_dim(w_key, i * HD, HD, axis=1),
                lax.dynamic_slice_in_dim(w_value, i * HD, HD, axis=1),
            ],
            axis=1,
        )

    fast = (
        n_tensor == 2 and J == 4 and Z == kv_heads and Z == J and Z % n_tensor == 0 and slots % 96 == 0
        and slots <= 256 and part == w_out.shape[1] and part % 128 == 0 and width % 128 == 0 and w_out.shape[0] % 64 == 0
    )
    if fast:
        operands = (
            depth[None, :], norm_gain.reshape(n_tensor, 1, width),
            hidden, w_query, w_key, w_value, w_out,
        )
        mixed, chosen = stepped(
            Z, J, n_tensor, slots,
            *(pltpu.with_memory_space_constraint(a, pltpu.HBM) for a in operands),
        )
        return jnp.einsum(
            "sr,sf->rf", chosen, mixed, preferred_element_type=jnp.float32
        ).astype(jnp.bfloat16)

    w_rows = rolled(exchange_j(columns_of), 0, j)
    weights = gather_z(w_rows, 0)
    out_rows = group * HD
    twice = jnp.concatenate([w_out, w_out], axis=0) if J > 1 else w_out
    w_out_turned = lax.dynamic_slice_in_dim(twice, j * out_rows, J * out_rows, axis=0)
    out_weights = gather_z(w_out_turned, 1)

    features = rolled([packed] + [shift_t(packed, n_tensor - m) for m in range(1, n_tensor)], 1, t)
    widened = features.astype(jnp.float32)
    inverse = lax.rsqrt(jnp.mean(widened * widened, axis=1, keepdims=True) + EPSILON)
    normed = (widened * inverse * norm_gain[None, :]).astype(jnp.bfloat16)
    block_rows = J * slots
    tokens = jnp.concatenate(gather_j(normed), axis=0)
    flags = jnp.concatenate(gather_j(filled), axis=0)

    qkv = jnp.dot(tokens, weights, preferred_element_type=jnp.float32).astype(jnp.bfloat16)
    queries = qkv[:, : group * HD].reshape(block_rows, group, HD)
    kv = qkv[:, group * HD :]
    flag_rows = -(-block_rows // (2 * HD))
    flag_pad = -(-flag_rows // 16) * 16
    flag_block = jnp.pad(flags, (0, flag_pad * 2 * HD - block_rows)).reshape(flag_pad, 2 * HD)
    arrived = gather_z(jnp.concatenate([kv, flag_block], axis=0), 0).reshape(
        Z, block_rows + flag_pad, 2 * HD
    )
    keys = arrived[:, :block_rows, :HD].reshape(Z * block_rows, HD)
    values = arrived[:, :block_rows, HD:].reshape(Z * block_rows, HD)
    key_flags = arrived[:, block_rows:].reshape(Z, -1)[:, :block_rows].reshape(Z * block_rows)

    local = jnp.arange(block_rows, dtype=jnp.int32)
    turned = lax.rem(local // slots + j, J) * slots + lax.rem(local, slots)
    query_pos = z * block_rows + turned
    key_pos = (jnp.arange(Z, dtype=jnp.int32)[:, None] * block_rows + turned[None, :]).reshape(-1)
    visible = (key_flags[None, :] > 0) & (key_pos[None, :] <= query_pos[:, None])
    scores = jnp.einsum(
        "qgd,kd->gqk", queries, keys, preferred_element_type=jnp.float32
    ) * HD ** (-0.5)
    scores = jnp.where(visible[None], scores, MASKED_SCORE)
    expons = jnp.exp(scores - jnp.max(scores, axis=-1, keepdims=True))
    total = jnp.sum(expons, axis=-1)
    weighted = jnp.einsum(
        "gqk,kd->gqd", expons.astype(jnp.bfloat16), values, preferred_element_type=jnp.float32
    )
    attended = (weighted / total[..., None]).astype(jnp.bfloat16)
    attended = jnp.transpose(attended, (1, 0, 2)).reshape(block_rows, group * HD)
    attended = rolled([attended[m * slots : (m + 1) * slots] for m in range(J)], 0, j)
    heads = jnp.concatenate(gather_j(attended), axis=1)
    terms = jnp.dot(heads, out_weights, preferred_element_type=jnp.float32).astype(jnp.bfloat16)
    own_cols = w_out.shape[1]
    mine = exchange_j(lambda i: lax.dynamic_slice_in_dim(terms, i * slots, slots, axis=0))
    mine = [piece.reshape(slots, Z, 1, own_cols) for piece in mine]
    mine = rolled(mine, 2, j).reshape(slots, d_model)

    def features_of(i):
        return lax.dynamic_slice_in_dim(mine, i * width, width, axis=1)

    owned = features_of(t).astype(jnp.float32)
    for k in range(1, n_tensor):
        owned = owned + shift_t(features_of(lax.rem(t + k, n_tensor)), k).astype(jnp.float32)
    mixed = owned.astype(jnp.bfloat16)
    return jnp.einsum(
        "sr,sf->rf", select, mixed, preferred_element_type=jnp.float32
    ).astype(jnp.bfloat16)


def solution(mesh):
    n_seq, n_tensor = mesh.shape["seq"], mesh.shape["tensor"]

    def step(*args):
        return body(n_seq, n_tensor, *args)

    return jax.shard_map(
        step,
        mesh=mesh,
        in_specs=(
            P("seq", "tensor"),
            P("seq"),
            P(),
            P("seq", "tensor"),
            P("seq", "tensor"),
            P("seq", "tensor"),
            P("tensor", "seq"),
        ),
        out_specs=P("seq", "tensor"),
        check_vma=False,
    )
```

```python
import functools

import jax
import jax.numpy as jnp
from jax import lax
from jax.experimental import pallas as pl
from jax.experimental.pallas import tpu as pltpu
from jax.sharding import PartitionSpec as P

HD = 128
STEP = 2
EPSILON = 1e-05
MASKED_SCORE = -1e30


def rolled(pieces, axis, my):
    n = len(pieces)
    if n == 1:
        return pieces[0]
    width = pieces[0].shape[axis]
    twice = jnp.concatenate(pieces + pieces, axis=axis)
    start = lax.rem(n - my, n) * width
    return lax.dynamic_slice_in_dim(twice, start, n * width, axis=axis)


LANES = 128
ORDER = {
    (0, 0): (
        "E0", "E1", "E2", "E3", "T10", "W1", "W3", "T11", "T12", "T13", "T20", "T14",
        "T21", "W2", "T22", "T15", "T23", "T24", "X", "T25", "T30", "WA", "T31", "P0",
        "P1", "T32", "T33", "P2", "T34", "T35", "P3", "A0", "A1", "KV", "ATT", "HR",
        "A2", "B0", "F0", "HH", "B1", "L0", "A3", "HX", "S1", "S2", "B2", "HP",
        "B3", "S3", "END",
    ),
    (0, 1): (
        "E0", "E1", "E2", "E3", "W1", "T10", "T11", "T12", "X", "T13", "F0", "W2",
        "T20", "T21", "T22", "T14", "W3", "T23", "T30", "T15", "T24", "T25", "T31", "WA",
        "P0", "T32", "T33", "T34", "P1", "T35", "P2", "P3", "KV", "ATT", "B0", "A0",
        "B1", "B2", "HR", "B3", "HH", "L0", "HX", "A1", "S1", "S2", "HP", "A2",
        "A3", "S3", "END",
    ),
    (1, 0): (
        "W1", "W2", "W3", "T10", "T11", "T12", "T20", "T21", "T22", "T13", "T23", "T24",
        "T14", "WA", "T25", "A0", "X", "T15", "T30", "T31", "P0", "T32", "O0", "T33",
        "T34", "I0", "P1", "P2", "T35", "O1", "O2", "I1", "I2", "B0", "A1", "F0",
        "O3", "I3", "P3", "KV", "ATT", "A2", "C0", "B1", "HR", "A3", "HH", "B2",
        "C1", "L0", "HX", "B3", "S1", "C2", "C3", "S2", "HP", "S3", "END",
    ),
    (1, 1): (
        "X", "W3", "T10", "W1", "T11", "W2", "T12", "T13", "T20", "T14", "T21", "T15",
        "T22", "A0", "T23", "T24", "I0", "T30", "WA", "A1", "F0", "T25", "T31", "I1",
        "I2", "P0", "I3", "P1", "T32", "T33", "T34", "C0", "P2", "T35", "B0", "P3",
        "B1", "B2", "O0", "KV", "ATT", "B3", "O1", "A2", "A3", "O2", "C1", "HR",
        "HH", "L0", "HX", "O3", "S1", "C2", "C3", "S2", "HP", "S3", "END",
    ),
}
STEPS = ("P0", "P1", "P2", "P3", "KV", "ATT", "HR", "HH", "L0", "HX", "S1", "S2", "HP", "S3", "END")
MESH = pl.DeviceIdType.MESH


def step_kernel(
    Z, J, T, TC, OC, depth, gain, hidden, w_query, w_key, w_value, w_out, mixed_ref, select_ref,
    depth_here, gain_here, raw, w_blocks, weights, tokens, counts, sq_own, sq_other, queries, kv, outw, outx, att, heads, terms, away, other,
    ws_z, ws_s, ws_x, wr, cs, cr, qs, qr, ts_up, ts_dn, ts_y, tr, ks_s, ks_x, kr,
    os_up, os_dn, os_s, orr, hs, hs_h, hr, xs, xr, ms, mr, ns, nr, ys, yr, ls, lw,
    ox_x, ox_s, oxr,
):
    me, t = lax.axis_index("seq"), lax.axis_index("tensor")
    z, j = me // J, lax.rem(me, J)
    rows, width = hidden.shape
    slots = mixed_ref.shape[0]
    part, cols = w_blocks.shape[1:]
    q_cols = cols - 2 * HD
    heads_here = q_cols // HD
    pad = counts.shape[1]
    block = slots + pad
    t_rows = slots // TC
    o_rows = w_out.shape[0] // OC
    share = Z // T
    x, c = j // 2, lax.rem(j, 2)
    sib = j + 1 - 2 * c
    across = lax.rem(j + J // 2, J)
    diag = lax.rem(sib + J // 2, J)
    has_up, has_down = z < Z - 1, z > 0

    low = 1 - z // (Z // 2)
    depth_in = low * z + (1 - low) * (Z - 1 - z)
    at_end, inside = depth_in == 0, depth_in > 0
    helps = depth_in == 1

    def mirrored(a):
        return low * a + (1 - low) * (Z - 1 - a)

    near = [z] + [mirrored(i - (i <= depth_in).astype(jnp.int32)) for i in range(1, Z)]
    end, far = mirrored(0), mirrored(Z - 1)
    keeps = (t == z // share).astype(jnp.int32)

    ty = T - 1 - t

    def dev(zz, jj, tt=t):
        return (zz * J + jj, tt)

    sib_dev, across_dev, y_dev = dev(z, sib), dev(z, across), (me, ty)
    mid = mirrored(1)
    up, down = dev(z + 1, j), dev(z - 1, j)
    inward, outward = dev(z + 2 * low - 1, j), dev(z + 1 - 2 * low, j)

    def if_(cond, act):
        if cond is None:
            act()
        else:
            pl.when(cond)(lambda: act())

    barrier = pltpu.get_barrier_semaphore()

    def greet(device):
        pl.semaphore_signal(barrier, inc=1, device_id=device, device_id_type=MESH)

    for i in range(1, Z):
        greet(dev(near[i], j))
    for device in (sib_dev, across_dev, y_dev, dev(z, across, ty)):
        greet(device)
    for jj, tt in ((across, t), (across, ty), (j, ty)):
        if_(helps, lambda: greet(dev(end, jj, tt)))
        if_(at_end, lambda: greet(dev(mid, jj, tt)))

    local = []

    def bring(src, dst, sem):
        moved = pltpu.make_async_copy(src, dst, sem)
        moved.start()
        return moved

    fetched = bring(hidden, raw, ls.at[0])
    depths = bring(depth, depth_here, ls.at[2])
    gains = bring(gain.at[t], gain_here, ls.at[3])
    own_rows = pl.ds(pl.multiple_of(me * part, part), part)
    for i in range(Z + 1):
        zz = i if i < Z else z
        for n, (w, first, size) in enumerate(
            ((w_query, 0, q_cols), (w_key, q_cols, HD), (w_value, q_cols + HD, HD))
        ):
            to = slice(first, first + size)
            local.append(
                bring(
                    w.at[:, pl.ds(pl.multiple_of(zz * size, HD), size)],
                    w_blocks.at[i, :, to] if i < Z else weights.at[own_rows, to],
                    lw.at[3 * i + n],
                )
            )
    placed = bring(w_out, outw.at[z * 2 + c], ls.at[1])

    depths.wait()
    living = (depth_here[...] > STEP).astype(jnp.float32)
    before = lax.broadcasted_iota(jnp.int32, (rows, rows), 0)
    before = before <= lax.broadcasted_iota(jnp.int32, (rows, rows), 1)
    rank = jnp.dot(
        jnp.broadcast_to(living, (16, rows)).astype(jnp.bfloat16),
        before.astype(jnp.bfloat16),
        preferred_element_type=jnp.float32,
    )[0:1]
    slot = lax.broadcasted_iota(jnp.int32, (slots, rows), 0).astype(jnp.float32) + 1.0
    select = jnp.where((rank == slot) & (living > 0), 1.0, 0.0).astype(jnp.bfloat16)
    select_ref[...] = select
    total = jnp.sum(living, axis=1, keepdims=True)
    counts[z] = jnp.broadcast_to(total, counts.shape[1:]).astype(jnp.bfloat16)
    fetched.wait()
    wide = jnp.dot(select, raw[...], preferred_element_type=jnp.float32)
    own_squares = jnp.sum(wide * wide, axis=1, keepdims=True)
    sq_own[...] = jnp.broadcast_to(own_squares, sq_own.shape)
    gains.wait()
    for moved in local:
        moved.wait()
    pl.semaphore_wait(barrier, Z + 3 + 3 * (depth_in < 2).astype(jnp.int32))

    def copy(src, dst, send_sem, recv_sem, device):
        return pltpu.make_async_remote_copy(
            src_ref=src, dst_ref=dst, send_sem=send_sem, recv_sem=recv_sem,
            device_id=device, device_id_type=MESH,
        )

    started = []

    def start(cond, make):
        if_(cond, lambda: make().start())
        started.append((cond, make))

    def arrive(cond, make):
        if_(cond, lambda: make().wait_recv())

    def w_at(b):
        return weights.at[pl.ds(pl.multiple_of(b * part, part), part), :]

    def w_copy(b, sems, device, own=False):
        return copy(w_blocks.at[z] if own else w_at(b), w_at(b), sems.at[b], wr.at[b], device)

    def w_z(zz):
        return copy(w_blocks.at[zz], w_at(me), ws_z.at[zz], wr.at[me], dev(zz, j))

    def c_copy(zz, to):
        return copy(counts.at[zz], counts.at[zz], cs.at[to], cr.at[zz], dev(to, j))

    def t_copy(zz, tt, k, sems, device):
        at = tokens.at[zz, tt, pl.ds(k * t_rows, t_rows)]
        return copy(at, at, sems.at[zz * TC + k], tr.at[(zz * T + tt) * TC + k], device)

    def k_copy(b, sems, device):
        at = kv.at[pl.ds(pl.multiple_of(b * block, 16), block), :]
        return copy(at, at, sems.at[b], kr.at[b], device)

    def o_copy(zb, cc, k, sems, device):
        b = zb * 2 + cc
        at = outw.at[b, pl.ds(k * o_rows, o_rows)]
        return copy(at, at, sems.at[zb * OC + k], orr.at[b * OC + k], device)

    def q_copy(cc, k, sems, device, first=False):
        rows_k = pl.ds(k * o_rows, o_rows)
        dst = outx.at[cc, rows_k]
        src = outw.at[z * 2 + c, rows_k] if first else dst
        return copy(src, dst, sems.at[k], oxr.at[cc * OC + k], device)

    def h_copy(kind, zq, source, to):
        sems = (hs, hs_h)[kind]
        return copy(att.at[zq], heads.at[kind, 0, source], sems.at[zq], hr.at[kind * Z + source], dev(to, j))

    def x_copy(kind, source):
        i = kind * Z + source
        return copy(heads.at[kind, 0, source], heads.at[kind, 1, source], xs.at[i], xr.at[i], across_dev)

    def m_copy(zb, slot, zz, leaving):
        zl = lax.rem(zb, share)
        if leaving:
            return copy(
                away.at[slot], other.at[zl, x], ms.at[slot], yr.at[zl * 2 + x], dev(zz, across, ty)
            )
        return copy(away.at[slot], terms.at[zb, x], ms.at[slot], mr.at[zb], dev(zz, across))

    def n_copy(leaving):
        zl = lax.rem(far, share)
        if leaving:
            return copy(away.at[Z + 1], other.at[zl, x], ns.at[0], yr.at[zl * 2 + x], dev(end, j, ty))
        return copy(away.at[Z + 1], terms.at[far, x], ns.at[0], nr.at[0], dev(end, j))

    def y_copy(zb, xx):
        zl = lax.rem(zb, share)
        return copy(
            terms.at[zb, xx], other.at[zl, xx], ys.at[zb * 2 + xx], yr.at[zl * 2 + xx], y_dev
        )

    for i in range(1, Z):
        start(None, lambda zz=near[i]: c_copy(z, zz))
    for i in range(1, Z):
        start(None, lambda zz=near[i]: w_z(zz))
    start(None, lambda: w_copy(me, ws_x, across_dev, True))
    start(None, lambda: w_copy(me, ws_s, sib_dev, True))

    q_make = lambda: copy(sq_own, sq_other, qs.at[0], qr.at[0], y_dev)
    start(None, q_make)
    arrive(None, q_make)
    squares = own_squares + sq_other[:, 0:1]
    inverse = lax.rsqrt(squares / (T * width) + EPSILON)
    tokens[z, t] = (wide * inverse * gain_here[...]).astype(jnp.bfloat16)

    for k in range(TC):
        start(has_up, lambda k=k: t_copy(z, t, k, ts_up, up))
        start(has_down, lambda k=k: t_copy(z, t, k, ts_dn, down))
        start(None, lambda k=k: t_copy(z, t, k, ts_y, y_dev))

    def own_o(k, in_):
        device = inward if in_ else outward
        ups = low if in_ else 1 - low
        return [
            (ups == 1, lambda: o_copy(z, c, k, os_up, device)),
            (ups == 0, lambda: o_copy(z, c, k, os_dn, device)),
        ]

    def cast_w(b):
        return [
            (None, lambda: w_copy(b, ws_x, across_dev)), (None, lambda: w_copy(b, ws_s, sib_dev))
        ]

    def pass_t(zz, k):
        return [
            ((zz < z) & has_up, lambda: t_copy(zz, t, k, ts_up, up)),
            ((zz > z) & has_down, lambda: t_copy(zz, t, k, ts_dn, down)),
            (None, lambda: t_copy(zz, t, k, ts_y, y_dev)),
        ]

    def pass_o(zb, k):
        return [
            (
                (zb < z) & has_up & ~((z + 1 == Z - 1) & (zb == 0)),
                lambda: o_copy(zb, c, k, os_up, up),
            ),
            (
                (zb > z) & has_down & ~((z - 1 == 0) & (zb == Z - 1)),
                lambda: o_copy(zb, c, k, os_dn, down),
            ),
            (None, lambda: o_copy(zb, c, k, os_s, sib_dev)),
        ]

    def moves(op):
        kind, last = op[0], op[-1]
        if op == "WA":
            return [
                (
                    lambda b=zz * J + across: w_copy(b, ws_s, sib_dev),
                    [(None, lambda b=zz * J + across: w_copy(b, ws_s, sib_dev))],
                )
                for zz in range(Z)
            ]
        if kind == "X":
            return [
                (None, [(None, lambda k=k: q_copy(c, k, ox_x, across_dev, True))]) for k in range(OC)
            ]
        if kind == "F":
            return [
                (
                    lambda k=k: q_copy(c, k, ox_s, sib_dev),
                    [(None, lambda k=k: q_copy(c, k, ox_s, sib_dev))],
                )
                for k in range(OC)
            ]
        n = int(last)
        if kind == "W":
            b = near[n] * J + j
            return [(lambda: w_copy(b, ws_s, sib_dev), cast_w(b))]
        if kind == "T":
            zz = near[int(op[1])]
            return [(lambda: t_copy(zz, t, n, ts_y, y_dev), pass_t(zz, n))]
        if kind in "IOE":
            return [(None, own_o(n, kind != "O"))]
        zb = near["ABC".index(kind) + 1]
        return [(lambda: o_copy(zb, c, n, os_s, sib_dev), pass_o(zb, n))]

    def act(op):
        for awaited, copies in moves(op):
            if awaited is not None:
                awaited().wait_recv()
            for cond, make in copies:
                if_(cond, lambda: make().start())

    def between(step):
        for (place, stays), order in ORDER.items():
            first = 0
            for i, op in enumerate(order):
                if op == step:
                    break
                if op in STEPS:
                    first = i + 1
            todo = order[first:i]
            if todo:
                mine = (inside if place else at_end) & (keeps == stays)

                def run():
                    for op in todo:
                        act(op)

                pl.when(mine)(run)

    everyone = (
        ["W1", "W2", "W3", "X", "F0", "WA"]
        + ["T%d%d" % (i, k) for i in range(1, Z) for k in range(TC)]
        + ["%s%d" % (f, k) for f in "AB" for k in range(OC)]
    )
    within = ["%s%d" % (f, k) for f in "IOC" for k in range(OC)]
    from_end = ["E%d" % k for k in range(OC)]
    for ops, base_cond in ((everyone, None), (within, inside), (from_end, at_end)):
        for op in ops:
            for _, copies in moves(op):
                for cond, make in copies:
                    if base_cond is not None:
                        cond = base_cond if cond is None else base_cond & cond
                    started.append((cond, make))

    placed.wait()
    for k in range(OC):
        start(None, lambda k=k: o_copy(z, c, k, os_s, sib_dev))

    def product(i):
        zz = near[i]
        for k in range(TC):
            arrive(None, lambda k=k: t_copy(zz, T - 1 - t, k, ts_y, y_dev))
        result = None
        for tt in range(T):
            term = jnp.dot(
                tokens[zz, tt], weights[tt * width : (tt + 1) * width, :],
                preferred_element_type=jnp.float32,
            )
            result = term if result is None else result + term
        for g in range(heads_here):
            queries[zz, g * slots : (g + 1) * slots, :] = result[
                :, g * HD : (g + 1) * HD
            ].astype(jnp.bfloat16)
        b = zz * J + j
        top = pl.multiple_of(b * block, 16)
        kv[pl.ds(top, slots), :] = result[:, q_cols:].astype(jnp.bfloat16)
        kv[pl.ds(pl.multiple_of(top + slots, 16), pad), :] = counts[zz]
        start(None, lambda: k_copy(b, ks_x, across_dev))
        start(None, lambda: k_copy(b, ks_s, sib_dev))

    between("P0")
    for i in range(1, Z):
        arrive(None, lambda: c_copy(near[i], z))
    for zz in range(Z):
        for jj in (sib, diag):
            arrive(None, lambda: w_copy(zz * J + jj, ws_s, sib_dev))
    product(0)
    for i in range(1, Z):
        between("P%d" % i)
        product(i)
    between("KV")
    for i in range(Z):
        b = near[i] * J + across
        arrive(None, lambda: k_copy(b, ks_s, sib_dev))
        start(None, lambda b=b: k_copy(b, ks_s, sib_dev))
    for zz in range(Z):
        for jj in (sib, diag):
            arrive(None, lambda: k_copy(zz * J + jj, ks_s, sib_dev))
    between("ATT")

    keys = Z * J * block
    key_pos = lax.broadcasted_iota(jnp.int32, (1, keys), 1)
    seen = jnp.zeros((1, keys), jnp.float32)
    for b in range(Z * J):
        limit = kv[b * block + slots : b * block + slots + 1, 0:1].astype(jnp.float32) + b * block
        inside_b = (key_pos >= b * block) & (key_pos < (b + 1) * block)
        seen = jnp.where(inside_b & (key_pos.astype(jnp.float32) < limit), 1.0, seen)
    key_pos = jnp.where(seen > 0, key_pos, keys)
    row = lax.broadcasted_iota(jnp.int32, (slots, 1), 0)
    row = jnp.concatenate([row] * heads_here, axis=0) + j * block

    for zq in range(Z):
        n = (zq + 1) * J * block
        scores = lax.dot_general(
            queries[zq], kv[:n, :HD], (((1,), (1,)), ((), ())), preferred_element_type=jnp.float32
        ) * HD ** (-0.5)
        visible = key_pos[:, :n] <= row + zq * J * block
        scores = jnp.where(visible, scores, MASKED_SCORE)
        expons = jnp.exp(scores - jnp.max(scores, axis=1, keepdims=True))
        row_total = jnp.sum(expons, axis=1, keepdims=True)
        weighted = jnp.dot(
            expons.astype(jnp.bfloat16), kv[:n, HD:], preferred_element_type=jnp.float32
        )
        attended = (weighted / row_total).astype(jnp.bfloat16)
        for g in range(heads_here):
            att[zq, :, g * HD : (g + 1) * HD] = attended[g * slots : (g + 1) * slots]

        @pl.when(z == zq)
        def _():
            heads[0, 0, z] = att[zq]

        start(z != zq, lambda zq=zq: h_copy(0, zq, z, zq))
        if zq in (0, Z - 1):
            helper = 1 if zq == 0 else Z - 2

            @pl.when(z == helper)
            def _():
                heads[1, 0, z] = att[zq]

            start(z != helper, lambda zq=zq, helper=helper: h_copy(1, zq, z, helper))

    start(None, lambda: x_copy(0, z))
    start(helps, lambda: x_copy(1, z))
    between("HR")
    for kind, cond in ((0, None), (1, helps)):
        if kind:
            between("HH")
        for i in range(1, Z):
            arrive(cond, lambda: h_copy(kind, 0, near[i], z))
            start(cond, lambda kind=kind, i=i: x_copy(kind, near[i]))

    begun = len(started)

    between("L0")
    for k in range(OC):
        arrive(None, lambda: o_copy(z, 1 - c, k, os_s, sib_dev))
        arrive(None, lambda: q_copy(1 - c, k, ox_s, sib_dev))
    every = jnp.concatenate([heads[0, 0, zz] for zz in range(Z)], axis=1)
    for cc in range(2):
        at = slice(cc * part, (cc + 1) * part)
        for to, block_of in ((x, outw.at[z * 2 + cc]), (1 - x, outx.at[cc])):
            terms[z, to, :, at] = jnp.dot(
                every, block_of[...], preferred_element_type=jnp.float32
            ).astype(jnp.bfloat16)
    for xx in (1 - x, x):
        start(z // share != t, lambda xx=xx: y_copy(z, xx))

    between("HX")
    for zz in range(Z):
        arrive(None, lambda: x_copy(0, zz))

    def emit(kind, zb, own_slot, away_slot):
        every = jnp.concatenate(
            [
                jnp.concatenate([heads[kind, xx, zz] for zz in range(Z)], axis=1)
                for xx in range(2)
            ],
            axis=0,
        )
        if kind == 0:
            for k in range(OC):
                o_copy(zb, 1 - c, k, os_s, sib_dev).wait_recv()
        for cc in range(2):
            result = jnp.dot(
                every, outw[zb * 2 + cc], preferred_element_type=jnp.float32
            ).astype(jnp.bfloat16)
            at = slice(cc * part, (cc + 1) * part)
            if own_slot is None:
                terms[zb, x, :, at] = result[:slots]
            else:
                away[own_slot, :, at] = result[:slots]
            away[away_slot, :, at] = result[slots:]

    def hand_out(zb, slot, zz, cond=None):
        stays = zb // share == t
        leaves = zb // share != t
        if cond is not None:
            stays, leaves = cond & stays, cond & leaves
        start(stays, lambda: m_copy(zb, slot, zz, False))
        start(leaves, lambda: m_copy(zb, slot, zz, True))
        return stays, leaves

    def emit_own(zb, cond=None):
        if_(cond, lambda: emit(0, zb, None, zb))
        _, leaves = hand_out(zb, zb, z, cond)
        start(leaves, lambda: y_copy(zb, x))

    early = keeps * near[2] + (1 - keeps) * near[1]
    late = keeps * near[1] + (1 - keeps) * near[2]
    between("S1")
    emit_own(early)
    between("S2")
    emit_own(far, inside)
    between("HP")
    for zz in range(Z):
        arrive(helps, lambda: x_copy(1, zz))
    if_(helps, lambda: emit(1, far, Z + 1, Z))
    stays, leaves = hand_out(far, Z, end, helps)
    start(stays, lambda: n_copy(False))
    start(leaves, lambda: n_copy(True))
    between("S3")
    emit_own(late)
    for cond, make in started[:begun]:
        if_(cond, lambda: make().wait_send())

    for zl in range(share):
        zb = t * share + zl
        arrive(zb != z, lambda: m_copy(zb, zb, z, False))
        arrive(at_end & (zb == far), lambda: n_copy(False))
        for xx in range(2):
            y_copy(zl, xx).wait_recv()
            top = (zl * 2 + xx) * 2 * part
            mixed_ref[:, top : top + 2 * part] = (
                terms[zb, xx].astype(jnp.float32) + other[zl, xx].astype(jnp.float32)
            ).astype(jnp.bfloat16)

    for cond, make in started[begun:]:
        if_(cond, lambda: make().wait_send())


def stepped(Z, J, T, slots, depth, gain, hidden, w_query, w_key, w_value, w_out):
    rows, width = hidden.shape
    part = w_query.shape[0]
    q_cols = w_query.shape[1] // Z
    cols = q_cols + 2 * HD
    pad = 16
    n = Z * J
    TC, OC = 6, 4
    vmem = pl.BlockSpec(memory_space=pltpu.VMEM)
    dma = pltpu.SemaphoreType.DMA
    bf16, f32 = jnp.bfloat16, jnp.float32
    return pl.pallas_call(
        functools.partial(step_kernel, Z, J, T, TC, OC),
        out_shape=(
            jax.ShapeDtypeStruct((slots, width), bf16), jax.ShapeDtypeStruct((slots, rows), bf16)
        ),
        in_specs=[pl.BlockSpec(memory_space=pltpu.HBM)] * 7,
        out_specs=(vmem, vmem),
        scratch_shapes=[
            pltpu.VMEM((1, rows), jnp.int32),
            pltpu.VMEM((1, width), f32),
            pltpu.VMEM((rows, width), bf16),
            pltpu.VMEM((Z, part, cols), bf16),
            pltpu.VMEM((n * part, cols), bf16),
            pltpu.VMEM((Z, T, slots, width), bf16),
            pltpu.VMEM((Z, pad, 2 * HD), bf16),
            pltpu.VMEM((slots, LANES), f32),
            pltpu.VMEM((slots, LANES), f32),
            pltpu.VMEM((Z, q_cols // HD * slots, HD), bf16),
            pltpu.VMEM((n * (slots + pad), 2 * HD), bf16),
            pltpu.VMEM((Z * 2,) + w_out.shape, bf16),
            pltpu.VMEM((2,) + w_out.shape, bf16),
            pltpu.VMEM((Z, slots, q_cols), bf16),
            pltpu.VMEM((2, 2, Z, slots, q_cols), bf16),
            pltpu.VMEM((Z, 2, slots, 2 * part), bf16),
            pltpu.VMEM((Z + 2, slots, 2 * part), bf16),
            pltpu.VMEM((Z // T, 2, slots, 2 * part), bf16),
            dma((Z,)), dma((n,)), dma((n,)), dma((n,)), dma((Z,)), dma((Z,)), dma((1,)), dma((1,)),
            dma((Z * TC,)), dma((Z * TC,)), dma((Z * TC,)), dma((Z * T * TC,)),
            dma((n,)), dma((n,)), dma((n,)),
            dma((Z * OC,)), dma((Z * OC,)), dma((Z * OC,)), dma((Z * 2 * OC,)),
            dma((Z,)), dma((Z,)), dma((2 * Z,)), dma((2 * Z,)), dma((2 * Z,)),
            dma((Z + 1,)), dma((Z,)), dma((1,)), dma((1,)), dma((2 * Z,)), dma((Z // T * 2,)),
            dma((4,)), dma((3 * (Z + 1),)),
            dma((OC,)), dma((OC,)), dma((2 * OC,)),
        ],
        compiler_params=pltpu.CompilerParams(
            collective_id=0, has_side_effects=True, vmem_limit_bytes=32 * 1024 * 1024
        ),
    )(depth, gain, hidden, w_query, w_key, w_value, w_out)


def body(n_seq, n_tensor, hidden, depth, norm_gain, w_query, w_key, w_value, w_out):
    rows, width = hidden.shape
    slots = rows // 2
    d_model = width * n_tensor
    kv_heads = w_key.shape[1] // HD
    group = w_query.shape[1] // w_key.shape[1]
    J = kv_heads
    Z = n_seq // J
    part = w_query.shape[0]
    head_cols = (group + 2) * HD
    me = lax.axis_index("seq")
    t = lax.axis_index("tensor")
    j = lax.rem(me, J)
    z = me // J
    z_groups = [[a * J + b for a in range(Z)] for b in range(J)]

    def shift_j(value, k):
        pairs = [(a * J + b, a * J + (b + k) % J) for a in range(Z) for b in range(J)]
        return lax.ppermute(value, "seq", pairs)

    def shift_t(value, k):
        return lax.ppermute(value, "tensor", [(b, (b + k) % n_tensor) for b in range(n_tensor)])

    def gather_z(value, axis):
        return lax.all_gather(value, "seq", axis=axis, tiled=True, axis_index_groups=z_groups)

    def gather_j(value):
        return [value] + [shift_j(value, J - m) for m in range(1, J)]

    def exchange_j(block_for):
        return [block_for(j)] + [
            shift_j(block_for(lax.rem(j + J - m, J)), J - m) for m in range(1, J)
        ]

    living = depth > STEP
    index = jnp.arange(rows, dtype=jnp.int32)
    rank = jnp.sum(
        jnp.where(living[None, :] & (index[None, :] <= index[:, None]), 1, 0), axis=1
    ) - 1
    slot_ids = jnp.arange(slots, dtype=jnp.int32)
    select = (living[None, :] & (rank[None, :] == slot_ids[:, None])).astype(jnp.bfloat16)
    filled = jnp.sum(select.astype(jnp.float32), axis=1).astype(jnp.bfloat16)
    packed = jnp.dot(select, hidden, preferred_element_type=jnp.float32).astype(jnp.bfloat16)

    def columns_of(i):
        return jnp.concatenate(
            [
                lax.dynamic_slice_in_dim(w_query, i * group * HD, group * HD, axis=1),
                lax.dynamic_slice_in_dim(w_key, i * HD, HD, axis=1),
                lax.dynamic_slice_in_dim(w_value, i * HD, HD, axis=1),
            ],
            axis=1,
        )

    fast = (
        n_tensor == 2 and J == 4 and Z == kv_heads and Z == J and Z % n_tensor == 0 and slots % 96 == 0
        and slots <= 256 and part == w_out.shape[1] and part % 128 == 0 and width % 128 == 0 and w_out.shape[0] % 64 == 0
    )
    if fast:
        operands = (
            depth[None, :], norm_gain.reshape(n_tensor, 1, width),
            hidden, w_query, w_key, w_value, w_out,
        )
        mixed, chosen = stepped(
            Z, J, n_tensor, slots,
            *(pltpu.with_memory_space_constraint(a, pltpu.HBM) for a in operands),
        )
        return jnp.einsum(
            "sr,sf->rf", chosen, mixed, preferred_element_type=jnp.float32
        ).astype(jnp.bfloat16)

    w_rows = rolled(exchange_j(columns_of), 0, j)
    weights = gather_z(w_rows, 0)
    out_rows = group * HD
    twice = jnp.concatenate([w_out, w_out], axis=0) if J > 1 else w_out
    w_out_turned = lax.dynamic_slice_in_dim(twice, j * out_rows, J * out_rows, axis=0)
    out_weights = gather_z(w_out_turned, 1)

    features = rolled([packed] + [shift_t(packed, n_tensor - m) for m in range(1, n_tensor)], 1, t)
    widened = features.astype(jnp.float32)
    inverse = lax.rsqrt(jnp.mean(widened * widened, axis=1, keepdims=True) + EPSILON)
    normed = (widened * inverse * norm_gain[None, :]).astype(jnp.bfloat16)
    block_rows = J * slots
    tokens = jnp.concatenate(gather_j(normed), axis=0)
    flags = jnp.concatenate(gather_j(filled), axis=0)

    qkv = jnp.dot(tokens, weights, preferred_element_type=jnp.float32).astype(jnp.bfloat16)
    queries = qkv[:, : group * HD].reshape(block_rows, group, HD)
    kv = qkv[:, group * HD :]
    flag_rows = -(-block_rows // (2 * HD))
    flag_pad = -(-flag_rows // 16) * 16
    flag_block = jnp.pad(flags, (0, flag_pad * 2 * HD - block_rows)).reshape(flag_pad, 2 * HD)
    arrived = gather_z(jnp.concatenate([kv, flag_block], axis=0), 0).reshape(
        Z, block_rows + flag_pad, 2 * HD
    )
    keys = arrived[:, :block_rows, :HD].reshape(Z * block_rows, HD)
    values = arrived[:, :block_rows, HD:].reshape(Z * block_rows, HD)
    key_flags = arrived[:, block_rows:].reshape(Z, -1)[:, :block_rows].reshape(Z * block_rows)

    local = jnp.arange(block_rows, dtype=jnp.int32)
    turned = lax.rem(local // slots + j, J) * slots + lax.rem(local, slots)
    query_pos = z * block_rows + turned
    key_pos = (jnp.arange(Z, dtype=jnp.int32)[:, None] * block_rows + turned[None, :]).reshape(-1)
    visible = (key_flags[None, :] > 0) & (key_pos[None, :] <= query_pos[:, None])
    scores = jnp.einsum(
        "qgd,kd->gqk", queries, keys, preferred_element_type=jnp.float32
    ) * HD ** (-0.5)
    scores = jnp.where(visible[None], scores, MASKED_SCORE)
    expons = jnp.exp(scores - jnp.max(scores, axis=-1, keepdims=True))
    total = jnp.sum(expons, axis=-1)
    weighted = jnp.einsum(
        "gqk,kd->gqd", expons.astype(jnp.bfloat16), values, preferred_element_type=jnp.float32
    )
    attended = (weighted / total[..., None]).astype(jnp.bfloat16)
    attended = jnp.transpose(attended, (1, 0, 2)).reshape(block_rows, group * HD)
    attended = rolled([attended[m * slots : (m + 1) * slots] for m in range(J)], 0, j)
    heads = jnp.concatenate(gather_j(attended), axis=1)
    terms = jnp.dot(heads, out_weights, preferred_element_type=jnp.float32).astype(jnp.bfloat16)
    own_cols = w_out.shape[1]
    mine = exchange_j(lambda i: lax.dynamic_slice_in_dim(terms, i * slots, slots, axis=0))
    mine = [piece.reshape(slots, Z, 1, own_cols) for piece in mine]
    mine = rolled(mine, 2, j).reshape(slots, d_model)

    def features_of(i):
        return lax.dynamic_slice_in_dim(mine, i * width, width, axis=1)

    owned = features_of(t).astype(jnp.float32)
    for k in range(1, n_tensor):
        owned = owned + shift_t(features_of(lax.rem(t + k, n_tensor)), k).astype(jnp.float32)
    mixed = owned.astype(jnp.bfloat16)
    return jnp.einsum(
        "sr,sf->rf", select, mixed, preferred_element_type=jnp.float32
    ).astype(jnp.bfloat16)


def solution(mesh):
    n_seq, n_tensor = mesh.shape["seq"], mesh.shape["tensor"]

    def step(*args):
        return body(n_seq, n_tensor, *args)

    return jax.shard_map(
        step,
        mesh=mesh,
        in_specs=(
            P("seq", "tensor"),
            P("seq"),
            P(),
            P("seq", "tensor"),
            P("seq", "tensor"),
            P("seq", "tensor"),
            P("tensor", "seq"),
        ),
        out_specs=P("seq", "tensor"),
        check_vma=False,
    )
```

```python
import functools

import jax
import jax.numpy as jnp
from jax import lax
from jax.experimental import pallas as pl
from jax.experimental.pallas import tpu as pltpu
from jax.sharding import PartitionSpec as P

HD = 128
STEP = 2
EPSILON = 1e-05
MASKED_SCORE = -1e30


def rolled(pieces, axis, my):
    n = len(pieces)
    if n == 1:
        return pieces[0]
    width = pieces[0].shape[axis]
    twice = jnp.concatenate(pieces + pieces, axis=axis)
    start = lax.rem(n - my, n) * width
    return lax.dynamic_slice_in_dim(twice, start, n * width, axis=axis)


LANES = 128
ORDER = {
    (0, 0): (
        "E0", "E1", "E2", "E3", "T10", "W1", "W3", "T11", "T12", "T13", "T20", "T14",
        "T21", "W2", "T22", "T15", "T23", "T24", "X", "T25", "T30", "WA", "T31", "P0",
        "P1", "T32", "T33", "P2", "T34", "T35", "P3", "A0", "A1", "KV", "ATT", "HR",
        "A2", "B0", "F0", "HH", "B1", "L0", "A3", "HX", "S1", "S2", "B2", "HP",
        "B3", "S3", "END",
    ),
    (0, 1): (
        "E0", "E1", "E2", "E3", "W1", "T10", "T11", "T12", "X", "T13", "F0", "W2",
        "T20", "T21", "T22", "T14", "W3", "T23", "T30", "T15", "T24", "T25", "T31", "WA",
        "P0", "T32", "T33", "T34", "P1", "T35", "P2", "P3", "KV", "ATT", "B0", "A0",
        "B1", "B2", "HR", "B3", "HH", "L0", "HX", "A1", "S1", "S2", "HP", "A2",
        "A3", "S3", "END",
    ),
    (1, 0): (
        "W1", "W2", "W3", "T10", "T11", "T12", "T20", "T21", "T22", "T13", "T23", "T24",
        "T14", "WA", "T25", "A0", "X", "T15", "T30", "T31", "P0", "T32", "O0", "T33",
        "T34", "I0", "P1", "P2", "T35", "O1", "O2", "I1", "I2", "B0", "A1", "F0",
        "O3", "I3", "P3", "KV", "ATT", "A2", "C0", "B1", "HR", "A3", "HH", "B2",
        "C1", "L0", "HX", "B3", "S1", "C2", "C3", "S2", "HP", "S3", "END",
    ),
    (1, 1): (
        "X", "W3", "T10", "W1", "T11", "W2", "T12", "T13", "T20", "T14", "T21", "T15",
        "T22", "A0", "T23", "T24", "I0", "T30", "WA", "A1", "F0", "T25", "T31", "I1",
        "I2", "P0", "I3", "P1", "T32", "T33", "T34", "C0", "P2", "T35", "B0", "P3",
        "B1", "B2", "O0", "KV", "ATT", "B3", "O1", "A2", "A3", "O2", "C1", "HR",
        "HH", "L0", "HX", "O3", "S1", "C2", "C3", "S2", "HP", "S3", "END",
    ),
}
STEPS = ("P0", "P1", "P2", "P3", "KV", "ATT", "HR", "HH", "L0", "HX", "S1", "S2", "HP", "S3", "END")
MESH = pl.DeviceIdType.MESH


def step_kernel(
    Z, J, T, TC, OC, depth, gain, hidden, w_query, w_key, w_value, w_out, mixed_ref, select_ref,
    depth_here, gain_here, raw, w_blocks, weights, tokens, counts, sq_own, sq_other, queries, kv, outw, outx, att, heads, terms, away, other,
    ws_z, ws_s, ws_x, wr, cs, cr, qs, qr, ts_up, ts_dn, ts_y, tr, ks_s, ks_x, kr,
    os_up, os_dn, os_s, orr, hs, hs_h, hr, xs, xr, ms, mr, ns, nr, ys, yr, ls, lw,
    ox_x, ox_s, oxr,
):
    me, t = lax.axis_index("seq"), lax.axis_index("tensor")
    z, j = me // J, lax.rem(me, J)
    rows, width = hidden.shape
    slots = mixed_ref.shape[0]
    part, cols = w_blocks.shape[1:]
    q_cols = cols - 2 * HD
    heads_here = q_cols // HD
    pad = counts.shape[1]
    block = slots + pad
    t_rows = slots // TC
    o_rows = w_out.shape[0] // OC
    share = Z // T
    x, c = j // 2, lax.rem(j, 2)
    sib = j + 1 - 2 * c
    across = lax.rem(j + J // 2, J)
    diag = lax.rem(sib + J // 2, J)
    has_up, has_down = z < Z - 1, z > 0

    low = 1 - z // (Z // 2)
    depth_in = low * z + (1 - low) * (Z - 1 - z)
    at_end, inside = depth_in == 0, depth_in > 0
    helps = depth_in == 1

    def mirrored(a):
        return low * a + (1 - low) * (Z - 1 - a)

    near = [z] + [mirrored(i - (i <= depth_in).astype(jnp.int32)) for i in range(1, Z)]
    end, far = mirrored(0), mirrored(Z - 1)
    keeps = (t == z // share).astype(jnp.int32)

    ty = T - 1 - t

    def dev(zz, jj, tt=t):
        return (zz * J + jj, tt)

    sib_dev, across_dev, y_dev = dev(z, sib), dev(z, across), (me, ty)
    mid = mirrored(1)
    up, down = dev(z + 1, j), dev(z - 1, j)
    inward, outward = dev(z + 2 * low - 1, j), dev(z + 1 - 2 * low, j)

    def if_(cond, act):
        if cond is None:
            act()
        else:
            pl.when(cond)(lambda: act())

    barrier = pltpu.get_barrier_semaphore()

    def greet(device):
        pl.semaphore_signal(barrier, inc=1, device_id=device, device_id_type=MESH)

    for i in range(1, Z):
        greet(dev(near[i], j))
    for device in (sib_dev, across_dev, y_dev, dev(z, across, ty)):
        greet(device)
    for jj, tt in ((across, t), (across, ty), (j, ty)):
        if_(helps, lambda: greet(dev(end, jj, tt)))
        if_(at_end, lambda: greet(dev(mid, jj, tt)))

    local = []

    def bring(src, dst, sem):
        moved = pltpu.make_async_copy(src, dst, sem)
        moved.start()
        return moved

    fetched = bring(hidden, raw, ls.at[0])
    depths = bring(depth, depth_here, ls.at[2])
    gains = bring(gain.at[t], gain_here, ls.at[3])
    own_rows = pl.ds(pl.multiple_of(me * part, part), part)
    for i in range(Z + 1):
        zz = i if i < Z else z
        for n, (w, first, size) in enumerate(
            ((w_query, 0, q_cols), (w_key, q_cols, HD), (w_value, q_cols + HD, HD))
        ):
            to = slice(first, first + size)
            local.append(
                bring(
                    w.at[:, pl.ds(pl.multiple_of(zz * size, HD), size)],
                    w_blocks.at[i, :, to] if i < Z else weights.at[own_rows, to],
                    lw.at[3 * i + n],
                )
            )
    placed = bring(w_out, outw.at[z * 2 + c], ls.at[1])

    depths.wait()
    living = (depth_here[...] > STEP).astype(jnp.float32)
    before = lax.broadcasted_iota(jnp.int32, (rows, rows), 0)
    before = before <= lax.broadcasted_iota(jnp.int32, (rows, rows), 1)
    rank = jnp.dot(
        jnp.broadcast_to(living, (16, rows)).astype(jnp.bfloat16),
        before.astype(jnp.bfloat16),
        preferred_element_type=jnp.float32,
    )[0:1]
    slot = lax.broadcasted_iota(jnp.int32, (slots, rows), 0).astype(jnp.float32) + 1.0
    select = jnp.where((rank == slot) & (living > 0), 1.0, 0.0).astype(jnp.bfloat16)
    select_ref[...] = select
    total = jnp.sum(living, axis=1, keepdims=True)
    counts[z] = jnp.broadcast_to(total, counts.shape[1:]).astype(jnp.bfloat16)
    fetched.wait()
    wide = jnp.dot(select, raw[...], preferred_element_type=jnp.float32)
    own_squares = jnp.sum(wide * wide, axis=1, keepdims=True)
    sq_own[...] = jnp.broadcast_to(own_squares, sq_own.shape)
    gains.wait()
    for moved in local:
        moved.wait()
    pl.semaphore_wait(barrier, Z + 3 + 3 * (depth_in < 2).astype(jnp.int32))

    def copy(src, dst, send_sem, recv_sem, device):
        return pltpu.make_async_remote_copy(
            src_ref=src, dst_ref=dst, send_sem=send_sem, recv_sem=recv_sem,
            device_id=device, device_id_type=MESH,
        )

    started = []

    def start(cond, make):
        if_(cond, lambda: make().start())
        started.append((cond, make))

    def arrive(cond, make):
        if_(cond, lambda: make().wait_recv())

    def w_at(b):
        return weights.at[pl.ds(pl.multiple_of(b * part, part), part), :]

    def w_copy(b, sems, device, own=False):
        return copy(w_blocks.at[z] if own else w_at(b), w_at(b), sems.at[b], wr.at[b], device)

    def w_z(zz):
        return copy(w_blocks.at[zz], w_at(me), ws_z.at[zz], wr.at[me], dev(zz, j))

    def c_copy(zz, to):
        return copy(counts.at[zz], counts.at[zz], cs.at[to], cr.at[zz], dev(to, j))

    def t_copy(zz, tt, k, sems, device):
        at = tokens.at[zz, tt, pl.ds(k * t_rows, t_rows)]
        return copy(at, at, sems.at[zz * TC + k], tr.at[(zz * T + tt) * TC + k], device)

    def k_copy(b, sems, device):
        at = kv.at[pl.ds(pl.multiple_of(b * block, 16), block), :]
        return copy(at, at, sems.at[b], kr.at[b], device)

    def o_copy(zb, cc, k, sems, device):
        b = zb * 2 + cc
        at = outw.at[b, pl.ds(k * o_rows, o_rows)]
        return copy(at, at, sems.at[zb * OC + k], orr.at[b * OC + k], device)

    def q_copy(cc, k, sems, device, first=False):
        rows_k = pl.ds(k * o_rows, o_rows)
        dst = outx.at[cc, rows_k]
        src = outw.at[z * 2 + c, rows_k] if first else dst
        return copy(src, dst, sems.at[k], oxr.at[cc * OC + k], device)

    def h_copy(kind, zq, source, to):
        sems = (hs, hs_h)[kind]
        return copy(att.at[zq], heads.at[kind, 0, source], sems.at[zq], hr.at[kind * Z + source], dev(to, j))

    def x_copy(kind, source):
        i = kind * Z + source
        return copy(heads.at[kind, 0, source], heads.at[kind, 1, source], xs.at[i], xr.at[i], across_dev)

    def m_copy(zb, slot, zz, leaving):
        zl = lax.rem(zb, share)
        if leaving:
            return copy(
                away.at[slot], other.at[zl, x], ms.at[slot], yr.at[zl * 2 + x], dev(zz, across, ty)
            )
        return copy(away.at[slot], terms.at[zb, x], ms.at[slot], mr.at[zb], dev(zz, across))

    def n_copy(leaving):
        zl = lax.rem(far, share)
        if leaving:
            return copy(away.at[Z + 1], other.at[zl, x], ns.at[0], yr.at[zl * 2 + x], dev(end, j, ty))
        return copy(away.at[Z + 1], terms.at[far, x], ns.at[0], nr.at[0], dev(end, j))

    def y_copy(zb, xx):
        zl = lax.rem(zb, share)
        return copy(
            terms.at[zb, xx], other.at[zl, xx], ys.at[zb * 2 + xx], yr.at[zl * 2 + xx], y_dev
        )

    for i in range(1, Z):
        start(None, lambda zz=near[i]: c_copy(z, zz))
    for i in range(1, Z):
        start(None, lambda zz=near[i]: w_z(zz))
    start(None, lambda: w_copy(me, ws_x, across_dev, True))
    start(None, lambda: w_copy(me, ws_s, sib_dev, True))

    q_make = lambda: copy(sq_own, sq_other, qs.at[0], qr.at[0], y_dev)
    start(None, q_make)
    arrive(None, q_make)
    squares = own_squares + sq_other[:, 0:1]
    inverse = lax.rsqrt(squares / (T * width) + EPSILON)
    tokens[z, t] = (wide * inverse * gain_here[...]).astype(jnp.bfloat16)

    for k in range(TC):
        start(has_up, lambda k=k: t_copy(z, t, k, ts_up, up))
        start(has_down, lambda k=k: t_copy(z, t, k, ts_dn, down))
        start(None, lambda k=k: t_copy(z, t, k, ts_y, y_dev))

    def own_o(k, in_):
        device = inward if in_ else outward
        ups = low if in_ else 1 - low
        return [
            (ups == 1, lambda: o_copy(z, c, k, os_up, device)),
            (ups == 0, lambda: o_copy(z, c, k, os_dn, device)),
        ]

    def cast_w(b):
        return [
            (None, lambda: w_copy(b, ws_x, across_dev)), (None, lambda: w_copy(b, ws_s, sib_dev))
        ]

    def pass_t(zz, k):
        return [
            ((zz < z) & has_up, lambda: t_copy(zz, t, k, ts_up, up)),
            ((zz > z) & has_down, lambda: t_copy(zz, t, k, ts_dn, down)),
            (None, lambda: t_copy(zz, t, k, ts_y, y_dev)),
        ]

    def pass_o(zb, k):
        return [
            (
                (zb < z) & has_up & ~((z + 1 == Z - 1) & (zb == 0)),
                lambda: o_copy(zb, c, k, os_up, up),
            ),
            (
                (zb > z) & has_down & ~((z - 1 == 0) & (zb == Z - 1)),
                lambda: o_copy(zb, c, k, os_dn, down),
            ),
            (None, lambda: o_copy(zb, c, k, os_s, sib_dev)),
        ]

    def moves(op):
        kind, last = op[0], op[-1]
        if op == "WA":
            return [
                (
                    lambda b=zz * J + across: w_copy(b, ws_s, sib_dev),
                    [(None, lambda b=zz * J + across: w_copy(b, ws_s, sib_dev))],
                )
                for zz in range(Z)
            ]
        if kind == "X":
            return [
                (None, [(None, lambda k=k: q_copy(c, k, ox_x, across_dev, True))]) for k in range(OC)
            ]
        if kind == "F":
            return [
                (
                    lambda k=k: q_copy(c, k, ox_s, sib_dev),
                    [(None, lambda k=k: q_copy(c, k, ox_s, sib_dev))],
                )
                for k in range(OC)
            ]
        n = int(last)
        if kind == "W":
            b = near[n] * J + j
            return [(lambda: w_copy(b, ws_s, sib_dev), cast_w(b))]
        if kind == "T":
            zz = near[int(op[1])]
            return [(lambda: t_copy(zz, t, n, ts_y, y_dev), pass_t(zz, n))]
        if kind in "IOE":
            return [(None, own_o(n, kind != "O"))]
        zb = near["ABC".index(kind) + 1]
        return [(lambda: o_copy(zb, c, n, os_s, sib_dev), pass_o(zb, n))]

    def act(op):
        for awaited, copies in moves(op):
            if awaited is not None:
                awaited().wait_recv()
            for cond, make in copies:
                if_(cond, lambda: make().start())

    def between(step):
        for (place, stays), order in ORDER.items():
            first = 0
            for i, op in enumerate(order):
                if op == step:
                    break
                if op in STEPS:
                    first = i + 1
            todo = order[first:i]
            if todo:
                mine = (inside if place else at_end) & (keeps == stays)

                def run():
                    for op in todo:
                        act(op)

                pl.when(mine)(run)

    everyone = (
        ["W1", "W2", "W3", "X", "F0", "WA"]
        + ["T%d%d" % (i, k) for i in range(1, Z) for k in range(TC)]
        + ["%s%d" % (f, k) for f in "AB" for k in range(OC)]
    )
    within = ["%s%d" % (f, k) for f in "IOC" for k in range(OC)]
    from_end = ["E%d" % k for k in range(OC)]
    for ops, base_cond in ((everyone, None), (within, inside), (from_end, at_end)):
        for op in ops:
            for _, copies in moves(op):
                for cond, make in copies:
                    if base_cond is not None:
                        cond = base_cond if cond is None else base_cond & cond
                    started.append((cond, make))

    placed.wait()
    for k in range(OC):
        start(None, lambda k=k: o_copy(z, c, k, os_s, sib_dev))

    def product(i):
        zz = near[i]
        for k in range(TC):
            arrive(None, lambda k=k: t_copy(zz, T - 1 - t, k, ts_y, y_dev))
        result = None
        for tt in range(T):
            term = jnp.dot(
                tokens[zz, tt], weights[tt * width : (tt + 1) * width, :],
                preferred_element_type=jnp.float32,
            )
            result = term if result is None else result + term
        for g in range(heads_here):
            queries[zz, g * slots : (g + 1) * slots, :] = result[
                :, g * HD : (g + 1) * HD
            ].astype(jnp.bfloat16)
        b = zz * J + j
        top = pl.multiple_of(b * block, 16)
        kv[pl.ds(top, slots), :] = result[:, q_cols:].astype(jnp.bfloat16)
        kv[pl.ds(pl.multiple_of(top + slots, 16), pad), :] = counts[zz]
        start(None, lambda: k_copy(b, ks_x, across_dev))
        start(None, lambda: k_copy(b, ks_s, sib_dev))

    between("P0")
    for i in range(1, Z):
        arrive(None, lambda: c_copy(near[i], z))
    for zz in range(Z):
        for jj in (sib, diag):
            arrive(None, lambda: w_copy(zz * J + jj, ws_s, sib_dev))
    product(0)
    for i in range(1, Z):
        between("P%d" % i)
        product(i)
    between("KV")
    for i in range(Z):
        b = near[i] * J + across
        arrive(None, lambda: k_copy(b, ks_s, sib_dev))
        start(None, lambda b=b: k_copy(b, ks_s, sib_dev))
    for zz in range(Z):
        for jj in (sib, diag):
            arrive(None, lambda: k_copy(zz * J + jj, ks_s, sib_dev))
    between("ATT")

    keys = Z * J * block
    key_pos = lax.broadcasted_iota(jnp.int32, (1, keys), 1)
    seen = jnp.zeros((1, keys), jnp.float32)
    for b in range(Z * J):
        limit = kv[b * block + slots : b * block + slots + 1, 0:1].astype(jnp.float32) + b * block
        inside_b = (key_pos >= b * block) & (key_pos < (b + 1) * block)
        seen = jnp.where(inside_b & (key_pos.astype(jnp.float32) < limit), 1.0, seen)
    key_pos = jnp.where(seen > 0, key_pos, keys)
    row = lax.broadcasted_iota(jnp.int32, (slots, 1), 0)
    row = jnp.concatenate([row] * heads_here, axis=0) + j * block

    for zq in range(Z):
        n = (zq + 1) * J * block
        scores = lax.dot_general(
            queries[zq], kv[:n, :HD], (((1,), (1,)), ((), ())), preferred_element_type=jnp.float32
        ) * HD ** (-0.5)
        visible = key_pos[:, :n] <= row + zq * J * block
        scores = jnp.where(visible, scores, MASKED_SCORE)
        expons = jnp.exp(scores - jnp.max(scores, axis=1, keepdims=True))
        row_total = jnp.sum(expons, axis=1, keepdims=True)
        weighted = jnp.dot(
            expons.astype(jnp.bfloat16), kv[:n, HD:], preferred_element_type=jnp.float32
        )
        attended = (weighted / row_total).astype(jnp.bfloat16)
        for g in range(heads_here):
            att[zq, :, g * HD : (g + 1) * HD] = attended[g * slots : (g + 1) * slots]

        @pl.when(z == zq)
        def _():
            heads[0, 0, z] = att[zq]

        start(z == zq, lambda: x_copy(0, z))
        start(z != zq, lambda zq=zq: h_copy(0, zq, z, zq))
        if zq in (0, Z - 1):
            helper = 1 if zq == 0 else Z - 2

            @pl.when(z == helper)
            def _():
                heads[1, 0, z] = att[zq]

            start(z == helper, lambda: x_copy(1, z))
            start(z != helper, lambda zq=zq, helper=helper: h_copy(1, zq, z, helper))

    between("HR")
    for kind, cond in ((0, None), (1, helps)):
        if kind:
            between("HH")
        for i in range(1, Z):
            arrive(cond, lambda: h_copy(kind, 0, near[i], z))
            start(cond, lambda kind=kind, i=i: x_copy(kind, near[i]))

    begun = len(started)

    between("L0")
    for k in range(OC):
        arrive(None, lambda: o_copy(z, 1 - c, k, os_s, sib_dev))
        arrive(None, lambda: q_copy(1 - c, k, ox_s, sib_dev))
    every = jnp.concatenate([heads[0, 0, zz] for zz in range(Z)], axis=1)
    for cc in range(2):
        at = slice(cc * part, (cc + 1) * part)
        for to, block_of in ((x, outw.at[z * 2 + cc]), (1 - x, outx.at[cc])):
            terms[z, to, :, at] = jnp.dot(
                every, block_of[...], preferred_element_type=jnp.float32
            ).astype(jnp.bfloat16)
    for xx in (1 - x, x):
        start(z // share != t, lambda xx=xx: y_copy(z, xx))

    between("HX")
    for zz in range(Z):
        arrive(None, lambda: x_copy(0, zz))

    def emit(kind, zb, own_slot, away_slot):
        every = jnp.concatenate(
            [
                jnp.concatenate([heads[kind, xx, zz] for zz in range(Z)], axis=1)
                for xx in range(2)
            ],
            axis=0,
        )
        if kind == 0:
            for k in range(OC):
                o_copy(zb, 1 - c, k, os_s, sib_dev).wait_recv()
        for cc in range(2):
            result = jnp.dot(
                every, outw[zb * 2 + cc], preferred_element_type=jnp.float32
            ).astype(jnp.bfloat16)
            at = slice(cc * part, (cc + 1) * part)
            if own_slot is None:
                terms[zb, x, :, at] = result[:slots]
            else:
                away[own_slot, :, at] = result[:slots]
            away[away_slot, :, at] = result[slots:]

    def hand_out(zb, slot, zz, cond=None):
        stays = zb // share == t
        leaves = zb // share != t
        if cond is not None:
            stays, leaves = cond & stays, cond & leaves
        start(stays, lambda: m_copy(zb, slot, zz, False))
        start(leaves, lambda: m_copy(zb, slot, zz, True))
        return stays, leaves

    def emit_own(zb, cond=None):
        if_(cond, lambda: emit(0, zb, None, zb))
        _, leaves = hand_out(zb, zb, z, cond)
        start(leaves, lambda: y_copy(zb, x))

    early = keeps * near[2] + (1 - keeps) * near[1]
    late = keeps * near[1] + (1 - keeps) * near[2]
    between("S1")
    emit_own(early)
    between("S2")
    emit_own(far, inside)
    between("HP")
    for zz in range(Z):
        arrive(helps, lambda: x_copy(1, zz))
    if_(helps, lambda: emit(1, far, Z + 1, Z))
    stays, leaves = hand_out(far, Z, end, helps)
    start(stays, lambda: n_copy(False))
    start(leaves, lambda: n_copy(True))
    between("S3")
    emit_own(late)
    for cond, make in started[:begun]:
        if_(cond, lambda: make().wait_send())

    for zl in range(share):
        zb = t * share + zl
        arrive(zb != z, lambda: m_copy(zb, zb, z, False))
        arrive(at_end & (zb == far), lambda: n_copy(False))
        for xx in range(2):
            y_copy(zl, xx).wait_recv()
            top = (zl * 2 + xx) * 2 * part
            mixed_ref[:, top : top + 2 * part] = (
                terms[zb, xx].astype(jnp.float32) + other[zl, xx].astype(jnp.float32)
            ).astype(jnp.bfloat16)

    for cond, make in started[begun:]:
        if_(cond, lambda: make().wait_send())


def stepped(Z, J, T, slots, depth, gain, hidden, w_query, w_key, w_value, w_out):
    rows, width = hidden.shape
    part = w_query.shape[0]
    q_cols = w_query.shape[1] // Z
    cols = q_cols + 2 * HD
    pad = 16
    n = Z * J
    TC, OC = 6, 4
    vmem = pl.BlockSpec(memory_space=pltpu.VMEM)
    dma = pltpu.SemaphoreType.DMA
    bf16, f32 = jnp.bfloat16, jnp.float32
    return pl.pallas_call(
        functools.partial(step_kernel, Z, J, T, TC, OC),
        out_shape=(
            jax.ShapeDtypeStruct((slots, width), bf16), jax.ShapeDtypeStruct((slots, rows), bf16)
        ),
        in_specs=[pl.BlockSpec(memory_space=pltpu.HBM)] * 7,
        out_specs=(vmem, vmem),
        scratch_shapes=[
            pltpu.VMEM((1, rows), jnp.int32),
            pltpu.VMEM((1, width), f32),
            pltpu.VMEM((rows, width), bf16),
            pltpu.VMEM((Z, part, cols), bf16),
            pltpu.VMEM((n * part, cols), bf16),
            pltpu.VMEM((Z, T, slots, width), bf16),
            pltpu.VMEM((Z, pad, 2 * HD), bf16),
            pltpu.VMEM((slots, LANES), f32),
            pltpu.VMEM((slots, LANES), f32),
            pltpu.VMEM((Z, q_cols // HD * slots, HD), bf16),
            pltpu.VMEM((n * (slots + pad), 2 * HD), bf16),
            pltpu.VMEM((Z * 2,) + w_out.shape, bf16),
            pltpu.VMEM((2,) + w_out.shape, bf16),
            pltpu.VMEM((Z, slots, q_cols), bf16),
            pltpu.VMEM((2, 2, Z, slots, q_cols), bf16),
            pltpu.VMEM((Z, 2, slots, 2 * part), bf16),
            pltpu.VMEM((Z + 2, slots, 2 * part), bf16),
            pltpu.VMEM((Z // T, 2, slots, 2 * part), bf16),
            dma((Z,)), dma((n,)), dma((n,)), dma((n,)), dma((Z,)), dma((Z,)), dma((1,)), dma((1,)),
            dma((Z * TC,)), dma((Z * TC,)), dma((Z * TC,)), dma((Z * T * TC,)),
            dma((n,)), dma((n,)), dma((n,)),
            dma((Z * OC,)), dma((Z * OC,)), dma((Z * OC,)), dma((Z * 2 * OC,)),
            dma((Z,)), dma((Z,)), dma((2 * Z,)), dma((2 * Z,)), dma((2 * Z,)),
            dma((Z + 1,)), dma((Z,)), dma((1,)), dma((1,)), dma((2 * Z,)), dma((Z // T * 2,)),
            dma((4,)), dma((3 * (Z + 1),)),
            dma((OC,)), dma((OC,)), dma((2 * OC,)),
        ],
        compiler_params=pltpu.CompilerParams(
            collective_id=0, has_side_effects=True, vmem_limit_bytes=32 * 1024 * 1024
        ),
    )(depth, gain, hidden, w_query, w_key, w_value, w_out)


def body(n_seq, n_tensor, hidden, depth, norm_gain, w_query, w_key, w_value, w_out):
    rows, width = hidden.shape
    slots = rows // 2
    d_model = width * n_tensor
    kv_heads = w_key.shape[1] // HD
    group = w_query.shape[1] // w_key.shape[1]
    J = kv_heads
    Z = n_seq // J
    part = w_query.shape[0]
    head_cols = (group + 2) * HD
    me = lax.axis_index("seq")
    t = lax.axis_index("tensor")
    j = lax.rem(me, J)
    z = me // J
    z_groups = [[a * J + b for a in range(Z)] for b in range(J)]

    def shift_j(value, k):
        pairs = [(a * J + b, a * J + (b + k) % J) for a in range(Z) for b in range(J)]
        return lax.ppermute(value, "seq", pairs)

    def shift_t(value, k):
        return lax.ppermute(value, "tensor", [(b, (b + k) % n_tensor) for b in range(n_tensor)])

    def gather_z(value, axis):
        return lax.all_gather(value, "seq", axis=axis, tiled=True, axis_index_groups=z_groups)

    def gather_j(value):
        return [value] + [shift_j(value, J - m) for m in range(1, J)]

    def exchange_j(block_for):
        return [block_for(j)] + [
            shift_j(block_for(lax.rem(j + J - m, J)), J - m) for m in range(1, J)
        ]

    living = depth > STEP
    index = jnp.arange(rows, dtype=jnp.int32)
    rank = jnp.sum(
        jnp.where(living[None, :] & (index[None, :] <= index[:, None]), 1, 0), axis=1
    ) - 1
    slot_ids = jnp.arange(slots, dtype=jnp.int32)
    select = (living[None, :] & (rank[None, :] == slot_ids[:, None])).astype(jnp.bfloat16)
    filled = jnp.sum(select.astype(jnp.float32), axis=1).astype(jnp.bfloat16)
    packed = jnp.dot(select, hidden, preferred_element_type=jnp.float32).astype(jnp.bfloat16)

    def columns_of(i):
        return jnp.concatenate(
            [
                lax.dynamic_slice_in_dim(w_query, i * group * HD, group * HD, axis=1),
                lax.dynamic_slice_in_dim(w_key, i * HD, HD, axis=1),
                lax.dynamic_slice_in_dim(w_value, i * HD, HD, axis=1),
            ],
            axis=1,
        )

    fast = (
        n_tensor == 2 and J == 4 and Z == kv_heads and Z == J and Z % n_tensor == 0 and slots % 96 == 0
        and slots <= 256 and part == w_out.shape[1] and part % 128 == 0 and width % 128 == 0 and w_out.shape[0] % 64 == 0
    )
    if fast:
        operands = (
            depth[None, :], norm_gain.reshape(n_tensor, 1, width),
            hidden, w_query, w_key, w_value, w_out,
        )
        mixed, chosen = stepped(
            Z, J, n_tensor, slots,
            *(pltpu.with_memory_space_constraint(a, pltpu.HBM) for a in operands),
        )
        return jnp.einsum(
            "sr,sf->rf", chosen, mixed, preferred_element_type=jnp.float32
        ).astype(jnp.bfloat16)

    w_rows = rolled(exchange_j(columns_of), 0, j)
    weights = gather_z(w_rows, 0)
    out_rows = group * HD
    twice = jnp.concatenate([w_out, w_out], axis=0) if J > 1 else w_out
    w_out_turned = lax.dynamic_slice_in_dim(twice, j * out_rows, J * out_rows, axis=0)
    out_weights = gather_z(w_out_turned, 1)

    features = rolled([packed] + [shift_t(packed, n_tensor - m) for m in range(1, n_tensor)], 1, t)
    widened = features.astype(jnp.float32)
    inverse = lax.rsqrt(jnp.mean(widened * widened, axis=1, keepdims=True) + EPSILON)
    normed = (widened * inverse * norm_gain[None, :]).astype(jnp.bfloat16)
    block_rows = J * slots
    tokens = jnp.concatenate(gather_j(normed), axis=0)
    flags = jnp.concatenate(gather_j(filled), axis=0)

    qkv = jnp.dot(tokens, weights, preferred_element_type=jnp.float32).astype(jnp.bfloat16)
    queries = qkv[:, : group * HD].reshape(block_rows, group, HD)
    kv = qkv[:, group * HD :]
    flag_rows = -(-block_rows // (2 * HD))
    flag_pad = -(-flag_rows // 16) * 16
    flag_block = jnp.pad(flags, (0, flag_pad * 2 * HD - block_rows)).reshape(flag_pad, 2 * HD)
    arrived = gather_z(jnp.concatenate([kv, flag_block], axis=0), 0).reshape(
        Z, block_rows + flag_pad, 2 * HD
    )
    keys = arrived[:, :block_rows, :HD].reshape(Z * block_rows, HD)
    values = arrived[:, :block_rows, HD:].reshape(Z * block_rows, HD)
    key_flags = arrived[:, block_rows:].reshape(Z, -1)[:, :block_rows].reshape(Z * block_rows)

    local = jnp.arange(block_rows, dtype=jnp.int32)
    turned = lax.rem(local // slots + j, J) * slots + lax.rem(local, slots)
    query_pos = z * block_rows + turned
    key_pos = (jnp.arange(Z, dtype=jnp.int32)[:, None] * block_rows + turned[None, :]).reshape(-1)
    visible = (key_flags[None, :] > 0) & (key_pos[None, :] <= query_pos[:, None])
    scores = jnp.einsum(
        "qgd,kd->gqk", queries, keys, preferred_element_type=jnp.float32
    ) * HD ** (-0.5)
    scores = jnp.where(visible[None], scores, MASKED_SCORE)
    expons = jnp.exp(scores - jnp.max(scores, axis=-1, keepdims=True))
    total = jnp.sum(expons, axis=-1)
    weighted = jnp.einsum(
        "gqk,kd->gqd", expons.astype(jnp.bfloat16), values, preferred_element_type=jnp.float32
    )
    attended = (weighted / total[..., None]).astype(jnp.bfloat16)
    attended = jnp.transpose(attended, (1, 0, 2)).reshape(block_rows, group * HD)
    attended = rolled([attended[m * slots : (m + 1) * slots] for m in range(J)], 0, j)
    heads = jnp.concatenate(gather_j(attended), axis=1)
    terms = jnp.dot(heads, out_weights, preferred_element_type=jnp.float32).astype(jnp.bfloat16)
    own_cols = w_out.shape[1]
    mine = exchange_j(lambda i: lax.dynamic_slice_in_dim(terms, i * slots, slots, axis=0))
    mine = [piece.reshape(slots, Z, 1, own_cols) for piece in mine]
    mine = rolled(mine, 2, j).reshape(slots, d_model)

    def features_of(i):
        return lax.dynamic_slice_in_dim(mine, i * width, width, axis=1)

    owned = features_of(t).astype(jnp.float32)
    for k in range(1, n_tensor):
        owned = owned + shift_t(features_of(lax.rem(t + k, n_tensor)), k).astype(jnp.float32)
    mixed = owned.astype(jnp.bfloat16)
    return jnp.einsum(
        "sr,sf->rf", select, mixed, preferred_element_type=jnp.float32
    ).astype(jnp.bfloat16)


def solution(mesh):
    n_seq, n_tensor = mesh.shape["seq"], mesh.shape["tensor"]

    def step(*args):
        return body(n_seq, n_tensor, *args)

    return jax.shard_map(
        step,
        mesh=mesh,
        in_specs=(
            P("seq", "tensor"),
            P("seq"),
            P(),
            P("seq", "tensor"),
            P("seq", "tensor"),
            P("seq", "tensor"),
            P("tensor", "seq"),
        ),
        out_specs=P("seq", "tensor"),
        check_vma=False,
    )
```
